32 devices in a mesh: fsdp: 4 (over z), ctx: 4 (over y, core), tp: 2 (over x).
Axes of the slice: x: 2, y: 2, z: 4, core: 2. Of those that a mesh axis runs over, the one named last changes fastest.
Arguments:
- prompt_input: bfloat16 [4, 1024, 2048], P('fsdp', 'ctx'), may hold values from -6 to 6
- continuation_input: bfloat16 [4, 8, 128, 2048], P('fsdp', 'ctx'), may hold values from -6 to 6
- prompt_lengths: int32 [4], P('fsdp'), may hold values from 769 to 1024, as said below
- continuation_lengths: int32 [4, 8], P('fsdp', 'ctx'), may hold values from 32 to 128, as said below
- query_weight: bfloat16 [2048, 2048], P('fsdp', 'tp'), may hold values from -0.1875 to 0.1875
- key_weight: bfloat16 [2048, 2048], P('fsdp', 'tp'), may hold values from -0.1875 to 0.1875
- value_weight: bfloat16 [2048, 2048], P('fsdp', 'tp'), may hold values from -0.125 to 0.125
- query_bias: bfloat16 [16, 128], P('tp', 'fsdp'), may hold values from -2 to 2
- value_bias: bfloat16 [16, 128], P('tp', 'fsdp'), may hold values from -0.59765625 to 0.59765625
- output_weight: bfloat16 [2048, 2048], P('tp', 'fsdp'), may hold values from -1 to 1
- output_bias: bfloat16 [2048], P('fsdp'), may hold values from -2 to 2
- first_gain: bfloat16 [2048], P('fsdp'), may hold values from 0.5 to 1.5
- first_shift: bfloat16 [2048], P('fsdp'), may hold values from -2 to 2
- second_gain: bfloat16 [2048], P('fsdp'), may hold values from 0.5 to 1.5
- second_shift: bfloat16 [2048], P('fsdp'), may hold values from -2 to 2
- up_weight: bfloat16 [2048, 8192], P('fsdp', 'tp'), may hold values from -0.125 to 0.125
- up_bias: bfloat16 [64, 128], P('tp', 'fsdp'), may hold values from -3 to 3
- down_weight: bfloat16 [8192, 2048], P('tp', 'fsdp'), may hold values from -0.09375 to 0.09375
- down_bias: bfloat16 [2048], P('fsdp'), may hold values from -2 to 2
- prompt_cotangent: bfloat16 [4, 1024, 2048], P('fsdp', 'ctx'), may hold values from -6 to 6
- continuation_cotangent: bfloat16 [4, 8, 128, 2048], P('fsdp', 'ctx'), may hold values from -6 to 6
Outputs:
- prompt_output: bfloat16 [4, 1024, 2048], P('fsdp', 'ctx')
- continuation_output: bfloat16 [4, 8, 128, 2048], P('fsdp', 'ctx')
- prompt_input_grad: bfloat16 [4, 1024, 2048], P('fsdp', 'ctx')
- continuation_input_grad: bfloat16 [4, 8, 128, 2048], P('fsdp', 'ctx')
- query_weight_grad: float32 [2048, 2048], P('fsdp', 'tp')
- key_weight_grad: float32 [2048, 2048], P('fsdp', 'tp')
- value_weight_grad: float32 [2048, 2048], P('fsdp', 'tp')
- query_bias_grad: float32 [16, 128], P('tp', 'fsdp')
- value_bias_grad: float32 [16, 128], P('tp', 'fsdp')
- output_weight_grad: float32 [2048, 2048], P('tp', 'fsdp')
- output_bias_grad: float32 [2048], P('fsdp')
- first_gain_grad: float32 [2048], P('fsdp')
- first_shift_grad: float32 [2048], P('fsdp')
- second_gain_grad: float32 [2048], P('fsdp')
- second_shift_grad: float32 [2048], P('fsdp')
- up_weight_grad: float32 [2048, 8192], P('fsdp', 'tp')
- up_bias_grad: float32 [64, 128], P('tp', 'fsdp')
- down_weight_grad: float32 [8192, 2048], P('tp', 'fsdp')
- down_bias_grad: float32 [2048], P('fsdp')
The draws below stay inside these ranges and needn't reach their ends.
Inputs may be any that keep to these rules, and one draw needn't show every extreme that they name: `prompt_lengths`: valid prompt tokens of each group; some group has all 1024. `continuation_lengths`: valid tokens of each continuation; every group has a continuation of all 128 tokens.
All inputs are finite; a program needn't handle non-finite values.
Results may differ from the reference program's by a relative error of at most 0.02.
Values may be sent and summed in bfloat16 or wider, within the bound.
No kernel may reach another device: no remote copies, remote signals or barrier semaphores. Data moves between devices by JAX's collectives and lax.ppermute only.
A program may use at most 512 MiB of HBM per device.

```python
import math
import jax
import jax.numpy as jnp
from jax import lax

D = 2048
HD = 128
FF = 8192
HEADS = 16
PROMPT_DEV = 256
CONT = 128
PROMPT = 1024
NCONT = 8
GROUPS = 4


def draw_prompt_lengths(key, part):
    first_key, second_key = jax.random.split(jax.random.fold_in(key, 11))
    drawn = jax.random.randint(first_key, (GROUPS,), PROMPT - PROMPT_DEV + 1, PROMPT + 1)
    chosen = jax.random.randint(second_key, (), 0, GROUPS)
    return jnp.where(jnp.arange(GROUPS) == chosen, PROMPT, drawn).astype(jnp.int32)


def draw_continuation_lengths(key, part):
    first_key, second_key = jax.random.split(jax.random.fold_in(key, 23))
    drawn = jax.random.randint(first_key, (GROUPS, NCONT), max(CONT // 4, 1), CONT + 1)
    chosen = jax.random.randint(second_key, (GROUPS, 1), 0, NCONT)
    return jnp.where(jnp.arange(NCONT)[None, :] == chosen, CONT, drawn).astype(jnp.int32)


def levels(key, dims, pieces, low, high):
    factor_of, own = 1.0, jax.random.fold_in(key, 6)
    for dim, shards_of in pieces:
        draws = jnp.exp(jax.random.uniform(jax.random.fold_in(own, dim), (shards_of,), jnp.float32, low / len(pieces), high / len(pieces)))
        factor_of = factor_of * jnp.repeat(draws, dims[dim] // shards_of).reshape([-1 if axis == dim else 1 for axis in range(len(dims))])
    return factor_of


def bell_draw(own_key, extent, scale, limit, shards=(), kind=jnp.bfloat16):
    array = jax.random.normal(own_key, extent, jnp.float32) * scale
    if len(shards) > 0:
        array = levels(own_key, extent, shards, -0.22, 0.18) * array
    return jnp.clip(array, min=-limit, max=limit).astype(kind)


def setup_inputs(seed: int = 0) -> dict:
    streams_of = jax.random.split(jax.random.key(seed), 22)
    prompt_input = bell_draw(streams_of[0], (GROUPS, PROMPT, D), 1.0, 6.0, ((0, 4), (1, 4)))
    continuation_input = bell_draw(streams_of[1], (GROUPS, NCONT, CONT, D), 1.0, 6.0, ((0, 4), (1, 4)))
    prompt_lengths = draw_prompt_lengths(jax.random.fold_in(streams_of[21], 71), 0)
    continuation_lengths = draw_continuation_lengths(jax.random.fold_in(streams_of[21], 71), 0)
    query_weight = bell_draw(streams_of[4], (D, D), (D // 2) ** -0.5, 0.1875, ((0, 4), (1, 2)))
    key_weight = bell_draw(streams_of[5], (D, D), (D // 2) ** -0.5, 0.1875, ((0, 4), (1, 2)))
    value_weight = bell_draw(streams_of[6], (D, D), D ** -0.5, 0.125, ((0, 4), (1, 2)))
    query_bias = bell_draw(streams_of[7], (HEADS, HD), 0.3, 2.0, ((0, 2), (1, 4)))
    value_bias = bell_draw(streams_of[8], (HEADS, HD), 0.1, 0.59765625, ((0, 2), (1, 4)))
    output_weight = bell_draw(streams_of[9], (D, D), (max(D // 64, 16)) ** -0.5, 1.0, ((0, 2), (1, 4)))
    output_bias = bell_draw(streams_of[10], (D,), 0.3, 2.0, ((0, 4),))
    first_gain = jnp.clip(1.0 + 0.1 * jax.random.normal(streams_of[11], (D,), jnp.float32), 0.5, 1.5).astype(jnp.bfloat16)
    first_shift = bell_draw(streams_of[12], (D,), 0.3, 2.0, ((0, 4),))
    second_gain = jnp.clip(1.0 + 0.1 * jax.random.normal(streams_of[13], (D,), jnp.float32), 0.5, 1.5).astype(jnp.bfloat16)
    second_shift = bell_draw(streams_of[14], (D,), 0.3, 2.0, ((0, 4),))
    up_weight = bell_draw(streams_of[15], (D, FF), D ** -0.5, 0.125, ((0, 4), (1, 2)))
    up_bias = bell_draw(streams_of[16], (FF // HD, HD), 0.5, 3.0, ((0, 2), (1, 4)))
    down_weight = bell_draw(streams_of[17], (FF, D), (FF // 2) ** -0.5, 0.09375, ((0, 2), (1, 4)))
    down_bias = bell_draw(streams_of[18], (D,), 0.3, 2.0, ((0, 4),))
    prompt_cotangent = bell_draw(streams_of[19], (GROUPS, PROMPT, D), 1.0, 6.0, ((0, 4), (1, 4)))
    continuation_cotangent = bell_draw(streams_of[20], (GROUPS, NCONT, CONT, D), 1.0, 6.0, ((0, 4), (1, 4)))
    return {"prompt_input": prompt_input, "continuation_input": continuation_input, "prompt_lengths": prompt_lengths, "continuation_lengths": continuation_lengths, "query_weight": query_weight, "key_weight": key_weight, "value_weight": value_weight, "query_bias": query_bias, "value_bias": value_bias, "output_weight": output_weight, "output_bias": output_bias, "first_gain": first_gain, "first_shift": first_shift, "second_gain": second_gain, "second_shift": second_shift, "up_weight": up_weight, "up_bias": up_bias, "down_weight": down_weight, "down_bias": down_bias, "prompt_cotangent": prompt_cotangent, "continuation_cotangent": continuation_cotangent}


@jax.custom_vjp
def low(v):
    return lax.optimization_barrier(v.astype(jnp.bfloat16)).astype(jnp.float32)

@jax.custom_vjp
def low_back(v):
    return v

def low_keep(v):
    return (low(v), None)

def low_pass(kept, grad):
    return (grad,)

def back_keep(v):
    return (v, None)

def back_low(kept, grad):
    return (low(grad),)
low.defvjp(low_keep, low_pass)
low_back.defvjp(back_keep, back_low)

def matmul(lhs_matrix, rhs_matrix):
    return jnp.dot(lhs_matrix, rhs_matrix, precision=lax.Precision.HIGHEST, preferred_element_type=jnp.float32)

def normalize(values, gain_vec, shift_vec):
    centre = lax.optimization_barrier(jnp.mean(values, axis=-1, keepdims=True))
    centered = values - centre
    inverse = lax.rsqrt(lax.optimization_barrier(jnp.mean(centered * centered, axis=-1, keepdims=True)) + 1e-05)
    return centered * inverse * gain_vec + shift_vec

def visibility(prompt_length, seq_lengths):
    row_count = PROMPT + NCONT * CONT
    row_index = jnp.arange(row_count, dtype=jnp.int32)
    is_prompt = row_index < PROMPT
    sequence = jnp.where(is_prompt, -1, (row_index - PROMPT) // CONT)
    position = jnp.where(is_prompt, row_index, (row_index - PROMPT) % CONT)
    key_limit = jnp.where(is_prompt, prompt_length, seq_lengths[jnp.maximum(sequence, 0)])
    is_valid = position < key_limit
    cross = is_prompt[None, :] & jnp.logical_not(is_prompt[:, None])
    causal = (sequence[None, :] == sequence[:, None]) & (position[None, :] <= position[:, None])
    return is_valid[None, :] & (cross | causal)

def group_layer(params, group_rows, prompt_length, seq_lengths):
    query_weight, key_weight, value_weight, query_bias, value_bias, output_weight, output_bias, first_gain, first_shift, second_gain, second_shift, up_weight, up_bias, down_weight, down_bias = params
    row_count = group_rows.shape[0]
    act_one = low(normalize(group_rows, first_gain, first_shift))
    queries = low(low_back(matmul(act_one, query_weight) + query_bias.reshape(D)))
    keys = low(low_back(matmul(act_one, key_weight)))
    values = low(low_back(matmul(act_one, value_weight) + value_bias.reshape(D)))
    query_heads = queries.reshape(row_count, HEADS, HD)
    key_heads = keys.reshape(row_count, HEADS, HD)
    value_heads = values.reshape(row_count, HEADS, HD)
    raw_scores = jnp.einsum('qhd,khd->hqk', query_heads, key_heads, precision=lax.Precision.HIGHEST) * (1.0 / math.sqrt(HD))
    raw_scores = low_back(raw_scores)
    masked = jnp.where(visibility(prompt_length, seq_lengths)[None, :, :], raw_scores, -1e+30)
    row_top = lax.optimization_barrier(jnp.max(masked, axis=-1, keepdims=True))
    exponent = jnp.exp(masked - row_top)
    probs = low(exponent / lax.optimization_barrier(jnp.sum(exponent, axis=-1, keepdims=True)))
    attended = jnp.einsum('hqk,khd->qhd', probs, value_heads, precision=lax.Precision.HIGHEST).reshape(row_count, D)
    attended = low(low_back(attended))
    middle = group_rows + low_back(matmul(attended, output_weight) + output_bias)
    act_two = low(normalize(middle, second_gain, second_shift))
    pre_act = low_back(matmul(act_two, up_weight) + up_bias.reshape(FF))
    hidden = low(jax.nn.gelu(pre_act, approximate=False))
    return middle + low_back(matmul(hidden, down_weight) + down_bias)

def reference(prompt_input, continuation_input, prompt_lengths, continuation_lengths, query_weight, key_weight, value_weight, query_bias, value_bias, output_weight, output_bias, first_gain, first_shift, second_gain, second_shift, up_weight, up_bias, down_weight, down_bias, prompt_cotangent, continuation_cotangent):
    params = tuple((weight.astype(jnp.float32) for weight in (query_weight, key_weight, value_weight, query_bias, value_bias, output_weight, output_bias, first_gain, first_shift, second_gain, second_shift, up_weight, up_bias, down_weight, down_bias)))
    stacked = jnp.concatenate([prompt_input.astype(jnp.float32), continuation_input.astype(jnp.float32).reshape(GROUPS, NCONT * CONT, D)], axis=1)
    upstream = jnp.concatenate([prompt_cotangent.astype(jnp.float32), continuation_cotangent.astype(jnp.float32).reshape(GROUPS, NCONT * CONT, D)], axis=1)

    def forward(weights, all_rows):

        def one_group(group_item):
            return jax.checkpoint(group_layer)(weights, group_item[0], group_item[1], group_item[2])
        return lax.map(one_group, (all_rows, prompt_lengths, continuation_lengths))
    result, pull = jax.vjp(forward, params, stacked)
    weight_grads, row_grads = pull(upstream)
    g_query, g_key, g_value, g_qbias, g_vbias, g_output, g_obias, g_gain_one, g_shift_one, g_gain_two, g_shift_two, g_up, g_ubias, g_down, g_dbias = weight_grads
    return (result[:, :PROMPT].astype(jnp.bfloat16), result[:, PROMPT:].reshape(GROUPS, NCONT, CONT, D).astype(jnp.bfloat16), row_grads[:, :PROMPT].astype(jnp.bfloat16), row_grads[:, PROMPT:].reshape(GROUPS, NCONT, CONT, D).astype(jnp.bfloat16), g_query, g_key, g_value, g_qbias, g_vbias, g_output, g_obias, g_gain_one, g_shift_one, g_gain_two, g_shift_two, g_up, g_ubias, g_down, g_dbias)
```

```python
from functools import partial
import math

import jax
import jax.numpy as jnp
from jax import lax
from jax.experimental import pallas as pl
from jax.experimental.pallas import tpu as pltpu
from jax.sharding import PartitionSpec as P

HD = 128
BF = jnp.bfloat16
F32 = jnp.float32


norm_epsilon = 1e-05


def normalize(values):
    centre = jnp.mean(values, axis=-1, keepdims=True)
    centered = values - centre
    inverse = lax.rsqrt(jnp.mean(centered * centered, axis=-1, keepdims=True) + norm_epsilon)
    return (centered * inverse, inverse)


def norm_backward(incoming, normed, inverse, gain_vec):
    scaled = incoming * gain_vec
    return inverse * (
        scaled
        - jnp.mean(scaled, axis=-1, keepdims=True)
        - normed * jnp.mean(scaled * normed, axis=-1, keepdims=True)
    )


def swap_tp(value):
    return lax.ppermute(value, "tp", [(0, 1), (1, 0)])


def swap_low(value):
    return lax.ppermute(value, "ctx", [(0, 1), (1, 0), (2, 3), (3, 2)])


def swap_high(value):
    return lax.ppermute(value, "ctx", [(0, 2), (2, 0), (1, 3), (3, 1)])


def gather_blocks(own):
    half = own.shape[0] // 2
    across = swap_tp(own)
    along = swap_high(own)
    corner = jnp.concatenate([swap_high(across[:half]), swap_tp(along[half:])], axis=0)
    return [
        own,
        across,
        swap_low(own),
        swap_low(across),
        along,
        corner,
        swap_low(along),
        swap_low(corner),
    ]


def scatter_blocks(parts):
    half = parts[0].shape[0] // 2
    kept = {p: parts[p].astype(F32) + swap_low(parts[p ^ 2]).astype(F32) for p in (5, 1, 4, 0)}
    corner = kept[5].astype(BF)
    via_high = swap_high(corner[:half]).astype(F32)
    via_tp = swap_tp(corner[half:]).astype(F32)
    across = jnp.concatenate([kept[1][:half] + via_high, kept[1][half:]], axis=0).astype(BF)
    along = jnp.concatenate([kept[4][:half], kept[4][half:] + via_tp], axis=0).astype(BF)
    return kept[0] + swap_tp(across).astype(F32) + swap_high(along).astype(F32)


def gather_ctx(pair):
    low = swap_low(pair)
    high = swap_high(pair)
    return jnp.concatenate([pair, low, high, swap_low(high)], axis=0)


def pair_mask(rows, limits, split):
    row = lax.broadcasted_iota(jnp.int32, (rows, rows), 0)
    col = lax.broadcasted_iota(jnp.int32, (rows, rows), 1)
    mask = col <= row
    for seq in range(rows // split):
        inside = (row >= seq * split) & (row < (seq + 1) * split)
        limit = jnp.where(inside, limits[seq] + seq * split, 0)
        lower = jnp.where(inside, seq * split, 0)
        ok = (col >= lower) & (col < limit)
        mask = mask & (jnp.logical_not(inside) | ok)
    return mask


def attention_tiles(info_ref, tiles, rows, cont_len):
    me = info_ref[0]
    prompt_len = info_ref[1]
    per_block = rows // cont_len
    col = lax.broadcasted_iota(jnp.int32, (rows, rows), 1)
    row = lax.broadcasted_iota(jnp.int32, (rows, rows), 0)
    plan = []
    for t in range(tiles):
        keys = []
        for j in range(t + 1):
            mask = (col + j * rows) < prompt_len
            if j == t:
                mask = mask & (col <= row)
            keys.append((2 * j, mask))
        plan.append((2 * t, keys))
    for t in range(tiles):
        keys = []
        for j in range(tiles):
            keys.append((2 * j, (col + j * rows) < prompt_len))
        base = 2 + ((2 * t) ^ (me & (2 * tiles - 2))) // 2 * per_block
        limits = [info_ref[base + s] for s in range(per_block)]
        keys.append((2 * t + 1, pair_mask(rows, limits, cont_len)))
        plan.append((2 * t + 1, keys))
    return me, plan


def dot_nt(a, b):
    return lax.dot_general(a, b, (((1,), (1,)), ((), ())), preferred_element_type=F32)


def dot_nn(a, b):
    return lax.dot_general(a, b, (((1,), (0,)), ((), ())), preferred_element_type=F32)


def dot_tn(a, b):
    return lax.dot_general(a, b, (((0,), (0,)), ((), ())), preferred_element_type=F32)


def softmax_tiles(query, keys, scale):
    scores = [jnp.where(mask, dot_nt(query, key) * scale, -1e30) for key, mask in keys]
    top = jnp.max(scores[0], axis=-1, keepdims=True)
    for s in scores[1:]:
        top = jnp.maximum(top, jnp.max(s, axis=-1, keepdims=True))
    weights = [jnp.exp(s - top) for s in scores]
    total = jnp.sum(weights[0], axis=-1, keepdims=True)
    for w in weights[1:]:
        total = total + jnp.sum(w, axis=-1, keepdims=True)
    inverse = 1.0 / total
    return [w * inverse for w in weights]


def attention_forward_kernel(tiles, rows, cont_len, heads, info_ref, qkv_ref, out_ref):
    h = pl.program_id(0)
    scale = 1.0 / math.sqrt(HD)
    me, plan = attention_tiles(info_ref, tiles, rows, cont_len)

    def load(kind, block):
        cols = pl.ds(pl.multiple_of((kind * heads + h) * HD, HD), HD)
        return qkv_ref[block ^ me, :, cols]

    for block, keys in plan:
        query = load(0, block)
        probs = softmax_tiles(query, [(load(1, kb), mask) for kb, mask in keys], scale)
        total = None
        for p, (kb, _) in zip(probs, keys):
            term = dot_nn(p.astype(BF), load(2, kb))
            total = term if total is None else total + term
        cols = pl.ds(pl.multiple_of(h * HD, HD), HD)
        out_ref[block ^ me, :, cols] = total.astype(BF)


def attention_backward_kernel(
    tiles, rows, cont_len, heads, info_ref, qkv_ref, grad_ref, out_ref, dkey_ref, dvalue_ref
):
    h = pl.program_id(0)
    scale = 1.0 / math.sqrt(HD)
    me, plan = attention_tiles(info_ref, tiles, rows, cont_len)

    def columns(kind):
        return pl.ds(pl.multiple_of((kind * heads + h) * HD, HD), HD)

    def load(kind, block):
        return qkv_ref[block ^ me, :, columns(kind)]

    seen = set()
    for block, keys in plan:
        query = load(0, block)
        grad = grad_ref[block ^ me, :, columns(0)]
        probs = softmax_tiles(query, [(load(1, kb), mask) for kb, mask in keys], scale)
        gprobs = [dot_nt(grad, load(2, kb)) for kb, _ in keys]
        delta = jnp.sum(probs[0] * gprobs[0], axis=-1, keepdims=True)
        for p, g in zip(probs[1:], gprobs[1:]):
            delta = delta + jnp.sum(p * g, axis=-1, keepdims=True)
        dquery = None
        for p, g, (kb, _) in zip(probs, gprobs, keys):
            dscore = (p * (g - delta)).astype(BF)
            term = dot_nn(dscore, load(1, kb))
            dquery = term if dquery is None else dquery + term
            dkey = dot_tn(dscore, query)
            dvalue = dot_tn(p.astype(BF), grad)
            if kb in seen:
                dkey_ref[kb] += dkey
                dvalue_ref[kb] += dvalue
            else:
                dkey_ref[kb] = dkey
                dvalue_ref[kb] = dvalue
                seen.add(kb)
        out_ref[block ^ me, :, columns(0)] = (dquery * scale).astype(BF)
    for kb in sorted(seen):
        out_ref[kb ^ me, :, columns(1)] = (dkey_ref[kb] * scale).astype(BF)
        out_ref[kb ^ me, :, columns(2)] = dvalue_ref[kb].astype(BF)


def attention_cost(blocks, rows, heads, matmuls):
    tiles = blocks // 2
    pairs = (tiles * (tiles + 1)) // 2 + tiles * (tiles + 1)
    return pl.CostEstimate(
        flops=2 * matmuls * pairs * heads * rows * rows * HD,
        transcendentals=pairs * heads * rows * rows,
        bytes_accessed=2 * blocks * rows * heads * HD * (4 if matmuls == 2 else 7),
    )


def attention_forward(info, qkv, cont_len):
    blocks, rows, width = qkv.shape
    heads = width // (3 * HD)
    return pl.pallas_call(
        partial(attention_forward_kernel, blocks // 2, rows, cont_len, heads),
        grid=(heads,),
        in_specs=[
            pl.BlockSpec(memory_space=pltpu.SMEM),
            pl.BlockSpec((blocks, rows, width), lambda h: (0, 0, 0)),
        ],
        out_specs=pl.BlockSpec((blocks, rows, heads * HD), lambda h: (0, 0, 0)),
        out_shape=jax.ShapeDtypeStruct((blocks, rows, heads * HD), BF),
        compiler_params=pltpu.CompilerParams(vmem_limit_bytes=40 << 20),
        cost_estimate=attention_cost(blocks, rows, heads, 2),
        name="attention_forward",
    )(info, qkv)


def attention_backward(info, qkv, grad, cont_len):
    blocks, rows, width = qkv.shape
    heads = width // (3 * HD)
    return pl.pallas_call(
        partial(attention_backward_kernel, blocks // 2, rows, cont_len, heads),
        grid=(heads,),
        in_specs=[
            pl.BlockSpec(memory_space=pltpu.SMEM),
            pl.BlockSpec((blocks, rows, width), lambda h: (0, 0, 0)),
            pl.BlockSpec((blocks, rows, heads * HD), lambda h: (0, 0, 0)),
        ],
        out_specs=pl.BlockSpec((blocks, rows, width), lambda h: (0, 0, 0)),
        out_shape=jax.ShapeDtypeStruct((blocks, rows, width), BF),
        scratch_shapes=[
            pltpu.VMEM((blocks, rows, HD), F32),
            pltpu.VMEM((blocks, rows, HD), F32),
        ],
        compiler_params=pltpu.CompilerParams(vmem_limit_bytes=40 << 20),
        cost_estimate=attention_cost(blocks, rows, heads, 7),
        name="attention_backward",
    )(info, qkv, grad)


def gather_small(packed, size):
    index = lax.axis_index("fsdp")
    out = lax.dynamic_update_slice(
        jnp.zeros((size,) + packed.shape, packed.dtype), packed[None], (index, 0)
    )
    for step in range(1, size):
        moved = lax.ppermute(packed, "fsdp", [(i, (i + step) % size) for i in range(size)])
        out = lax.dynamic_update_slice(out, moved[None], ((index + size - step) % size, 0))
    return out


def body(
    prompt_input,
    continuation_input,
    prompt_lengths,
    continuation_lengths,
    query_weight,
    key_weight,
    value_weight,
    query_bias,
    value_bias,
    output_weight,
    output_bias,
    first_gain,
    first_shift,
    second_gain,
    second_shift,
    up_weight,
    up_bias,
    down_weight,
    down_bias,
    prompt_cotangent,
    continuation_cotangent,
):
    prompt_dev = prompt_input.shape[1]
    cont_dev = continuation_input.shape[1]
    cont_len = continuation_input.shape[2]
    width = prompt_input.shape[2]
    rows = prompt_dev
    fsdp_size = lax.axis_size("fsdp")
    ctx_size = lax.axis_size("ctx")
    tp_size = lax.axis_size("tp")
    assert ctx_size == 4 and tp_size == 2 and cont_dev * cont_len == rows
    blocks = ctx_size * tp_size
    total_rows = blocks * rows
    z = lax.axis_index("fsdp")
    ctx = lax.axis_index("ctx")
    tp = lax.axis_index("tp")
    me = 2 * ctx + tp

    heads_tp = query_bias.shape[0]
    heads = heads_tp // ctx_size
    head_width = heads * HD
    units = up_weight.shape[1] // ctx_size
    unit_rows = units // HD
    d_local = query_weight.shape[0]

    def cols(weight, count):
        return lax.dynamic_slice_in_dim(weight, ctx * count, count, axis=1)

    def rws(weight, count):
        return lax.dynamic_slice_in_dim(weight, ctx * count, count, axis=0)

    attn_shard = jnp.concatenate(
        [
            cols(query_weight, head_width),
            cols(key_weight, head_width),
            cols(value_weight, head_width),
            rws(output_weight, head_width).T,
        ],
        axis=1,
    )
    attn_full = lax.all_gather(attn_shard, "fsdp", axis=0, tiled=True)
    w_qkv = attn_full[:, : 3 * head_width]
    w_out = attn_full[:, 3 * head_width :]
    w_up = lax.all_gather(cols(up_weight, units), "fsdp", axis=0, tiled=True)
    w_down = lax.all_gather(rws(down_weight, units).T, "fsdp", axis=0, tiled=True)

    packed = jnp.concatenate(
        [
            output_bias,
            first_gain,
            first_shift,
            second_gain,
            second_shift,
            down_bias,
            rws(query_bias, heads).reshape(-1),
            rws(value_bias, heads).reshape(-1),
            rws(up_bias, unit_rows).reshape(-1),
        ]
    )
    small = gather_small(packed, fsdp_size).astype(F32)
    vectors = [small[:, i * d_local : (i + 1) * d_local].reshape(-1) for i in range(6)]
    obias, gain_one, shift_one, gain_two, shift_two, dbias = vectors
    hd_local = HD // fsdp_size

    def head_vector(start, count):
        piece = small[:, start : start + count * hd_local].reshape(fsdp_size, count, hd_local)
        return piece.transpose(1, 0, 2).reshape(-1)

    start = 6 * d_local
    qbias = head_vector(start, heads)
    vbias = head_vector(start + heads * hd_local, heads)
    ubias = head_vector(start + 2 * heads * hd_local, unit_rows)
    qkv_bias = jnp.concatenate([qbias, jnp.zeros_like(qbias), vbias])

    lens = continuation_lengths[0]
    lens_high = swap_high(lens)
    info = jnp.concatenate(
        [me[None].astype(jnp.int32), prompt_lengths, lens, swap_low(lens), lens_high, swap_low(lens_high)]
    )

    def own_pair(first, second):
        a = first[0]
        b = second[0].reshape(rows, width)
        return jnp.where(tp == 0, a, b), jnp.where(tp == 0, b, a)

    in_own, in_other = own_pair(prompt_input, continuation_input)
    up_own, up_other = own_pair(prompt_cotangent, continuation_cotangent)
    stacked = jnp.concatenate([in_own, in_other], axis=0).astype(F32)
    normed_pair, inverse_pair = normalize(stacked)
    act_pair = (normed_pair * gain_one + shift_one).astype(BF)
    act_one = gather_ctx(act_pair)
    normed_one = normed_pair[:rows]
    inverse_one = inverse_pair[:rows]
    x_own = stacked[:rows]

    qkv = (jnp.dot(act_one, w_qkv, preferred_element_type=F32) + qkv_bias).astype(BF)
    qkv = qkv.reshape(blocks, rows, 3 * head_width)
    attended = attention_forward(info, qkv, cont_len)

    def scatter_matmul(left, right):
        parts = {}
        for group in ((2, 3), (6, 7), (4, 5), (0, 1)):
            lhs = left[group[0] : group[0] + 2].reshape(2 * rows, -1)
            res = dot_nt(lhs, right).astype(BF)
            parts[group[0]] = res[:rows]
            parts[group[1]] = res[rows:]
        return scatter_blocks(parts)

    attn_sum = scatter_matmul(attended, w_out)
    middle = x_own + (attn_sum + obias)
    normed_two, inverse_two = normalize(middle)
    act_two_own = (normed_two * gain_two + shift_two).astype(BF)
    act_two = jnp.concatenate(gather_blocks(act_two_own), axis=0)
    upstream_low = gather_ctx(jnp.concatenate([up_own, up_other], axis=0))

    pre_act = jnp.dot(act_two, w_up, preferred_element_type=F32) + ubias
    hidden = jax.nn.gelu(pre_act, approximate=False).astype(BF)
    down_term = dot_tn(upstream_low, hidden).astype(BF)
    down_piece = lax.psum_scatter(down_term, "fsdp", scatter_dimension=0, tiled=True)
    grad_hidden = jnp.dot(upstream_low, w_down, preferred_element_type=F32)
    gelu_pull = jax.vjp(partial(jax.nn.gelu, approximate=False), pre_act)[1]
    grad_pre = gelu_pull(grad_hidden)[0].astype(BF)
    up_term = dot_tn(act_two, grad_pre).astype(BF)
    up_piece = lax.psum_scatter(up_term, "fsdp", scatter_dimension=0, tiled=True)
    grad_act_two = scatter_matmul(grad_pre.reshape(blocks, rows, units), w_up)
    grad_middle = up_own.astype(F32) + norm_backward(
        grad_act_two, normed_two, inverse_two, gain_two
    )
    middle_low_own = grad_middle.astype(BF)
    middle_low = jnp.concatenate(gather_blocks(middle_low_own), axis=0)

    mlp_sum = scatter_matmul(hidden.reshape(blocks, rows, units), w_down)
    result = (middle + (mlp_sum + dbias)).astype(BF)
    result_other = swap_tp(result)

    out_term = dot_tn(middle_low, attended.reshape(total_rows, head_width)).astype(BF)
    grad_attended = jnp.dot(middle_low, w_out, preferred_element_type=F32).astype(BF)
    dqkv = attention_backward(info, qkv, grad_attended.reshape(blocks, rows, head_width), cont_len)
    dqkv_flat = dqkv.reshape(total_rows, 3 * head_width)
    qkv_term = dot_tn(act_one, dqkv_flat).astype(BF)
    attn_piece = lax.psum_scatter(
        jnp.concatenate([qkv_term, out_term], axis=1), "fsdp", scatter_dimension=0, tiled=True
    )
    grad_act_one = scatter_matmul(dqkv, w_qkv)
    grad_stacked = (
        grad_middle + norm_backward(grad_act_one, normed_one, inverse_one, gain_one)
    ).astype(BF)
    stacked_other = swap_tp(grad_stacked)

    def to_outputs(own, other):
        first = jnp.where(tp == 0, own, other)
        second = jnp.where(tp == 0, other, own)
        return first[None], second.reshape(1, cont_dev, cont_len, width)

    prompt_output, continuation_output = to_outputs(result, result_other)
    prompt_input_grad, continuation_input_grad = to_outputs(grad_stacked, stacked_other)

    def colsum(value):
        return jnp.sum(value, axis=0, dtype=F32)

    d_vectors = jnp.stack(
        [
            colsum(middle_low_own),
            colsum(grad_act_one * normed_one),
            colsum(grad_act_one),
            colsum(grad_act_two * normed_two),
            colsum(grad_act_two),
            colsum(up_own),
        ]
    )
    summed = lax.psum(d_vectors, ("fsdp", "ctx", "tp"))
    summed = lax.dynamic_slice_in_dim(summed, z * d_local, d_local, axis=1)
    obias_grad, gain_one_grad, shift_one_grad, gain_two_grad, shift_two_grad, dbias_grad = [
        summed[i] for i in range(6)
    ]
    colsum_qkv = colsum(dqkv_flat)
    head_terms = jnp.concatenate(
        [
            colsum_qkv[:head_width].reshape(heads, HD),
            colsum_qkv[2 * head_width :].reshape(heads, HD),
            colsum(grad_pre).reshape(unit_rows, HD),
        ]
    )
    head_slots = jnp.where(
        lax.broadcasted_iota(jnp.int32, (ctx_size, 1, 1), 0) == ctx, head_terms[None], 0.0
    )
    head_sums = lax.psum(head_slots, ("fsdp", "ctx"))
    head_sums = lax.dynamic_slice_in_dim(head_sums, z * hd_local, hd_local, axis=2)
    qbias_grad = head_sums[:, :heads].reshape(heads_tp, hd_local)
    vbias_grad = head_sums[:, heads : 2 * heads].reshape(heads_tp, hd_local)
    ubias_grad = head_sums[:, 2 * heads :].reshape(ctx_size * unit_rows, hd_local)

    def spread(piece, axis):
        count = piece.shape[axis]
        shape = list(piece.shape)
        shape[axis] = count * ctx_size
        low = swap_low(piece)
        high = swap_high(piece)
        both = swap_low(high)
        out = jnp.zeros(shape, F32)
        for offset, part in ((0, piece), (1, low), (2, high), (3, both)):
            position = [0, 0]
            position[axis] = (ctx ^ offset) * count
            out = lax.dynamic_update_slice(out, part.astype(F32), tuple(position))
        return out

    down_grad = spread(down_piece.T, 0)
    up_grad = spread(up_piece, 1)
    query_grad = spread(attn_piece[:, :head_width], 1)
    key_grad = spread(attn_piece[:, head_width : 2 * head_width], 1)
    value_grad = spread(attn_piece[:, 2 * head_width : 3 * head_width], 1)
    output_grad = spread(attn_piece[:, 3 * head_width :].T, 0)
    return (
        prompt_output,
        continuation_output,
        prompt_input_grad,
        continuation_input_grad,
        query_grad,
        key_grad,
        value_grad,
        qbias_grad,
        vbias_grad,
        output_grad,
        obias_grad,
        gain_one_grad,
        shift_one_grad,
        gain_two_grad,
        shift_two_grad,
        up_grad,
        ubias_grad,
        down_grad,
        dbias_grad,
    )


def solution(mesh):
    return jax.shard_map(
        body,
        mesh=mesh,
        in_specs=(
            P("fsdp", "ctx", None),
            P("fsdp", "ctx", None, None),
            P("fsdp"),
            P("fsdp", "ctx"),
            P("fsdp", "tp"),
            P("fsdp", "tp"),
            P("fsdp", "tp"),
            P("tp", "fsdp"),
            P("tp", "fsdp"),
            P("tp", "fsdp"),
            P("fsdp"),
            P("fsdp"),
            P("fsdp"),
            P("fsdp"),
            P("fsdp"),
            P("fsdp", "tp"),
            P("tp", "fsdp"),
            P("tp", "fsdp"),
            P("fsdp"),
            P("fsdp", "ctx", None),
            P("fsdp", "ctx", None, None),
        ),
        out_specs=(
            P("fsdp", "ctx", None),
            P("fsdp", "ctx", None, None),
            P("fsdp", "ctx", None),
            P("fsdp", "ctx", None, None),
            P("fsdp", "tp"),
            P("fsdp", "tp"),
            P("fsdp", "tp"),
            P("tp", "fsdp"),
            P("tp", "fsdp"),
            P("tp", "fsdp"),
            P("fsdp"),
            P("fsdp"),
            P("fsdp"),
            P("fsdp"),
            P("fsdp"),
            P("fsdp", "tp"),
            P("tp", "fsdp"),
            P("tp", "fsdp"),
            P("fsdp"),
        ),
        check_vma=False,
    )
```

```python
from functools import partial
import math

import jax
import jax.numpy as jnp
from jax import lax
from jax.experimental import pallas as pl
from jax.experimental.pallas import tpu as pltpu
from jax.sharding import PartitionSpec as P

HD = 128
BF = jnp.bfloat16
F32 = jnp.float32


norm_epsilon = 1e-05


def normalize(values):
    centre = jnp.mean(values, axis=-1, keepdims=True)
    centered = values - centre
    inverse = lax.rsqrt(jnp.mean(centered * centered, axis=-1, keepdims=True) + norm_epsilon)
    return (centered * inverse, inverse)


def norm_backward(incoming, normed, inverse, gain_vec):
    scaled = incoming * gain_vec
    return inverse * (
        scaled
        - jnp.mean(scaled, axis=-1, keepdims=True)
        - normed * jnp.mean(scaled * normed, axis=-1, keepdims=True)
    )


def swap_tp(value):
    return lax.ppermute(value, "tp", [(0, 1), (1, 0)])


def swap_low(value):
    return lax.ppermute(value, "ctx", [(0, 1), (1, 0), (2, 3), (3, 2)])


def swap_high(value):
    return lax.ppermute(value, "ctx", [(0, 2), (2, 0), (1, 3), (3, 1)])


def after(value, *earlier):
    return lax.optimization_barrier((value,) + earlier)[0]


def gather_blocks(own):
    half = own.shape[0] // 2
    across = swap_tp(own)
    along = swap_high(own)
    corner_a = swap_high(across[:half])
    corner_b = swap_tp(along[half:])
    return [
        [own, swap_low(own)],
        [across, swap_low(across)],
        [along, swap_low(along)],
        [corner_a, corner_b, swap_low(corner_a), swap_low(corner_b)],
    ]


GROUPS = ((0, 2), (1, 3), (4, 6), (5, 7))


def scatter_blocks(parts):
    half = parts[0].shape[0] // 2
    kept = {p: parts[p].astype(F32) + swap_low(parts[p ^ 2]).astype(F32) for p in (5, 1, 4, 0)}
    corner = kept[5].astype(BF)
    via_high = swap_high(corner[:half]).astype(F32)
    via_tp = swap_tp(corner[half:]).astype(F32)
    across = jnp.concatenate([kept[1][:half] + via_high, kept[1][half:]], axis=0).astype(BF)
    along = jnp.concatenate([kept[4][:half], kept[4][half:] + via_tp], axis=0).astype(BF)
    return kept[0] + swap_tp(across).astype(F32) + swap_high(along).astype(F32)


def gather_ctx(pair):
    low = swap_low(pair)
    high = swap_high(pair)
    return [pair, low, high, swap_low(high)]


def pair_mask(rows, limits, split):
    row = lax.broadcasted_iota(jnp.int32, (rows, rows), 0)
    col = lax.broadcasted_iota(jnp.int32, (rows, rows), 1)
    mask = col <= row
    for seq in range(rows // split):
        inside = (row >= seq * split) & (row < (seq + 1) * split)
        limit = jnp.where(inside, limits[seq] + seq * split, 0)
        lower = jnp.where(inside, seq * split, 0)
        ok = (col >= lower) & (col < limit)
        mask = mask & (jnp.logical_not(inside) | ok)
    return mask


def attention_tiles(info_ref, tiles, rows, cont_len):
    me = info_ref[0]
    prompt_len = info_ref[1]
    per_block = rows // cont_len
    col = lax.broadcasted_iota(jnp.int32, (rows, rows), 1)
    row = lax.broadcasted_iota(jnp.int32, (rows, rows), 0)
    plan = []
    for t in range(tiles):
        keys = []
        for j in range(t + 1):
            mask = (col + j * rows) < prompt_len
            if j == t:
                mask = mask & (col <= row)
            keys.append((2 * j, mask))
        plan.append((2 * t, keys))
    for t in range(tiles):
        keys = []
        for j in range(tiles):
            keys.append((2 * j, (col + j * rows) < prompt_len))
        base = 2 + ((2 * t) ^ (me & (2 * tiles - 2))) // 2 * per_block
        limits = [info_ref[base + s] for s in range(per_block)]
        keys.append((2 * t + 1, pair_mask(rows, limits, cont_len)))
        plan.append((2 * t + 1, keys))
    return me, plan


def dot_nt(a, b):
    return lax.dot_general(a, b, (((1,), (1,)), ((), ())), preferred_element_type=F32)


def dot_nn(a, b):
    return lax.dot_general(a, b, (((1,), (0,)), ((), ())), preferred_element_type=F32)


def dot_tn(a, b):
    return lax.dot_general(a, b, (((0,), (0,)), ((), ())), preferred_element_type=F32)


def softmax_tiles(query, keys, scale):
    scores = [jnp.where(mask, dot_nt(query, key) * scale, -1e30) for key, mask in keys]
    top = jnp.max(scores[0], axis=-1, keepdims=True)
    for s in scores[1:]:
        top = jnp.maximum(top, jnp.max(s, axis=-1, keepdims=True))
    weights = [jnp.exp(s - top) for s in scores]
    total = jnp.sum(weights[0], axis=-1, keepdims=True)
    for w in weights[1:]:
        total = total + jnp.sum(w, axis=-1, keepdims=True)
    inverse = 1.0 / total
    return [w * inverse for w in weights]


def attention_forward_kernel(tiles, rows, cont_len, heads, info_ref, qkv_ref, out_ref):
    h = pl.program_id(0)
    scale = 1.0 / math.sqrt(HD)
    me, plan = attention_tiles(info_ref, tiles, rows, cont_len)

    def load(kind, block):
        cols = pl.ds(pl.multiple_of((kind * heads + h) * HD, HD), HD)
        return qkv_ref[block ^ me, :, cols]

    for block, keys in plan:
        query = load(0, block)
        probs = softmax_tiles(query, [(load(1, kb), mask) for kb, mask in keys], scale)
        total = None
        for p, (kb, _) in zip(probs, keys):
            term = dot_nn(p.astype(BF), load(2, kb))
            total = term if total is None else total + term
        cols = pl.ds(pl.multiple_of(h * HD, HD), HD)
        out_ref[block ^ me, :, cols] = total.astype(BF)


def attention_backward_kernel(
    tiles, rows, cont_len, heads, info_ref, qkv_ref, grad_ref, out_ref, dkey_ref, dvalue_ref
):
    h = pl.program_id(0)
    scale = 1.0 / math.sqrt(HD)
    me, plan = attention_tiles(info_ref, tiles, rows, cont_len)

    def columns(kind):
        return pl.ds(pl.multiple_of((kind * heads + h) * HD, HD), HD)

    def load(kind, block):
        return qkv_ref[block ^ me, :, columns(kind)]

    seen = set()
    for block, keys in plan:
        query = load(0, block)
        grad = grad_ref[block ^ me, :, columns(0)]
        probs = softmax_tiles(query, [(load(1, kb), mask) for kb, mask in keys], scale)
        gprobs = [dot_nt(grad, load(2, kb)) for kb, _ in keys]
        delta = jnp.sum(probs[0] * gprobs[0], axis=-1, keepdims=True)
        for p, g in zip(probs[1:], gprobs[1:]):
            delta = delta + jnp.sum(p * g, axis=-1, keepdims=True)
        dquery = None
        for p, g, (kb, _) in zip(probs, gprobs, keys):
            dscore = (p * (g - delta)).astype(BF)
            term = dot_nn(dscore, load(1, kb))
            dquery = term if dquery is None else dquery + term
            dkey = dot_tn(dscore, query)
            dvalue = dot_tn(p.astype(BF), grad)
            if kb in seen:
                dkey_ref[kb] += dkey
                dvalue_ref[kb] += dvalue
            else:
                dkey_ref[kb] = dkey
                dvalue_ref[kb] = dvalue
                seen.add(kb)
        out_ref[block ^ me, :, columns(0)] = (dquery * scale).astype(BF)
    for kb in sorted(seen):
        out_ref[kb ^ me, :, columns(1)] = (dkey_ref[kb] * scale).astype(BF)
        out_ref[kb ^ me, :, columns(2)] = dvalue_ref[kb].astype(BF)


def attention_cost(blocks, rows, heads, matmuls):
    tiles = blocks // 2
    pairs = (tiles * (tiles + 1)) // 2 + tiles * (tiles + 1)
    return pl.CostEstimate(
        flops=2 * matmuls * pairs * heads * rows * rows * HD,
        transcendentals=pairs * heads * rows * rows,
        bytes_accessed=2 * blocks * rows * heads * HD * (4 if matmuls == 2 else 7),
    )


def attention_forward(info, qkv, cont_len):
    blocks, rows, width = qkv.shape
    heads = width // (3 * HD)
    return pl.pallas_call(
        partial(attention_forward_kernel, blocks // 2, rows, cont_len, heads),
        grid=(heads,),
        in_specs=[
            pl.BlockSpec(memory_space=pltpu.SMEM),
            pl.BlockSpec((blocks, rows, width), lambda h: (0, 0, 0)),
        ],
        out_specs=pl.BlockSpec((blocks, rows, heads * HD), lambda h: (0, 0, 0)),
        out_shape=jax.ShapeDtypeStruct((blocks, rows, heads * HD), BF),
        compiler_params=pltpu.CompilerParams(vmem_limit_bytes=40 << 20),
        cost_estimate=attention_cost(blocks, rows, heads, 2),
        name="attention_forward",
    )(info, qkv)


def attention_backward(info, qkv, grad, cont_len):
    blocks, rows, width = qkv.shape
    heads = width // (3 * HD)
    return pl.pallas_call(
        partial(attention_backward_kernel, blocks // 2, rows, cont_len, heads),
        grid=(heads,),
        in_specs=[
            pl.BlockSpec(memory_space=pltpu.SMEM),
            pl.BlockSpec((blocks, rows, width), lambda h: (0, 0, 0)),
            pl.BlockSpec((blocks, rows, heads * HD), lambda h: (0, 0, 0)),
        ],
        out_specs=pl.BlockSpec((blocks, rows, width), lambda h: (0, 0, 0)),
        out_shape=jax.ShapeDtypeStruct((blocks, rows, width), BF),
        scratch_shapes=[
            pltpu.VMEM((blocks, rows, HD), F32),
            pltpu.VMEM((blocks, rows, HD), F32),
        ],
        compiler_params=pltpu.CompilerParams(vmem_limit_bytes=40 << 20),
        cost_estimate=attention_cost(blocks, rows, heads, 7),
        name="attention_backward",
    )(info, qkv, grad)


def grad_matmul_kernel(n_left, spans, *refs):
    out_ref = refs[-1]
    total = None
    for li, lo, ri, ro, size in spans:
        left = refs[li][pl.ds(lo, size), :]
        right = refs[n_left + ri][pl.ds(ro, size), :]
        term = dot_tn(left, right)
        total = term if total is None else total + term
    out_ref[...] = total.astype(BF)


def row_chunks(pieces, order, rows, chunk):
    where = {}
    place = 0
    spots = []
    for index, piece in enumerate(pieces):
        for offset in range(0, piece.shape[0], chunk):
            spots.append((index, offset))
    per_block = rows // chunk
    for block in order:
        where[block] = spots[place : place + per_block]
        place += per_block
    return [spot for block in sorted(where) for spot in where[block]]


def grad_matmul(lefts, left_order, rights, right_order, rows, name):
    chunk = min([rows] + [p.shape[0] for p in list(lefts) + list(rights)])
    spans = []
    for left, right in zip(
        row_chunks(lefts, left_order, rows, chunk), row_chunks(rights, right_order, rows, chunk)
    ):
        last = spans[-1] if spans else None
        if last and left == (last[0], last[1] + last[4]) and right == (last[2], last[3] + last[4]):
            spans[-1] = last[:4] + (last[4] + chunk,)
        else:
            spans.append(left + right + (chunk,))
    d = lefts[0].shape[1]
    n = rights[0].shape[1]
    tile = 256
    total_rows = sum(p.shape[0] for p in lefts)
    return pl.pallas_call(
        partial(grad_matmul_kernel, len(lefts), spans),
        grid=(d // tile,),
        in_specs=[pl.BlockSpec((p.shape[0], tile), lambda i: (0, i)) for p in lefts]
        + [pl.BlockSpec(p.shape, lambda i: (0, 0), pipeline_mode=pl.Buffered(1)) for p in rights],
        out_specs=pl.BlockSpec((tile, n), lambda i: (i, 0)),
        out_shape=jax.ShapeDtypeStruct((d, n), BF),
        compiler_params=pltpu.CompilerParams(vmem_limit_bytes=40 << 20),
        cost_estimate=pl.CostEstimate(
            flops=2 * total_rows * d * n,
            transcendentals=0,
            bytes_accessed=2 * (total_rows * (d + n) + d * n),
        ),
        name=name,
    )(*lefts, *rights)


def assemble_kernel(turn, count, width, ctx_ref, *refs):
    pieces, outs = refs[:count], refs[count:]
    step = pl.program_id(0)
    for k in range(count):

        @pl.when(step == k)
        def _():
            for i, out in enumerate(outs):
                part = pieces[k][:, i * width : (i + 1) * width].astype(F32)
                out[...] = part.T if turn else part


def assemble(ctx, pieces, turn, outputs, name):
    count = len(pieces)
    rows, cols = pieces[0].shape
    width = cols // outputs
    if turn:
        block, shape = (width, rows), (width * count, rows)
        index = lambda k, ctx_ref: (k ^ ctx_ref[0], 0)
    else:
        block, shape = (rows, width), (rows, width * count)
        index = lambda k, ctx_ref: (0, k ^ ctx_ref[0])
    return pl.pallas_call(
        partial(assemble_kernel, turn, count, width),
        grid_spec=pltpu.PrefetchScalarGridSpec(
            num_scalar_prefetch=1,
            grid=(count,),
            in_specs=[
                pl.BlockSpec((rows, cols), lambda k, ctx_ref: (0, 0), pipeline_mode=pl.Buffered(1))
                for _ in pieces
            ],
            out_specs=[pl.BlockSpec(block, index) for _ in range(outputs)],
        ),
        out_shape=[jax.ShapeDtypeStruct(shape, F32) for _ in range(outputs)],
        compiler_params=pltpu.CompilerParams(vmem_limit_bytes=32 << 20),
        cost_estimate=pl.CostEstimate(
            flops=0, transcendentals=0, bytes_accessed=6 * count * rows * cols
        ),
        name=name,
    )(ctx[None].astype(jnp.int32), *pieces)


def gelu_and_slope(u):
    half = 0.5 * (1.0 + lax.erf(u * math.sqrt(0.5)))
    density = jnp.exp(-0.5 * u * u) * (1.0 / math.sqrt(2.0 * math.pi))
    return u * half, half + u * density


def forward_kernel(pieces, rows, *refs):
    lefts, (w_ref, bias_ref, hidden_ref, slope_ref) = refs[: len(pieces)], refs[len(pieces) :]
    for left, (start, size) in zip(lefts, pieces):
        pre_act = dot_nn(left[...], w_ref[...]) + bias_ref[...]
        hidden, slope = gelu_and_slope(pre_act)
        hidden_ref[pl.ds(start, size), :] = hidden.astype(BF)
        slope_ref[pl.ds(start, size), :] = slope


def feed_forward(lefts, starts, weights, bias, units, name):
    total = sum(p.shape[0] for p in lefts)
    width = lefts[0].shape[1]
    tile = 256
    pieces = [(start, p.shape[0]) for start, p in zip(starts, lefts)]
    return pl.pallas_call(
        partial(forward_kernel, pieces, total),
        grid=(units // tile,),
        in_specs=[
            pl.BlockSpec(p.shape, lambda i: (0, 0), pipeline_mode=pl.Buffered(1)) for p in lefts
        ]
        + [
            pl.BlockSpec((width, tile), lambda i: (0, i)),
            pl.BlockSpec((1, tile), lambda i: (0, i)),
        ],
        out_specs=[pl.BlockSpec((total, tile), lambda i: (0, i))] * 2,
        out_shape=[
            jax.ShapeDtypeStruct((total, units), BF),
            jax.ShapeDtypeStruct((total, units), F32),
        ],
        compiler_params=pltpu.CompilerParams(vmem_limit_bytes=48 << 20),
        cost_estimate=pl.CostEstimate(
            flops=2 * total * width * units,
            transcendentals=0,
            bytes_accessed=2 * (total * width + width * units) + 6 * total * units,
        ),
        name=name,
    )(*lefts, weights, bias)


def backward_kernel(pieces, *refs):
    lefts, (w_ref, slope_ref, grad_ref, sum_ref) = refs[: len(pieces)], refs[len(pieces) :]
    sums = None
    for left, (start, size) in zip(lefts, pieces):
        grad = dot_nn(left[...], w_ref[...]) * slope_ref[pl.ds(start, size), :]
        grad = grad.astype(BF)
        grad_ref[pl.ds(start, size), :] = grad
        part = jnp.sum(grad.astype(F32), axis=0, keepdims=True)
        sums = part if sums is None else sums + part
    sum_ref[...] = sums


def feed_backward(lefts, starts, weights, slope, units, name):
    total = sum(p.shape[0] for p in lefts)
    width = lefts[0].shape[1]
    tile = 256
    skip = units // tile
    pieces = [(start, p.shape[0]) for start, p in zip(starts, lefts)]
    return pl.pallas_call(
        partial(backward_kernel, pieces),
        grid=(units // tile,),
        in_specs=[
            pl.BlockSpec(p.shape, lambda i: (0, 0), pipeline_mode=pl.Buffered(1)) for p in lefts
        ]
        + [
            pl.BlockSpec((width, tile), lambda i: (0, skip + i)),
            pl.BlockSpec((total, tile), lambda i: (0, i)),
        ],
        out_specs=[
            pl.BlockSpec((total, tile), lambda i: (0, i)),
            pl.BlockSpec((1, tile), lambda i: (0, i)),
        ],
        out_shape=[
            jax.ShapeDtypeStruct((total, units), BF),
            jax.ShapeDtypeStruct((1, units), F32),
        ],
        compiler_params=pltpu.CompilerParams(vmem_limit_bytes=48 << 20),
        cost_estimate=pl.CostEstimate(
            flops=2 * total * width * units,
            transcendentals=0,
            bytes_accessed=2 * (total * width + width * units) + 6 * total * units,
        ),
        name=name,
    )(*lefts, weights, slope)


def gather_small(packed, size):
    index = lax.axis_index("fsdp")
    out = lax.dynamic_update_slice(
        jnp.zeros((size,) + packed.shape, packed.dtype), packed[None], (index, 0)
    )
    for step in range(1, size):
        moved = lax.ppermute(packed, "fsdp", [(i, (i + step) % size) for i in range(size)])
        out = lax.dynamic_update_slice(out, moved[None], ((index + size - step) % size, 0))
    return out


def body(
    prompt_input,
    continuation_input,
    prompt_lengths,
    continuation_lengths,
    query_weight,
    key_weight,
    value_weight,
    query_bias,
    value_bias,
    output_weight,
    output_bias,
    first_gain,
    first_shift,
    second_gain,
    second_shift,
    up_weight,
    up_bias,
    down_weight,
    down_bias,
    prompt_cotangent,
    continuation_cotangent,
):
    prompt_dev = prompt_input.shape[1]
    cont_dev = continuation_input.shape[1]
    cont_len = continuation_input.shape[2]
    width = prompt_input.shape[2]
    rows = prompt_dev
    fsdp_size = lax.axis_size("fsdp")
    ctx_size = lax.axis_size("ctx")
    tp_size = lax.axis_size("tp")
    assert ctx_size == 4 and tp_size == 2 and cont_dev * cont_len == rows
    blocks = ctx_size * tp_size
    total_rows = blocks * rows
    z = lax.axis_index("fsdp")
    ctx = lax.axis_index("ctx")
    tp = lax.axis_index("tp")
    me = 2 * ctx + tp

    heads_tp = query_bias.shape[0]
    heads = heads_tp // ctx_size
    head_width = heads * HD
    units = up_weight.shape[1] // ctx_size
    unit_rows = units // HD
    d_local = query_weight.shape[0]

    def cols(weight, count):
        return lax.dynamic_slice_in_dim(weight, ctx * count, count, axis=1)

    def rws(weight, count):
        return lax.dynamic_slice_in_dim(weight, ctx * count, count, axis=0)

    attn_shard = jnp.concatenate(
        [
            cols(query_weight, head_width),
            cols(key_weight, head_width),
            cols(value_weight, head_width),
            rws(output_weight, head_width).T,
        ],
        axis=1,
    )
    feed_shard = jnp.concatenate([cols(up_weight, units), rws(down_weight, units).T], axis=1)
    attn_full = lax.all_gather(attn_shard, "fsdp", axis=0, tiled=True)
    w_qkv = attn_full[:, : 3 * head_width]
    w_out = attn_full[:, 3 * head_width :]
    w_feed = lax.all_gather(feed_shard, "fsdp", axis=0, tiled=True)
    w_up = w_feed[:, :units]
    w_down = w_feed[:, units:]

    packed = jnp.concatenate(
        [
            output_bias,
            first_gain,
            first_shift,
            second_gain,
            second_shift,
            down_bias,
            rws(query_bias, heads).reshape(-1),
            rws(value_bias, heads).reshape(-1),
            rws(up_bias, unit_rows).reshape(-1),
        ]
    )
    small = gather_small(after(packed, attn_shard), fsdp_size).astype(F32)
    vectors = [small[:, i * d_local : (i + 1) * d_local].reshape(-1) for i in range(6)]
    obias, gain_one, shift_one, gain_two, shift_two, dbias = vectors
    hd_local = HD // fsdp_size

    def head_vector(start, count):
        piece = small[:, start : start + count * hd_local].reshape(fsdp_size, count, hd_local)
        return piece.transpose(1, 0, 2).reshape(-1)

    start = 6 * d_local
    qbias = head_vector(start, heads)
    vbias = head_vector(start + heads * hd_local, heads)
    ubias = head_vector(start + 2 * heads * hd_local, unit_rows)
    qkv_bias = jnp.concatenate([qbias, jnp.zeros_like(qbias), vbias])

    lens = continuation_lengths[0]
    lens_high = swap_high(lens)
    info = jnp.concatenate(
        [me[None].astype(jnp.int32), prompt_lengths, lens, swap_low(lens), lens_high, swap_low(lens_high)]
    )

    def own_pair(first, second):
        a = first[0]
        b = second[0].reshape(rows, width)
        return jnp.where(tp == 0, a, b), jnp.where(tp == 0, b, a)

    in_own, in_other = own_pair(prompt_input, continuation_input)
    up_own, up_other = own_pair(prompt_cotangent, continuation_cotangent)
    up_pair = jnp.concatenate([up_own, up_other], axis=0)
    stacked = jnp.concatenate([in_own, in_other], axis=0).astype(F32)
    stacked = after(stacked, feed_shard)
    normed_pair, inverse_pair = normalize(stacked)
    act_pieces = gather_ctx((normed_pair * gain_one + shift_one).astype(BF))
    act_one = jnp.concatenate(act_pieces, axis=0)
    normed_one = normed_pair[:rows]
    inverse_one = inverse_pair[:rows]
    x_own = stacked[:rows]
    natural = list(range(blocks))
    grouped = [p for group in GROUPS for p in group]

    qkv = (jnp.dot(act_one, w_qkv, preferred_element_type=F32) + qkv_bias).astype(BF)
    qkv = qkv.reshape(blocks, rows, 3 * head_width)
    up_pieces = gather_ctx(after(up_pair, act_one))
    attended = attention_forward(info, qkv, cont_len)

    def scatter_parts(lefts, order, right):
        parts = {}
        for left, pair in zip(lefts, order):
            res = dot_nt(left, right).astype(BF)
            parts[pair[0]] = res[:rows]
            parts[pair[1]] = res[rows:]
        return parts

    def row_pairs(value):
        flat = value.reshape(total_rows, -1)
        return [flat[p * rows : (p + 2) * rows] for p in (6, 4, 2, 0)]

    pairs = ((6, 7), (4, 5), (2, 3), (0, 1))
    attn_sum = scatter_blocks(
        scatter_parts(row_pairs(attended), pairs, w_out)
    )
    middle = x_own + (attn_sum + obias)
    normed_two, inverse_two = normalize(middle)
    act_two_own = (normed_two * gain_two + shift_two).astype(BF)
    act_two_own, *up_pieces = lax.optimization_barrier((act_two_own, *up_pieces))
    act_two = gather_blocks(act_two_own)

    act_two_flat = [piece for group in act_two for piece in group]
    starts = [0, 2, 1, 3, 4, 6, 5, 5.5, 7, 7.5]
    starts = [int(p * rows) for p in starts]
    hidden, slope = feed_forward(
        act_two_flat, starts, w_feed, ubias[None], units, "feed_forward"
    )
    down_term = grad_matmul(up_pieces, natural, [hidden], natural, rows, "down_weight_term")
    down_piece = lax.psum_scatter(down_term, "fsdp", scatter_dimension=0, tiled=True)
    pair_starts = [0, 2 * rows, 4 * rows, 6 * rows]
    slope, down_term = lax.optimization_barrier((slope, down_term))
    grad_pre, ubias_sum = feed_backward(
        up_pieces, pair_starts, w_feed, slope, units, "feed_backward"
    )

    grad_act_two = scatter_blocks(scatter_parts(row_pairs(grad_pre), pairs, w_up))
    up_term = grad_matmul(act_two_flat, grouped, [grad_pre], natural, rows, "up_weight_term")
    up_piece = lax.psum_scatter(up_term, "fsdp", scatter_dimension=0, tiled=True)
    mlp_parts = scatter_parts(row_pairs(hidden), pairs, w_down)
    grad_middle = up_own.astype(F32) + norm_backward(
        after(grad_act_two, up_term), normed_two, inverse_two, gain_two
    )
    middle_low_own = grad_middle.astype(BF)
    middle_low = gather_blocks(middle_low_own)

    grad_attended = []
    for group in middle_low:
        lhs = jnp.concatenate(group, axis=0)
        grad_attended.append(jnp.dot(lhs, w_out, preferred_element_type=F32).astype(BF))
    by_block = {}
    for pair, piece in zip(GROUPS, grad_attended):
        by_block[pair[0]], by_block[pair[1]] = piece[:rows], piece[rows:]
    grad_attended = jnp.stack([by_block[p] for p in range(blocks)])
    middle_flat = [piece for group in middle_low for piece in group]
    grad_attended, mlp_parts, *middle_flat = lax.optimization_barrier(
        (grad_attended, mlp_parts, *middle_flat)
    )
    dqkv = attention_backward(info, qkv, grad_attended, cont_len)
    dqkv, down_piece = lax.optimization_barrier((dqkv, down_piece))
    mlp_sum = scatter_blocks(mlp_parts)
    dqkv_flat = dqkv.reshape(total_rows, 3 * head_width)
    out_term = grad_matmul(
        middle_flat, grouped, [attended.reshape(total_rows, head_width)], natural, rows, "output_weight_term"
    )
    qkv_term = grad_matmul(act_pieces, natural, [dqkv_flat], natural, rows, "attention_weight_term")
    attn_term = jnp.concatenate([qkv_term, out_term], axis=1)
    attn_piece = lax.psum_scatter(attn_term, "fsdp", scatter_dimension=0, tiled=True)
    dqkv, mlp_sum, attn_term = lax.optimization_barrier((dqkv, mlp_sum, attn_term))
    result = (middle + (mlp_sum + dbias)).astype(BF)
    grad_act_one = scatter_blocks(
        scatter_parts(row_pairs(dqkv), pairs, w_qkv)
    )
    grad_stacked = (
        grad_middle + norm_backward(grad_act_one, normed_one, inverse_one, gain_one)
    ).astype(BF)
    result_other = swap_tp(result)

    def to_outputs(own, other):
        first = jnp.where(tp == 0, own, other)
        second = jnp.where(tp == 0, other, own)
        return first[None], second.reshape(1, cont_dev, cont_len, width)

    def colsum(value):
        return jnp.sum(value, axis=0, dtype=F32)

    d_vectors = jnp.stack(
        [
            colsum(middle_low_own),
            colsum(grad_act_one * normed_one),
            colsum(grad_act_one),
            colsum(grad_act_two * normed_two),
            colsum(grad_act_two),
            colsum(up_own),
        ]
    )
    for swap in (swap_tp, swap_low, swap_high):
        d_vectors = d_vectors + swap(d_vectors)
    colsum_qkv = colsum(dqkv_flat)
    head_terms = jnp.concatenate(
        [
            colsum_qkv[:head_width].reshape(heads, HD),
            colsum_qkv[2 * head_width :].reshape(heads, HD),
            ubias_sum.reshape(unit_rows, HD),
        ]
    )

    def by_owner(value):
        count = value.shape[0]
        return value.reshape(count, fsdp_size, -1).transpose(1, 0, 2).reshape(fsdp_size, -1)

    owners = jnp.concatenate([by_owner(d_vectors), by_owner(head_terms)], axis=1)
    summed = lax.dynamic_slice_in_dim(owners, z, 1, axis=0)
    for step in range(1, fsdp_size):
        share = lax.dynamic_slice_in_dim(owners, (z + step) % fsdp_size, 1, axis=0)
        pairs = [(i, (i + step) % fsdp_size) for i in range(fsdp_size)]
        summed = summed + lax.ppermute(share, "fsdp", pairs)
    summed = summed[0]
    obias_grad, gain_one_grad, shift_one_grad, gain_two_grad, shift_two_grad, dbias_grad = [
        summed[i * d_local : (i + 1) * d_local] for i in range(6)
    ]
    mine = summed[6 * d_local :].reshape(2 * heads + unit_rows, hd_local)
    mine_high = swap_high(mine)
    relative = jnp.stack([mine, swap_low(mine), mine_high, swap_low(mine_high)])
    head_sums = jnp.stack(
        [lax.dynamic_index_in_dim(relative, ctx ^ i, keepdims=False) for i in range(ctx_size)]
    )
    qbias_grad = head_sums[:, :heads].reshape(heads_tp, hd_local)
    vbias_grad = head_sums[:, heads : 2 * heads].reshape(heads_tp, hd_local)
    ubias_grad = head_sums[:, 2 * heads :].reshape(ctx_size * unit_rows, hd_local)

    def spread(piece):
        high = swap_high(piece)
        return [piece, swap_low(piece), high, swap_low(high)]

    grad_stacked, up_piece, *down_pieces = lax.optimization_barrier(
        (grad_stacked, up_piece, *spread(down_piece))
    )
    stacked_other = swap_tp(grad_stacked)
    down_grad = assemble(ctx, down_pieces, True, 1, "down_weight_grad")[0]
    up_grad = assemble(ctx, spread(up_piece), False, 1, "up_weight_grad")[0]
    prompt_output, continuation_output = to_outputs(result, result_other)
    prompt_input_grad, continuation_input_grad = to_outputs(grad_stacked, stacked_other)
    attn_piece, down_grad, up_grad = lax.optimization_barrier((attn_piece, down_grad, up_grad))
    attn_pieces = spread(attn_piece)
    query_grad, key_grad, value_grad = assemble(
        ctx, [p[:, : 3 * head_width] for p in attn_pieces], False, 3, "attention_weight_grads"
    )
    output_grad = assemble(
        ctx, [p[:, 3 * head_width :] for p in attn_pieces], True, 1, "output_weight_grad"
    )[0]
    return (
        prompt_output,
        continuation_output,
        prompt_input_grad,
        continuation_input_grad,
        query_grad,
        key_grad,
        value_grad,
        qbias_grad,
        vbias_grad,
        output_grad,
        obias_grad,
        gain_one_grad,
        shift_one_grad,
        gain_two_grad,
        shift_two_grad,
        up_grad,
        ubias_grad,
        down_grad,
        dbias_grad,
    )


def solution(mesh):
    return jax.shard_map(
        body,
        mesh=mesh,
        in_specs=(
            P("fsdp", "ctx", None),
            P("fsdp", "ctx", None, None),
            P("fsdp"),
            P("fsdp", "ctx"),
            P("fsdp", "tp"),
            P("fsdp", "tp"),
            P("fsdp", "tp"),
            P("tp", "fsdp"),
            P("tp", "fsdp"),
            P("tp", "fsdp"),
            P("fsdp"),
            P("fsdp"),
            P("fsdp"),
            P("fsdp"),
            P("fsdp"),
            P("fsdp", "tp"),
            P("tp", "fsdp"),
            P("tp", "fsdp"),
            P("fsdp"),
            P("fsdp", "ctx", None),
            P("fsdp", "ctx", None, None),
        ),
        out_specs=(
            P("fsdp", "ctx", None),
            P("fsdp", "ctx", None, None),
            P("fsdp", "ctx", None),
            P("fsdp", "ctx", None, None),
            P("fsdp", "tp"),
            P("fsdp", "tp"),
            P("fsdp", "tp"),
            P("tp", "fsdp"),
            P("tp", "fsdp"),
            P("tp", "fsdp"),
            P("fsdp"),
            P("fsdp"),
            P("fsdp"),
            P("fsdp"),
            P("fsdp"),
            P("fsdp", "tp"),
            P("tp", "fsdp"),
            P("tp", "fsdp"),
            P("fsdp"),
        ),
        check_vma=False,
    )
```

```python
from functools import partial
import math

import jax
import jax.numpy as jnp
from jax import lax
from jax.experimental import pallas as pl
from jax.experimental.pallas import tpu as pltpu
from jax.sharding import PartitionSpec as P

HD = 128
BF = jnp.bfloat16
F32 = jnp.float32
VMEM_BYTES = 62 << 20


norm_epsilon = 1e-05


def normalize(values):
    centre = jnp.mean(values, axis=-1, keepdims=True)
    centered = values - centre
    inverse = lax.rsqrt(jnp.mean(centered * centered, axis=-1, keepdims=True) + norm_epsilon)
    return (centered * inverse, inverse)


def norm_backward(incoming, normed, inverse, gain_vec):
    scaled = incoming * gain_vec
    return inverse * (
        scaled
        - jnp.mean(scaled, axis=-1, keepdims=True)
        - normed * jnp.mean(scaled * normed, axis=-1, keepdims=True)
    )


def swap_tp(value):
    return lax.ppermute(value, "tp", [(0, 1), (1, 0)])


def swap_low(value):
    return lax.ppermute(value, "ctx", [(0, 1), (1, 0), (2, 3), (3, 2)])


def swap_high(value):
    return lax.ppermute(value, "ctx", [(0, 2), (2, 0), (1, 3), (3, 1)])


def stage(*values):
    return lax.optimization_barrier(values)


def swap_any(value, distance):
    return lax.ppermute(value, ("ctx", "tp"), [(i, i ^ distance) for i in range(8)])


GATHERED = (0, 2, 1, 4, 3, 6, 5, 7)


def scatter_first(sums):
    return [swap_tp(sums[2]), swap_high(sums[3])]


def scatter_second(sums, first):
    half = sums[1].shape[0]
    by_tp, by_high = first
    across = sums[1].astype(F32) + by_high[:half].astype(F32)
    along = sums[4].astype(F32) + by_tp[half:].astype(F32)
    return [swap_tp(across.astype(BF)), swap_high(along.astype(BF))]


def scatter_sum(sums, first, second):
    half = sums[1].shape[0]
    by_tp = jnp.concatenate([second[0], first[0][:half]], axis=0)
    by_high = jnp.concatenate([first[1][half:], second[1]], axis=0)
    return sums[0] + by_tp.astype(F32) + by_high.astype(F32)


def pair_mask(rows, limits, split):
    row = lax.broadcasted_iota(jnp.int32, (rows, rows), 0)
    col = lax.broadcasted_iota(jnp.int32, (rows, rows), 1)
    mask = col <= row
    for seq in range(rows // split):
        inside = (row >= seq * split) & (row < (seq + 1) * split)
        limit = jnp.where(inside, limits[seq] + seq * split, 0)
        lower = jnp.where(inside, seq * split, 0)
        ok = (col >= lower) & (col < limit)
        mask = mask & (jnp.logical_not(inside) | ok)
    return mask


def attention_tiles(info_ref, tiles, rows, cont_len):
    me = info_ref[0]
    prompt_len = info_ref[1]
    per_block = rows // cont_len
    col = lax.broadcasted_iota(jnp.int32, (rows, rows), 1)
    row = lax.broadcasted_iota(jnp.int32, (rows, rows), 0)
    plan = []
    for t in range(tiles):
        keys = []
        for j in range(t + 1):
            mask = None
            if j == tiles - 1:
                mask = (col + j * rows) < prompt_len
            if j == t:
                mask = (col <= row) if mask is None else mask & (col <= row)
            keys.append((2 * j, mask))
        plan.append((2 * t, keys))
    for t in range(tiles):
        keys = []
        for j in range(tiles):
            keys.append((2 * j, (col + j * rows) < prompt_len if j == tiles - 1 else None))
        base = 2 + ((2 * t) ^ (me & (2 * tiles - 2))) // 2 * per_block
        limits = [info_ref[base + s] for s in range(per_block)]
        keys.append((2 * t + 1, pair_mask(rows, limits, cont_len)))
        plan.append((2 * t + 1, keys))
    return me, plan


def dot_nt(a, b):
    return lax.dot_general(a, b, (((1,), (1,)), ((), ())), preferred_element_type=F32)


def dot_nn(a, b):
    return lax.dot_general(a, b, (((1,), (0,)), ((), ())), preferred_element_type=F32)


def dot_tn(a, b):
    return lax.dot_general(a, b, (((0,), (0,)), ((), ())), preferred_element_type=F32)


def softmax_tiles(query, keys, scale):
    scores = []
    for key, mask in keys:
        score = dot_nt(query, key) * scale
        scores.append(score if mask is None else jnp.where(mask, score, -1e30))
    top = jnp.max(scores[0], axis=-1, keepdims=True)
    for s in scores[1:]:
        top = jnp.maximum(top, jnp.max(s, axis=-1, keepdims=True))
    weights = [jnp.exp(s - top) for s in scores]
    total = jnp.sum(weights[0], axis=-1, keepdims=True)
    for w in weights[1:]:
        total = total + jnp.sum(w, axis=-1, keepdims=True)
    inverse = 1.0 / total
    return [w * inverse for w in weights]


def attention_forward_kernel(tiles, rows, cont_len, heads, info_ref, qkv_ref, out_ref):
    h = pl.program_id(0)
    scale = 1.0 / math.sqrt(HD)
    me, plan = attention_tiles(info_ref, tiles, rows, cont_len)

    def load(kind, block):
        cols = pl.ds(pl.multiple_of((kind * heads + h) * HD, HD), HD)
        return qkv_ref[block ^ me, :, cols]

    for block, keys in plan:
        query = load(0, block)
        probs = softmax_tiles(query, [(load(1, kb), mask) for kb, mask in keys], scale)
        total = None
        for p, (kb, _) in zip(probs, keys):
            term = dot_nn(p.astype(BF), load(2, kb))
            total = term if total is None else total + term
        cols = pl.ds(pl.multiple_of(h * HD, HD), HD)
        out_ref[block ^ me, :, cols] = total.astype(BF)


def attention_backward_kernel(
    tiles, rows, cont_len, heads, info_ref, qkv_ref, grad_ref, out_ref, dkey_ref, dvalue_ref
):
    h = pl.program_id(0)
    scale = 1.0 / math.sqrt(HD)
    me, plan = attention_tiles(info_ref, tiles, rows, cont_len)

    def columns(kind):
        return pl.ds(pl.multiple_of((kind * heads + h) * HD, HD), HD)

    def load(kind, block):
        return qkv_ref[block ^ me, :, columns(kind)]

    seen = set()
    for block, keys in plan:
        query = load(0, block)
        grad = grad_ref[block ^ me, :, columns(0)]
        probs = softmax_tiles(query, [(load(1, kb), mask) for kb, mask in keys], scale)
        gprobs = [dot_nt(grad, load(2, kb)) for kb, _ in keys]
        delta = jnp.sum(probs[0] * gprobs[0], axis=-1, keepdims=True)
        for p, g in zip(probs[1:], gprobs[1:]):
            delta = delta + jnp.sum(p * g, axis=-1, keepdims=True)
        dquery = None
        for p, g, (kb, _) in zip(probs, gprobs, keys):
            dscore = (p * (g - delta)).astype(BF)
            term = dot_nn(dscore, load(1, kb))
            dquery = term if dquery is None else dquery + term
            dkey = dot_tn(dscore, query)
            dvalue = dot_tn(p.astype(BF), grad)
            if kb in seen:
                dkey_ref[kb] += dkey
                dvalue_ref[kb] += dvalue
            else:
                dkey_ref[kb] = dkey
                dvalue_ref[kb] = dvalue
                seen.add(kb)
        out_ref[block ^ me, :, columns(0)] = (dquery * scale).astype(BF)
    for kb in sorted(seen):
        out_ref[kb ^ me, :, columns(1)] = (dkey_ref[kb] * scale).astype(BF)
        out_ref[kb ^ me, :, columns(2)] = dvalue_ref[kb].astype(BF)


def attention_cost(blocks, rows, heads, matmuls):
    tiles = blocks // 2
    pairs = (tiles * (tiles + 1)) // 2 + tiles * (tiles + 1)
    return pl.CostEstimate(
        flops=2 * matmuls * pairs * heads * rows * rows * HD,
        transcendentals=pairs * heads * rows * rows,
        bytes_accessed=2 * blocks * rows * heads * HD * (4 if matmuls == 2 else 7),
    )


def attention_forward(info, qkv, cont_len):
    blocks, rows, width = qkv.shape
    heads = width // (3 * HD)
    return pl.pallas_call(
        partial(attention_forward_kernel, blocks // 2, rows, cont_len, heads),
        grid=(heads,),
        in_specs=[
            pl.BlockSpec(memory_space=pltpu.SMEM),
            pl.BlockSpec((blocks, rows, width), lambda h: (0, 0, 0)),
        ],
        out_specs=pl.BlockSpec((blocks, rows, heads * HD), lambda h: (0, 0, 0)),
        out_shape=jax.ShapeDtypeStruct((blocks, rows, heads * HD), BF),
        compiler_params=pltpu.CompilerParams(vmem_limit_bytes=32 << 20),
        cost_estimate=attention_cost(blocks, rows, heads, 2),
        name="attention_forward",
    )(info, qkv)


def attention_backward(info, qkv, grad, cont_len):
    blocks, rows, width = qkv.shape
    heads = width // (3 * HD)
    return pl.pallas_call(
        partial(attention_backward_kernel, blocks // 2, rows, cont_len, heads),
        grid=(heads,),
        in_specs=[
            pl.BlockSpec(memory_space=pltpu.SMEM),
            pl.BlockSpec((blocks, rows, width), lambda h: (0, 0, 0)),
            pl.BlockSpec((blocks, rows, heads * HD), lambda h: (0, 0, 0)),
        ],
        out_specs=pl.BlockSpec((blocks, rows, width), lambda h: (0, 0, 0)),
        out_shape=jax.ShapeDtypeStruct((blocks, rows, width), BF),
        scratch_shapes=[
            pltpu.VMEM((blocks, rows, HD), F32),
            pltpu.VMEM((blocks, rows, HD), F32),
        ],
        compiler_params=pltpu.CompilerParams(vmem_limit_bytes=32 << 20),
        cost_estimate=attention_cost(blocks, rows, heads, 7),
        name="attention_backward",
    )(info, qkv, grad)


def grad_matmul_kernel(n_left, spans, widths, *refs):
    total = None
    for li, lo, ri, ro, size in spans:
        left = refs[li][pl.ds(lo, size), :]
        right = refs[n_left + ri][pl.ds(ro, size), :]
        term = dot_tn(left, right)
        total = term if total is None else total + term
    start = 0
    for out_ref, n in zip(refs[len(refs) - len(widths) :], widths):
        out_ref[...] = total[:, start : start + n].astype(BF)
        start += n


def row_chunks(pieces, order, rows, chunk):
    where = {}
    place = 0
    spots = []
    for index, piece in enumerate(pieces):
        for offset in range(0, piece.shape[0], chunk):
            spots.append((index, offset))
    per_block = rows // chunk
    for block in order:
        where[block] = spots[place : place + per_block]
        place += per_block
    return [spot for block in sorted(where) for spot in where[block]]


def matched_spans(lefts, left_order, rights, right_order, rows):
    chunk = min([rows] + [p.shape[0] for p in list(lefts) + list(rights)])
    spans = []
    for left, right in zip(
        row_chunks(lefts, left_order, rows, chunk), row_chunks(rights, right_order, rows, chunk)
    ):
        last = spans[-1] if spans else None
        if last and left == (last[0], last[1] + last[4]) and right == (last[2], last[3] + last[4]):
            spans[-1] = last[:4] + (last[4] + chunk,)
        else:
            spans.append(left + right + (chunk,))
    return spans


def grad_matmul(lefts, left_order, rights, right_order, rows, name, widths=None):
    spans = matched_spans(lefts, left_order, rights, right_order, rows)
    d = lefts[0].shape[1]
    n = rights[0].shape[1]
    widths = widths or [n]
    tile = 512
    total_rows = sum(p.shape[0] for p in lefts)
    return pl.pallas_call(
        partial(grad_matmul_kernel, len(lefts), spans, widths),
        grid=(d // tile,),
        in_specs=[pl.BlockSpec((p.shape[0], tile), lambda i: (0, i)) for p in lefts]
        + [pl.BlockSpec(p.shape, lambda i: (0, 0), pipeline_mode=pl.Buffered(1)) for p in rights],
        out_specs=[pl.BlockSpec((tile, w), lambda i: (i, 0)) for w in widths],
        out_shape=[jax.ShapeDtypeStruct((d, w), BF) for w in widths],
        compiler_params=pltpu.CompilerParams(vmem_limit_bytes=32 << 20),
        cost_estimate=pl.CostEstimate(
            flops=2 * total_rows * d * n,
            transcendentals=0,
            bytes_accessed=2 * (total_rows * (d + n) + d * n),
        ),
        name=name,
    )(*lefts, *rights)


def sent_kernel(rows, low_ref, high_ref, w_ref, out_ref):
    for i, left in enumerate((low_ref, high_ref)):
        out_ref[pl.ds(2 * i * rows, 2 * rows), :] = dot_nt(left[...], w_ref[...]).astype(BF)


def kept_kernel(rows, low_ref, high_ref, w_ref, arrived_ref, own_ref, *outs):
    across_ref, to_tp_ref, to_high_ref, along_ref = outs
    half = rows // 2
    low = dot_nt(low_ref[...], w_ref[...])
    low = low + arrived_ref[pl.ds(0, 2 * rows), :].astype(F32)
    own_ref[...] = low[:rows]
    across_ref[...] = low[rows : rows + half].astype(BF)
    to_tp_ref[pl.ds(0, half), :] = low[rows + half :].astype(BF)
    high = dot_nt(high_ref[...], w_ref[...])
    high = (high + arrived_ref[pl.ds(2 * rows, 2 * rows), :].astype(F32)).astype(BF)
    to_tp_ref[pl.ds(half, half), :] = high[rows + half :]
    to_high_ref[pl.ds(0, half), :] = high[rows : rows + half]
    to_high_ref[pl.ds(half, half), :] = high[:half]
    along_ref[...] = high[half:rows]


def partial_blocks(left, rows, weights, column, arrived, name):
    k = left.shape[1]
    d = weights.shape[0]
    tile = 512
    pair = 2 * rows
    if arrived is None:
        first, kernel, more = 1, sent_kernel, []
        outs = [(4 * rows, BF)]
    else:
        first, kernel, more = 0, kept_kernel, [arrived]
        outs = [(rows, F32), (rows // 2, BF), (rows, BF), (rows, BF), (rows // 2, BF)]
    result = pl.pallas_call(
        partial(kernel, rows),
        grid=(d // tile,),
        in_specs=[
            pl.BlockSpec((pair, k), lambda i: (first, 0), pipeline_mode=pl.Buffered(1)),
            pl.BlockSpec((pair, k), lambda i: (first + 2, 0), pipeline_mode=pl.Buffered(1)),
            pl.BlockSpec((tile, k), lambda i: (i, column)),
        ]
        + [pl.BlockSpec((2 * pair, tile), lambda i: (0, i)) for _ in more],
        out_specs=[pl.BlockSpec((n, tile), lambda i: (0, i)) for n, _ in outs],
        out_shape=[jax.ShapeDtypeStruct((n, d), t) for n, t in outs],
        compiler_params=pltpu.CompilerParams(vmem_limit_bytes=VMEM_BYTES),
        cost_estimate=pl.CostEstimate(
            flops=8 * rows * d * k,
            transcendentals=0,
            bytes_accessed=2 * (4 * rows * (k + d) + d * k),
        ),
        name=name,
    )(left, left, weights, *more)
    return result[0] if arrived is None else result


def block_copies(pieces, rows, total):
    seen, plan = set(), []
    for start in range(0, total, rows):
        need = [
            i
            for i, (begin, size) in enumerate(pieces)
            if begin < start + rows and start < begin + size and i not in seen
        ]
        seen.update(need)
        plan.append(need)
    return plan


def piece_copy(refs, pieces, buffer, sems, i):
    begin, size = pieces[i]
    return pltpu.make_async_copy(refs[i], buffer.at[pl.ds(begin, size), :], sems.at[i])


def project_kernel(pieces, rows, *refs):
    lefts, (w_ref, bias_ref, out_ref, buffer, sems) = refs[: len(pieces)], refs[len(pieces) :]
    total = out_ref.shape[0]
    plan = block_copies(pieces, rows, total)

    def compute(p):
        block = pl.ds(p * rows, rows)
        out_ref[block, :] = (dot_nn(buffer[block, :], w_ref[...]) + bias_ref[...]).astype(BF)

    @pl.when(pl.program_id(0) == 0)
    def _():
        for need in plan:
            for i in need:
                piece_copy(lefts, pieces, buffer, sems, i).start()
        for p, need in enumerate(plan):
            for i in need:
                piece_copy(lefts, pieces, buffer, sems, i).wait()
            compute(p)

    @pl.when(pl.program_id(0) > 0)
    def _():
        for p in range(len(plan)):
            compute(p)


def project(lefts, starts, rows, weights, bias, column, n, name):
    total = sum(p.shape[0] for p in lefts)
    width = lefts[0].shape[1]
    pieces = [(start, p.shape[0]) for start, p in zip(starts, lefts)]
    tile = 256
    skip = column // tile
    return pl.pallas_call(
        partial(project_kernel, pieces, rows),
        grid=(n // tile,),
        in_specs=[pl.BlockSpec(memory_space=pl.ANY) for _ in lefts]
        + [
            pl.BlockSpec((width, tile), lambda i: (0, skip + i)),
            pl.BlockSpec((1, tile), lambda i: (0, i)),
        ],
        out_specs=pl.BlockSpec((total, tile), lambda i: (0, i)),
        out_shape=jax.ShapeDtypeStruct((total, n), BF),
        scratch_shapes=[
            pltpu.VMEM((total, width), BF),
            pltpu.SemaphoreType.DMA((len(lefts),)),
        ],
        compiler_params=pltpu.CompilerParams(vmem_limit_bytes=VMEM_BYTES),
        cost_estimate=pl.CostEstimate(
            flops=2 * total * width * n,
            transcendentals=0,
            bytes_accessed=2 * (total * (width + n) + width * n),
        ),
        name=name,
    )(*lefts, weights, bias)


def middle_kernel(pieces, tile, *refs):
    lefts = refs[: len(pieces)]
    att_ref, w_ref, term_ref, grad_ref, buffer, total_ref, sems = refs[len(pieces) :]
    step = pl.program_id(0)

    @pl.when(step == 0)
    def _():
        for i in range(len(pieces)):
            piece_copy(lefts, pieces, buffer, sems, i).start()
        for i in range(len(pieces)):
            piece_copy(lefts, pieces, buffer, sems, i).wait()

    left = buffer[:, pl.ds(pl.multiple_of(step * tile, tile), tile)]
    term_ref[...] = dot_tn(left, att_ref[...]).astype(BF)
    grad = dot_nn(left, w_ref[...])

    @pl.when(step == 0)
    def _():
        total_ref[...] = grad

    @pl.when(step > 0)
    def _():
        total_ref[...] += grad

    @pl.when(step == pl.num_programs(0) - 1)
    def _():
        grad_ref[...] = total_ref[...].astype(BF)


def middle_terms(lefts, starts, attended, weights, column, name):
    total, n = attended.shape
    d = lefts[0].shape[1]
    tile = 512
    pieces = [(start, p.shape[0]) for start, p in zip(starts, lefts)]
    return pl.pallas_call(
        partial(middle_kernel, pieces, tile),
        grid=(d // tile,),
        in_specs=[pl.BlockSpec(memory_space=pl.ANY) for _ in lefts]
        + [
            pl.BlockSpec((total, n), lambda i: (0, 0), pipeline_mode=pl.Buffered(1)),
            pl.BlockSpec((tile, n), lambda i: (i, column)),
        ],
        out_specs=[
            pl.BlockSpec((tile, n), lambda i: (i, 0)),
            pl.BlockSpec((total, n), lambda i: (0, 0)),
        ],
        out_shape=[
            jax.ShapeDtypeStruct((d, n), BF),
            jax.ShapeDtypeStruct((total, n), BF),
        ],
        scratch_shapes=[
            pltpu.VMEM((total, d), BF),
            pltpu.VMEM((total, n), F32),
            pltpu.SemaphoreType.DMA((len(lefts),)),
        ],
        compiler_params=pltpu.CompilerParams(vmem_limit_bytes=VMEM_BYTES),
        cost_estimate=pl.CostEstimate(
            flops=4 * total * d * n,
            transcendentals=0,
            bytes_accessed=2 * total * (d + 2 * n) + 4 * d * n,
        ),
        name=name,
    )(*lefts, attended, weights)


def shard_kernel(n_cols, ctx_ref, *refs):
    ins, out = refs[:-1], refs[-1]
    start = 0
    for i, ref in enumerate(ins):
        value = ref[...] if i < n_cols else ref[...].T
        out[:, start : start + value.shape[1]] = value
        start += value.shape[1]


def weight_shard(ctx, by_column, by_row, size, name):
    d = by_column[0].shape[0]
    count = len(by_column) + len(by_row)
    return pl.pallas_call(
        partial(shard_kernel, len(by_column)),
        grid_spec=pltpu.PrefetchScalarGridSpec(
            num_scalar_prefetch=1,
            grid=(1,),
            in_specs=[pl.BlockSpec((d, size), lambda i, c: (0, c[0])) for _ in by_column]
            + [pl.BlockSpec((size, d), lambda i, c: (c[0], 0)) for _ in by_row],
            out_specs=pl.BlockSpec((d, count * size), lambda i, c: (0, 0)),
        ),
        out_shape=jax.ShapeDtypeStruct((d, count * size), BF),
        compiler_params=pltpu.CompilerParams(vmem_limit_bytes=VMEM_BYTES),
        cost_estimate=pl.CostEstimate(
            flops=0, transcendentals=0, bytes_accessed=4 * d * count * size
        ),
        name=name,
    )(ctx[None].astype(jnp.int32), *by_column, *by_row)


def assemble_kernel(turn, count, width, ctx_ref, *refs):
    pieces, outs = refs[:count], refs[count:]
    step = pl.program_id(0)
    for k in range(count):

        @pl.when(step == k)
        def _():
            for i, out in enumerate(outs):
                part = pieces[k][:, i * width : (i + 1) * width].astype(F32)
                out[...] = part.T if turn else part


def assemble(ctx, pieces, turn, outputs, name):
    count = len(pieces)
    rows, cols = pieces[0].shape
    width = cols // outputs
    if turn:
        block, shape = (width, rows), (width * count, rows)
        index = lambda k, ctx_ref: (k ^ ctx_ref[0], 0)
    else:
        block, shape = (rows, width), (rows, width * count)
        index = lambda k, ctx_ref: (0, k ^ ctx_ref[0])
    return pl.pallas_call(
        partial(assemble_kernel, turn, count, width),
        grid_spec=pltpu.PrefetchScalarGridSpec(
            num_scalar_prefetch=1,
            grid=(count,),
            in_specs=[
                pl.BlockSpec((rows, cols), lambda k, ctx_ref: (0, 0), pipeline_mode=pl.Buffered(1))
                for _ in pieces
            ],
            out_specs=[pl.BlockSpec(block, index) for _ in range(outputs)],
        ),
        out_shape=[jax.ShapeDtypeStruct(shape, F32) for _ in range(outputs)],
        compiler_params=pltpu.CompilerParams(vmem_limit_bytes=VMEM_BYTES),
        cost_estimate=pl.CostEstimate(
            flops=0, transcendentals=0, bytes_accessed=6 * count * rows * cols
        ),
        name=name,
    )(ctx[None].astype(jnp.int32), *pieces)


def gelu_and_slope(u):
    half = 0.5 * (1.0 + lax.erf(u * math.sqrt(0.5)))
    density = jnp.exp(-0.5 * u * u) * (1.0 / math.sqrt(2.0 * math.pi))
    return u * half, half + u * density


def feed_kernel(act_pieces, up_pieces, rows, *refs):
    count = len(act_pieces)
    acts, ups = refs[:count], refs[count : count + len(up_pieces)]
    (
        w_up_ref,
        w_down_ref,
        bias_ref,
        hidden_ref,
        grad_ref,
        sum_ref,
        act_buffer,
        up_buffer,
        act_sems,
        up_sems,
    ) = refs[count + len(up_pieces) :]
    total = hidden_ref.shape[0]
    act_plan = block_copies(act_pieces, rows, total)
    up_plan = block_copies(up_pieces, rows, total)

    def compute(p):
        block = pl.ds(p * rows, rows)
        pre_act = dot_nn(act_buffer[block, :], w_up_ref[...]) + bias_ref[...]
        grad_hidden = dot_nn(up_buffer[block, :], w_down_ref[...])
        hidden, slope = gelu_and_slope(pre_act)
        hidden_ref[block, :] = hidden.astype(BF)
        grad = (grad_hidden * slope).astype(BF)
        grad_ref[block, :] = grad
        part = jnp.sum(grad.astype(F32), axis=0, keepdims=True)
        if p == 0:
            sum_ref[...] = part
        else:
            sum_ref[...] += part

    def act_copy(i):
        return piece_copy(acts, act_pieces, act_buffer, act_sems, i)

    def up_copy(i):
        return piece_copy(ups, up_pieces, up_buffer, up_sems, i)

    @pl.when(pl.program_id(0) == 0)
    def _():
        for act_need, up_need in zip(act_plan, up_plan):
            for i in act_need:
                act_copy(i).start()
            for i in up_need:
                up_copy(i).start()
        for p, (act_need, up_need) in enumerate(zip(act_plan, up_plan)):
            for i in act_need:
                act_copy(i).wait()
            for i in up_need:
                up_copy(i).wait()
            compute(p)

    @pl.when(pl.program_id(0) > 0)
    def _():
        for p in range(len(act_plan)):
            compute(p)


def feed_both(acts, act_starts, ups, up_starts, rows, weights, bias, units, name):
    total = sum(p.shape[0] for p in acts)
    width = acts[0].shape[1]
    tile = 256
    skip = units // tile
    act_pieces = [(start, p.shape[0]) for start, p in zip(act_starts, acts)]
    up_pieces = [(start, p.shape[0]) for start, p in zip(up_starts, ups)]
    return pl.pallas_call(
        partial(feed_kernel, act_pieces, up_pieces, rows),
        grid=(units // tile,),
        in_specs=[pl.BlockSpec(memory_space=pl.ANY) for _ in acts + ups]
        + [
            pl.BlockSpec((width, tile), lambda i: (0, i)),
            pl.BlockSpec((width, tile), lambda i: (0, skip + i)),
            pl.BlockSpec((1, tile), lambda i: (0, i)),
        ],
        out_specs=[
            pl.BlockSpec((total, tile), lambda i: (0, i)),
            pl.BlockSpec((total, tile), lambda i: (0, i)),
            pl.BlockSpec((1, tile), lambda i: (0, i)),
        ],
        out_shape=[
            jax.ShapeDtypeStruct((total, units), BF),
            jax.ShapeDtypeStruct((total, units), BF),
            jax.ShapeDtypeStruct((1, units), F32),
        ],
        scratch_shapes=[
            pltpu.VMEM((total, width), BF),
            pltpu.VMEM((total, width), BF),
            pltpu.SemaphoreType.DMA((len(acts),)),
            pltpu.SemaphoreType.DMA((len(ups),)),
        ],
        compiler_params=pltpu.CompilerParams(vmem_limit_bytes=VMEM_BYTES),
        cost_estimate=pl.CostEstimate(
            flops=4 * total * width * units,
            transcendentals=0,
            bytes_accessed=4 * (total * width + width * units + total * units),
        ),
        name=name,
    )(*acts, *ups, weights, weights, bias)


def gather_small(packed, size):
    index = lax.axis_index("fsdp")
    out = lax.dynamic_update_slice(
        jnp.zeros((size,) + packed.shape, packed.dtype), packed[None], (index, 0)
    )
    for step in range(1, size):
        moved = lax.ppermute(packed, "fsdp", [(i, (i + step) % size) for i in range(size)])
        out = lax.dynamic_update_slice(out, moved[None], ((index + size - step) % size, 0))
    return out


def body(
    prompt_input,
    continuation_input,
    prompt_lengths,
    continuation_lengths,
    query_weight,
    key_weight,
    value_weight,
    query_bias,
    value_bias,
    output_weight,
    output_bias,
    first_gain,
    first_shift,
    second_gain,
    second_shift,
    up_weight,
    up_bias,
    down_weight,
    down_bias,
    prompt_cotangent,
    continuation_cotangent,
):
    prompt_dev = prompt_input.shape[1]
    cont_dev = continuation_input.shape[1]
    cont_len = continuation_input.shape[2]
    width = prompt_input.shape[2]
    rows = prompt_dev
    fsdp_size = lax.axis_size("fsdp")
    ctx_size = lax.axis_size("ctx")
    tp_size = lax.axis_size("tp")
    assert ctx_size == 4 and tp_size == 2 and cont_dev * cont_len == rows
    blocks = ctx_size * tp_size
    total_rows = blocks * rows
    z = lax.axis_index("fsdp")
    ctx = lax.axis_index("ctx")
    tp = lax.axis_index("tp")
    me = 2 * ctx + tp

    heads_tp = query_bias.shape[0]
    heads = heads_tp // ctx_size
    head_width = heads * HD
    units = up_weight.shape[1] // ctx_size
    unit_rows = units // HD
    d_local = query_weight.shape[0]

    def rws(weight, count):
        return lax.dynamic_slice_in_dim(weight, ctx * count, count, axis=0)

    attn_shard = weight_shard(
        ctx, [query_weight, key_weight, value_weight], [output_weight], head_width, "attention_shard"
    )
    (
        attn_shard,
        prompt_input,
        continuation_input,
        prompt_cotangent,
        continuation_cotangent,
        continuation_lengths,
    ) = stage(
        attn_shard,
        prompt_input,
        continuation_input,
        prompt_cotangent,
        continuation_cotangent,
        continuation_lengths,
    )
    attn_full = lax.all_gather(attn_shard, "fsdp", axis=0, tiled=True)
    w_qkv = attn_full[:, : 3 * head_width]
    def own_pair(first, second):
        a = first[0]
        b = second[0].reshape(rows, width)
        return jnp.where(tp == 0, a, b), jnp.where(tp == 0, b, a)

    in_own, in_other = own_pair(prompt_input, continuation_input)
    up_own, up_other = own_pair(prompt_cotangent, continuation_cotangent)
    stacked = jnp.concatenate([in_own, in_other], axis=0).astype(F32)
    normed_pair, inverse_pair = normalize(stacked)
    (
        output_bias,
        first_gain,
        first_shift,
        second_gain,
        second_shift,
        down_bias,
        query_bias,
        value_bias,
        up_bias,
        up_weight,
        continuation_lengths,
        inverse_pair,
    ) = stage(
        output_bias,
        first_gain,
        first_shift,
        second_gain,
        second_shift,
        down_bias,
        query_bias,
        value_bias,
        up_bias,
        up_weight,
        continuation_lengths,
        inverse_pair,
    )
    packed = jnp.concatenate(
        [
            output_bias,
            first_gain,
            first_shift,
            second_gain,
            second_shift,
            down_bias,
            rws(query_bias, heads).reshape(-1),
            rws(value_bias, heads).reshape(-1),
            rws(up_bias, unit_rows).reshape(-1),
        ]
    )
    feed_shard = weight_shard(ctx, [up_weight], [down_weight], units, "feed_shard")
    small, feed_shard = stage(gather_small(packed, fsdp_size), feed_shard)
    w_feed = lax.all_gather(feed_shard, "fsdp", axis=0, tiled=True)
    small = small.astype(F32)
    vectors = [small[:, i * d_local : (i + 1) * d_local].reshape(-1) for i in range(6)]
    obias, gain_one, shift_one, gain_two, shift_two, dbias = vectors
    hd_local = HD // fsdp_size

    def head_vector(start, count):
        piece = small[:, start : start + count * hd_local].reshape(fsdp_size, count, hd_local)
        return piece.transpose(1, 0, 2).reshape(-1)

    start = 6 * d_local
    qbias = head_vector(start, heads)
    vbias = head_vector(start + heads * hd_local, heads)
    ubias = head_vector(start + 2 * heads * hd_local, unit_rows)
    qkv_bias = jnp.concatenate([qbias, jnp.zeros_like(qbias), vbias])

    lens = continuation_lengths[0]
    lens_high = swap_high(lens)
    info = jnp.concatenate(
        [me[None].astype(jnp.int32), prompt_lengths, lens, swap_low(lens), lens_high, swap_low(lens_high)]
    )

    natural = list(range(blocks))
    up_along = swap_high(up_own)
    act_pair = (normed_pair * gain_one + shift_one).astype(BF)
    act_pair, up_along = stage(act_pair, up_along)
    up_pair = jnp.concatenate([up_own, up_other], axis=0)
    act_high, act_low, up_corner, up_low, up_far = stage(
        swap_high(act_pair), swap_low(act_pair), swap_tp(up_along), swap_low(up_pair), swap_low(up_along)
    )
    act_pieces = [act_pair, act_low, act_high, swap_low(act_high)]
    act_starts = [0, 2 * rows, 4 * rows, 6 * rows]
    up_pieces = [up_pair, up_low, up_along, up_corner, up_far, swap_low(up_corner)]
    up_starts = [0, 2 * rows, 4 * rows, 5 * rows, 6 * rows, 7 * rows]
    act_pieces, up_pieces = stage(act_pieces, up_pieces)
    normed_one = normed_pair[:rows]
    inverse_one = inverse_pair[:rows]
    x_own = stacked[:rows]

    qkv = project(
        act_pieces, act_starts, rows, attn_full, qkv_bias[None], 0, 3 * head_width, "heads"
    ).reshape(blocks, rows, 3 * head_width)
    attended = attention_forward(info, qkv, cont_len).reshape(total_rows, head_width)
    parts = partial_blocks(attended, rows, attn_full, 3, None, "attention_sent")
    parts = swap_low(parts)
    sums = partial_blocks(attended, rows, attn_full, 3, parts, "attention_kept")
    first = stage(*scatter_first(sums))
    second = scatter_second(sums, first)
    middle = x_own + (scatter_sum(sums, first, second) + obias)
    normed_two, inverse_two = normalize(middle)
    act_two_own = (normed_two * gain_two + shift_two).astype(BF)

    def gather_blocks(own, beside=(), between=None):
        half = rows // 2
        across, along, low, *beside = stage(swap_tp(own), swap_high(own), swap_low(own), *beside)
        if between is not None:
            beside = between(*beside)
        corner_a, corner_b, across_low, along_low, *beside = stage(
            swap_high(across[:half]),
            swap_tp(along[half:]),
            swap_low(across),
            swap_low(along),
            *beside,
        )
        pieces = stage(
            own,
            low,
            across,
            along,
            across_low,
            along_low,
            corner_a,
            corner_b,
            swap_low(corner_a),
            swap_low(corner_b),
        )
        return list(pieces), beside

    act_two, _ = gather_blocks(act_two_own)
    starts = []
    for p in GATHERED[:6]:
        starts.append(p * rows)
    for p in GATHERED[6:]:
        starts += [p * rows, p * rows + rows // 2]

    def to_outputs(own, other):
        first = jnp.where(tp == 0, own, other)
        second = jnp.where(tp == 0, other, own)
        return first[None], second.reshape(1, cont_dev, cont_len, width)

    hidden, grad_pre, ubias_sum = feed_both(
        act_two, starts, up_pieces, up_starts, 2 * rows, w_feed, ubias[None], units, "feed_both"
    )
    parts = partial_blocks(grad_pre, rows, w_feed, 0, None, "act_two_sent")
    parts, hidden = stage(parts, hidden)
    (down_term,) = grad_matmul(up_pieces, natural, [hidden], natural, rows, "down_weight_term")
    parts, grad_pre, down_term = stage(swap_low(parts), grad_pre, down_term)
    down_piece = lax.psum_scatter(down_term, "fsdp", scatter_dimension=0, tiled=True)
    sums = partial_blocks(grad_pre, rows, w_feed, 0, parts, "act_two_kept")
    sums, grad_pre = stage(sums, grad_pre)
    (up_term,) = grad_matmul(act_two, GATHERED, [grad_pre], natural, rows, "up_weight_term")
    first, up_term, hidden = stage(scatter_first(sums), up_term, hidden)
    mlp_parts = partial_blocks(hidden, rows, w_feed, 1, None, "feed_sent")
    second, mlp_parts, up_term, hidden = stage(
        scatter_second(sums, first), mlp_parts, up_term, hidden
    )
    up_piece = lax.psum_scatter(up_term, "fsdp", scatter_dimension=0, tiled=True)
    grad_act_two = scatter_sum(sums, first, second)
    grad_middle = up_own.astype(F32) + norm_backward(
        grad_act_two, normed_two, inverse_two, gain_two
    )
    middle_low_own = grad_middle.astype(BF)

    def feed_sums(mlp_parts, hidden, down_piece):
        return partial_blocks(hidden, rows, w_feed, 1, mlp_parts, "feed_kept"), down_piece

    middle_low, (mlp_sums, down_piece) = gather_blocks(
        middle_low_own, (swap_low(mlp_parts), hidden, down_piece), feed_sums
    )

    def colsum(value):
        return jnp.sum(value, axis=0, dtype=F32)

    middle_low, mlp_sums = stage(middle_low, mlp_sums)
    out_term, grad_attended = middle_terms(
        middle_low, starts, attended, attn_full, 3, "middle_terms"
    )
    mlp_first, grad_attended, out_term = stage(
        scatter_first(mlp_sums), grad_attended, out_term
    )
    out_piece = lax.psum_scatter(out_term, "fsdp", scatter_dimension=0, tiled=True)
    dqkv = attention_backward(
        info, qkv, grad_attended.reshape(blocks, rows, head_width), cont_len
    ).reshape(total_rows, 3 * head_width)
    mlp_second, dqkv, up_piece = stage(scatter_second(mlp_sums, mlp_first), dqkv, up_piece)
    parts = partial_blocks(dqkv, rows, attn_full, 0, None, "act_one_sent")
    result = (middle + (scatter_sum(mlp_sums, mlp_first, mlp_second) + dbias)).astype(BF)
    parts, result, dqkv, down_high = stage(parts, result, dqkv, swap_high(down_piece))
    (qkv_term,) = grad_matmul(
        act_pieces, natural, [dqkv], natural, rows, "attention_weight_term"
    )
    qkv_piece = lax.psum_scatter(qkv_term, "fsdp", scatter_dimension=0, tiled=True)
    dqkv, parts, result_other, up_high, out_piece = stage(
        dqkv, swap_low(parts), swap_tp(result), swap_high(up_piece), out_piece
    )
    sums = partial_blocks(dqkv, rows, attn_full, 0, parts, "act_one_kept")
    sums, up_far, down_low, down_far, up_low, out_high = stage(
        sums,
        swap_low(up_high),
        swap_low(down_piece),
        swap_low(down_high),
        swap_low(up_piece),
        swap_high(out_piece),
    )
    (down_grad,) = assemble(
        ctx, [down_piece, down_low, down_high, down_far], True, 1, "down_weight_grad"
    )
    first, down_grad, out_low = stage(scatter_first(sums), down_grad, swap_low(out_piece))
    (up_grad,) = assemble(ctx, [up_piece, up_low, up_high, up_far], False, 1, "up_weight_grad")
    second, up_grad, out_far = stage(scatter_second(sums, first), up_grad, swap_low(out_high))
    grad_act_one = scatter_sum(sums, first, second)
    grad_stacked = (
        grad_middle + norm_backward(grad_act_one, normed_one, inverse_one, gain_one)
    ).astype(BF)
    vectors = jnp.stack(
        [
            colsum(middle_low_own),
            colsum(grad_act_one * normed_one),
            colsum(grad_act_one),
            colsum(grad_act_two * normed_two),
            colsum(grad_act_two),
            colsum(up_own),
        ]
    )
    colsum_qkv = colsum(dqkv)
    head_terms = jnp.concatenate(
        [
            colsum_qkv[:head_width].reshape(heads, HD),
            colsum_qkv[2 * head_width :].reshape(heads, HD),
            ubias_sum.reshape(unit_rows, HD),
        ]
    )
    place = lax.broadcasted_iota(jnp.int32, (blocks, 1, 1), 0)
    places = jnp.where(place == me, head_terms[None], 0.0)

    def by_owner(values):
        flat = values.reshape(-1, fsdp_size, values.shape[-1] // fsdp_size)
        return flat.transpose(1, 0, 2).reshape(fsdp_size, -1)

    small = jnp.concatenate([by_owner(vectors), by_owner(places)], axis=1)
    grad_stacked, small, qkv_piece = stage(grad_stacked, small, qkv_piece)
    small = small + swap_low(small)
    small = small + swap_tp(small)
    (output_grad,) = assemble(
        ctx, [out_piece, out_low, out_high, out_far], True, 1, "output_weight_grad"
    )
    stacked_other, small, qkv_high, qkv_low, output_grad, outputs = stage(
        swap_tp(grad_stacked),
        small,
        swap_high(qkv_piece),
        swap_low(qkv_piece),
        output_grad,
        to_outputs(result, result_other),
    )
    small, qkv_far = stage(small + swap_high(small), swap_low(qkv_high))
    summed = lax.dynamic_slice_in_dim(small, z, 1, axis=0)
    for step in range(1, fsdp_size):
        share = lax.dynamic_slice_in_dim(small, (z + step) % fsdp_size, 1, axis=0)
        pairs = [(i, (i + step) % fsdp_size) for i in range(fsdp_size)]
        summed = summed + lax.ppermute(share, "fsdp", pairs)
    summed = summed[0]
    obias_grad, gain_one_grad, shift_one_grad, gain_two_grad, shift_two_grad, dbias_grad = [
        summed[i * d_local : (i + 1) * d_local] for i in range(6)
    ]
    head_sums = summed[6 * d_local :].reshape(ctx_size, tp_size, 2 * heads + unit_rows, hd_local)
    head_sums = lax.dynamic_index_in_dim(head_sums, tp, axis=1, keepdims=False)
    qbias_grad = head_sums[:, :heads].reshape(heads_tp, hd_local)
    vbias_grad = head_sums[:, heads : 2 * heads].reshape(heads_tp, hd_local)
    ubias_grad = head_sums[:, 2 * heads :].reshape(ctx_size * unit_rows, hd_local)

    prompt_output, continuation_output = outputs
    prompt_input_grad, continuation_input_grad = to_outputs(grad_stacked, stacked_other)
    query_grad, key_grad, value_grad = assemble(
        ctx, [qkv_piece, qkv_low, qkv_high, qkv_far], False, 3, "attention_weight_grads"
    )
    return (
        prompt_output,
        continuation_output,
        prompt_input_grad,
        continuation_input_grad,
        query_grad,
        key_grad,
        value_grad,
        qbias_grad,
        vbias_grad,
        output_grad,
        obias_grad,
        gain_one_grad,
        shift_one_grad,
        gain_two_grad,
        shift_two_grad,
        up_grad,
        ubias_grad,
        down_grad,
        dbias_grad,
    )


def solution(mesh):
    return jax.shard_map(
        body,
        mesh=mesh,
        in_specs=(
            P("fsdp", "ctx", None),
            P("fsdp", "ctx", None, None),
            P("fsdp"),
            P("fsdp", "ctx"),
            P("fsdp", "tp"),
            P("fsdp", "tp"),
            P("fsdp", "tp"),
            P("tp", "fsdp"),
            P("tp", "fsdp"),
            P("tp", "fsdp"),
            P("fsdp"),
            P("fsdp"),
            P("fsdp"),
            P("fsdp"),
            P("fsdp"),
            P("fsdp", "tp"),
            P("tp", "fsdp"),
            P("tp", "fsdp"),
            P("fsdp"),
            P("fsdp", "ctx", None),
            P("fsdp", "ctx", None, None),
        ),
        out_specs=(
            P("fsdp", "ctx", None),
            P("fsdp", "ctx", None, None),
            P("fsdp", "ctx", None),
            P("fsdp", "ctx", None, None),
            P("fsdp", "tp"),
            P("fsdp", "tp"),
            P("fsdp", "tp"),
            P("tp", "fsdp"),
            P("tp", "fsdp"),
            P("tp", "fsdp"),
            P("fsdp"),
            P("fsdp"),
            P("fsdp"),
            P("fsdp"),
            P("fsdp"),
            P("fsdp", "tp"),
            P("tp", "fsdp"),
            P("tp", "fsdp"),
            P("fsdp"),
        ),
        check_vma=False,
    )
```

```python
from functools import partial
import math

import jax
import jax.numpy as jnp
from jax import lax
from jax.experimental import pallas as pl
from jax.experimental.pallas import tpu as pltpu
from jax.sharding import PartitionSpec as P

HD = 128
BF = jnp.bfloat16
F32 = jnp.float32
VMEM_BYTES = 62 << 20


norm_epsilon = 1e-05


def normalize(values):
    centre = jnp.mean(values, axis=-1, keepdims=True)
    centered = values - centre
    inverse = lax.rsqrt(jnp.mean(centered * centered, axis=-1, keepdims=True) + norm_epsilon)
    return (centered * inverse, inverse)


def norm_backward(incoming, normed, inverse, gain_vec):
    scaled = incoming * gain_vec
    return inverse * (
        scaled
        - jnp.mean(scaled, axis=-1, keepdims=True)
        - normed * jnp.mean(scaled * normed, axis=-1, keepdims=True)
    )


def swap_tp(value):
    return lax.ppermute(value, "tp", [(0, 1), (1, 0)])


def swap_low(value):
    return lax.ppermute(value, "ctx", [(0, 1), (1, 0), (2, 3), (3, 2)])


def swap_high(value):
    return lax.ppermute(value, "ctx", [(0, 2), (2, 0), (1, 3), (3, 1)])


def stage(*values):
    return lax.optimization_barrier(values)


def swap_any(value, distance):
    return lax.ppermute(value, ("ctx", "tp"), [(i, i ^ distance) for i in range(8)])


GATHERED = (0, 2, 1, 4, 3, 6, 5, 7)


def scatter_first(sums):
    return [swap_tp(sums[2]), swap_high(sums[3])]


def scatter_second(sums, first):
    half = sums[1].shape[0]
    by_tp, by_high = first
    across = sums[1].astype(F32) + by_high[:half].astype(F32)
    along = sums[4].astype(F32) + by_tp[half:].astype(F32)
    return [swap_tp(across.astype(BF)), swap_high(along.astype(BF))]


def scatter_sum(sums, first, second):
    half = sums[1].shape[0]
    by_tp = jnp.concatenate([second[0], first[0][:half]], axis=0)
    by_high = jnp.concatenate([first[1][half:], second[1]], axis=0)
    return sums[0] + by_tp.astype(F32) + by_high.astype(F32)


def pair_mask(rows, limits, split):
    row = lax.broadcasted_iota(jnp.int32, (rows, rows), 0)
    col = lax.broadcasted_iota(jnp.int32, (rows, rows), 1)
    mask = col <= row
    for seq in range(rows // split):
        inside = (row >= seq * split) & (row < (seq + 1) * split)
        limit = jnp.where(inside, limits[seq] + seq * split, 0)
        lower = jnp.where(inside, seq * split, 0)
        ok = (col >= lower) & (col < limit)
        mask = mask & (jnp.logical_not(inside) | ok)
    return mask


def attention_tiles(info_ref, tiles, rows, cont_len):
    me = info_ref[0]
    prompt_len = info_ref[1]
    per_block = rows // cont_len
    col = lax.broadcasted_iota(jnp.int32, (rows, rows), 1)
    row = lax.broadcasted_iota(jnp.int32, (rows, rows), 0)
    plan = []
    for t in range(tiles):
        keys = []
        for j in range(t + 1):
            mask = None
            if j == tiles - 1:
                mask = (col + j * rows) < prompt_len
            if j == t:
                mask = (col <= row) if mask is None else mask & (col <= row)
            keys.append((2 * j, mask))
        plan.append((2 * t, keys))
    for t in range(tiles):
        keys = []
        for j in range(tiles):
            keys.append((2 * j, (col + j * rows) < prompt_len if j == tiles - 1 else None))
        base = 2 + ((2 * t) ^ (me & (2 * tiles - 2))) // 2 * per_block
        limits = [info_ref[base + s] for s in range(per_block)]
        keys.append((2 * t + 1, pair_mask(rows, limits, cont_len)))
        plan.append((2 * t + 1, keys))
    return me, plan


def dot_nt(a, b):
    return lax.dot_general(a, b, (((1,), (1,)), ((), ())), preferred_element_type=F32)


def dot_nn(a, b):
    return lax.dot_general(a, b, (((1,), (0,)), ((), ())), preferred_element_type=F32)


def dot_tn(a, b):
    return lax.dot_general(a, b, (((0,), (0,)), ((), ())), preferred_element_type=F32)


def softmax_tiles(query, keys, scale):
    scores = []
    for key, mask in keys:
        score = dot_nt(query, key) * scale
        scores.append(score if mask is None else jnp.where(mask, score, -1e30))
    top = jnp.max(scores[0], axis=-1, keepdims=True)
    for s in scores[1:]:
        top = jnp.maximum(top, jnp.max(s, axis=-1, keepdims=True))
    weights = [jnp.exp(s - top) for s in scores]
    total = jnp.sum(weights[0], axis=-1, keepdims=True)
    for w in weights[1:]:
        total = total + jnp.sum(w, axis=-1, keepdims=True)
    inverse = 1.0 / total
    return [w * inverse for w in weights]


def attention_forward_kernel(tiles, rows, cont_len, heads, info_ref, qkv_ref, out_ref):
    h = pl.program_id(0)
    scale = 1.0 / math.sqrt(HD)
    me, plan = attention_tiles(info_ref, tiles, rows, cont_len)

    def load(kind, block):
        cols = pl.ds(pl.multiple_of((kind * heads + h) * HD, HD), HD)
        return qkv_ref[block ^ me, :, cols]

    for block, keys in plan:
        query = load(0, block)
        probs = softmax_tiles(query, [(load(1, kb), mask) for kb, mask in keys], scale)
        total = None
        for p, (kb, _) in zip(probs, keys):
            term = dot_nn(p.astype(BF), load(2, kb))
            total = term if total is None else total + term
        cols = pl.ds(pl.multiple_of(h * HD, HD), HD)
        out_ref[block ^ me, :, cols] = total.astype(BF)


def attention_backward_kernel(
    tiles, rows, cont_len, heads, info_ref, qkv_ref, grad_ref, out_ref, dkey_ref, dvalue_ref
):
    h = pl.program_id(0)
    scale = 1.0 / math.sqrt(HD)
    me, plan = attention_tiles(info_ref, tiles, rows, cont_len)

    def columns(kind):
        return pl.ds(pl.multiple_of((kind * heads + h) * HD, HD), HD)

    def load(kind, block):
        return qkv_ref[block ^ me, :, columns(kind)]

    seen = set()
    for block, keys in plan:
        query = load(0, block)
        grad = grad_ref[block ^ me, :, columns(0)]
        probs = softmax_tiles(query, [(load(1, kb), mask) for kb, mask in keys], scale)
        gprobs = [dot_nt(grad, load(2, kb)) for kb, _ in keys]
        delta = jnp.sum(probs[0] * gprobs[0], axis=-1, keepdims=True)
        for p, g in zip(probs[1:], gprobs[1:]):
            delta = delta + jnp.sum(p * g, axis=-1, keepdims=True)
        dquery = None
        for p, g, (kb, _) in zip(probs, gprobs, keys):
            dscore = (p * (g - delta)).astype(BF)
            term = dot_nn(dscore, load(1, kb))
            dquery = term if dquery is None else dquery + term
            dkey = dot_tn(dscore, query)
            dvalue = dot_tn(p.astype(BF), grad)
            if kb in seen:
                dkey_ref[kb] += dkey
                dvalue_ref[kb] += dvalue
            else:
                dkey_ref[kb] = dkey
                dvalue_ref[kb] = dvalue
                seen.add(kb)
        out_ref[block ^ me, :, columns(0)] = (dquery * scale).astype(BF)
    for kb in sorted(seen):
        out_ref[kb ^ me, :, columns(1)] = (dkey_ref[kb] * scale).astype(BF)
        out_ref[kb ^ me, :, columns(2)] = dvalue_ref[kb].astype(BF)


def attention_cost(blocks, rows, heads, matmuls):
    tiles = blocks // 2
    pairs = (tiles * (tiles + 1)) // 2 + tiles * (tiles + 1)
    return pl.CostEstimate(
        flops=2 * matmuls * pairs * heads * rows * rows * HD,
        transcendentals=pairs * heads * rows * rows,
        bytes_accessed=2 * blocks * rows * heads * HD * (4 if matmuls == 2 else 7),
    )


def attention_forward(info, qkv, cont_len):
    blocks, rows, width = qkv.shape
    heads = width // (3 * HD)
    return pl.pallas_call(
        partial(attention_forward_kernel, blocks // 2, rows, cont_len, heads),
        grid=(heads,),
        in_specs=[
            pl.BlockSpec(memory_space=pltpu.SMEM),
            pl.BlockSpec((blocks, rows, width), lambda h: (0, 0, 0)),
        ],
        out_specs=pl.BlockSpec((blocks, rows, heads * HD), lambda h: (0, 0, 0)),
        out_shape=jax.ShapeDtypeStruct((blocks, rows, heads * HD), BF),
        compiler_params=pltpu.CompilerParams(vmem_limit_bytes=32 << 20),
        cost_estimate=attention_cost(blocks, rows, heads, 2),
        name="attention_forward",
    )(info, qkv)


def attention_backward(info, qkv, grad, cont_len):
    blocks, rows, width = qkv.shape
    heads = width // (3 * HD)
    return pl.pallas_call(
        partial(attention_backward_kernel, blocks // 2, rows, cont_len, heads),
        grid=(heads,),
        in_specs=[
            pl.BlockSpec(memory_space=pltpu.SMEM),
            pl.BlockSpec((blocks, rows, width), lambda h: (0, 0, 0)),
            pl.BlockSpec((blocks, rows, heads * HD), lambda h: (0, 0, 0)),
        ],
        out_specs=pl.BlockSpec((blocks, rows, width), lambda h: (0, 0, 0)),
        out_shape=jax.ShapeDtypeStruct((blocks, rows, width), BF),
        scratch_shapes=[
            pltpu.VMEM((blocks, rows, HD), F32),
            pltpu.VMEM((blocks, rows, HD), F32),
        ],
        compiler_params=pltpu.CompilerParams(vmem_limit_bytes=32 << 20),
        cost_estimate=attention_cost(blocks, rows, heads, 7),
        name="attention_backward",
    )(info, qkv, grad)


def block_copies(pieces, rows, total):
    seen, plan = set(), []
    for start in range(0, total, rows):
        need = [
            i
            for i, (begin, size) in enumerate(pieces)
            if begin < start + rows and start < begin + size and i not in seen
        ]
        seen.update(need)
        plan.append(need)
    return plan


def piece_copy(refs, pieces, buffer, sems, i):
    begin, size = pieces[i]
    return pltpu.make_async_copy(refs[i], buffer.at[pl.ds(begin, size), :], sems.at[i])


def grad_matmul_kernel(pieces, rows, tile, *refs):
    lefts = refs[: len(pieces)]
    right_hbm, out_ref, buffer, right_ref, sems, right_sems = refs[len(pieces) :]
    step = pl.program_id(0)
    plan = block_copies(pieces, rows, right_ref.shape[0])
    columns = pl.ds(pl.multiple_of(step * tile, tile), tile)

    def right_copy(p):
        block = pl.ds(p * rows, rows)
        return pltpu.make_async_copy(right_hbm.at[block], right_ref.at[block], right_sems.at[p])

    @pl.when(step == 0)
    def _():
        for p, need in enumerate(plan):
            right_copy(p).start()
            for i in need:
                piece_copy(lefts, pieces, buffer, sems, i).start()
        total = None
        for p, need in enumerate(plan):
            right_copy(p).wait()
            for i in need:
                piece_copy(lefts, pieces, buffer, sems, i).wait()
            block = pl.ds(p * rows, rows)
            term = dot_tn(buffer[block, columns], right_ref[block, :])
            total = term if total is None else total + term
        out_ref[...] = total.astype(BF)

    @pl.when(step > 0)
    def _():
        out_ref[...] = dot_tn(buffer[:, columns], right_ref[...]).astype(BF)


def grad_matmul(lefts, starts, right, rows, name):
    d = lefts[0].shape[1]
    total_rows, n = right.shape
    tile = 512
    pieces = [(start, p.shape[0]) for start, p in zip(starts, lefts)]
    return pl.pallas_call(
        partial(grad_matmul_kernel, pieces, rows, tile),
        grid=(d // tile,),
        in_specs=[pl.BlockSpec(memory_space=pl.ANY) for _ in range(len(lefts) + 1)],
        out_specs=pl.BlockSpec((tile, n), lambda i: (i, 0)),
        out_shape=jax.ShapeDtypeStruct((d, n), BF),
        scratch_shapes=[
            pltpu.VMEM((total_rows, d), BF),
            pltpu.VMEM((total_rows, n), BF),
            pltpu.SemaphoreType.DMA((len(lefts),)),
            pltpu.SemaphoreType.DMA((total_rows // rows,)),
        ],
        compiler_params=pltpu.CompilerParams(vmem_limit_bytes=VMEM_BYTES),
        cost_estimate=pl.CostEstimate(
            flops=2 * total_rows * d * n,
            transcendentals=0,
            bytes_accessed=2 * (total_rows * (d + n) + d * n),
        ),
        name=name,
    )(*lefts, right)


def sent_kernel(rows, low_ref, high_ref, w_ref, out_ref):
    for i, left in enumerate((low_ref, high_ref)):
        out_ref[pl.ds(2 * i * rows, 2 * rows), :] = dot_nt(left[...], w_ref[...]).astype(BF)


def kept_kernel(rows, low_ref, high_ref, w_ref, arrived_ref, own_ref, *outs):
    across_ref, to_tp_ref, to_high_ref, along_ref = outs
    half = rows // 2
    low = dot_nt(low_ref[...], w_ref[...])
    low = low + arrived_ref[pl.ds(0, 2 * rows), :].astype(F32)
    own_ref[...] = low[:rows]
    across_ref[...] = low[rows : rows + half].astype(BF)
    to_tp_ref[pl.ds(0, half), :] = low[rows + half :].astype(BF)
    high = dot_nt(high_ref[...], w_ref[...])
    high = (high + arrived_ref[pl.ds(2 * rows, 2 * rows), :].astype(F32)).astype(BF)
    to_tp_ref[pl.ds(half, half), :] = high[rows + half :]
    to_high_ref[pl.ds(0, half), :] = high[rows : rows + half]
    to_high_ref[pl.ds(half, half), :] = high[:half]
    along_ref[...] = high[half:rows]


def partial_blocks(left, rows, weights, column, arrived, name):
    k = left.shape[1]
    d = weights.shape[0]
    tile = 512
    pair = 2 * rows
    if arrived is None:
        first, kernel, more = 1, sent_kernel, []
        outs = [(4 * rows, BF)]
    else:
        first, kernel, more = 0, kept_kernel, [arrived]
        outs = [(rows, F32), (rows // 2, BF), (rows, BF), (rows, BF), (rows // 2, BF)]
    result = pl.pallas_call(
        partial(kernel, rows),
        grid=(d // tile,),
        in_specs=[
            pl.BlockSpec((pair, k), lambda i: (first, 0), pipeline_mode=pl.Buffered(1)),
            pl.BlockSpec((pair, k), lambda i: (first + 2, 0), pipeline_mode=pl.Buffered(1)),
            pl.BlockSpec((tile, k), lambda i: (i, column)),
        ]
        + [pl.BlockSpec((2 * pair, tile), lambda i: (0, i)) for _ in more],
        out_specs=[pl.BlockSpec((n, tile), lambda i: (0, i)) for n, _ in outs],
        out_shape=[jax.ShapeDtypeStruct((n, d), t) for n, t in outs],
        compiler_params=pltpu.CompilerParams(vmem_limit_bytes=VMEM_BYTES),
        cost_estimate=pl.CostEstimate(
            flops=8 * rows * d * k,
            transcendentals=0,
            bytes_accessed=2 * (4 * rows * (k + d) + d * k),
        ),
        name=name,
    )(left, left, weights, *more)
    return result[0] if arrived is None else result


def project_kernel(pieces, rows, *refs):
    lefts, (w_ref, bias_ref, out_ref, buffer, sems) = refs[: len(pieces)], refs[len(pieces) :]
    total = out_ref.shape[0]
    plan = block_copies(pieces, rows, total)

    def compute(p):
        block = pl.ds(p * rows, rows)
        out_ref[block, :] = (dot_nn(buffer[block, :], w_ref[...]) + bias_ref[...]).astype(BF)

    @pl.when(pl.program_id(0) == 0)
    def _():
        for need in plan:
            for i in need:
                piece_copy(lefts, pieces, buffer, sems, i).start()
        for p, need in enumerate(plan):
            for i in need:
                piece_copy(lefts, pieces, buffer, sems, i).wait()
            compute(p)

    @pl.when(pl.program_id(0) > 0)
    def _():
        for p in range(len(plan)):
            compute(p)


def project(lefts, starts, rows, weights, bias, column, n, name):
    total = sum(p.shape[0] for p in lefts)
    width = lefts[0].shape[1]
    pieces = [(start, p.shape[0]) for start, p in zip(starts, lefts)]
    tile = 256
    skip = column // tile
    return pl.pallas_call(
        partial(project_kernel, pieces, rows),
        grid=(n // tile,),
        in_specs=[pl.BlockSpec(memory_space=pl.ANY) for _ in lefts]
        + [
            pl.BlockSpec((width, tile), lambda i: (0, skip + i)),
            pl.BlockSpec((1, tile), lambda i: (0, i)),
        ],
        out_specs=pl.BlockSpec((total, tile), lambda i: (0, i)),
        out_shape=jax.ShapeDtypeStruct((total, n), BF),
        scratch_shapes=[
            pltpu.VMEM((total, width), BF),
            pltpu.SemaphoreType.DMA((len(lefts),)),
        ],
        compiler_params=pltpu.CompilerParams(vmem_limit_bytes=VMEM_BYTES),
        cost_estimate=pl.CostEstimate(
            flops=2 * total * width * n,
            transcendentals=0,
            bytes_accessed=2 * (total * (width + n) + width * n),
        ),
        name=name,
    )(*lefts, weights, bias)


def middle_kernel(pieces, tile, *refs):
    lefts = refs[: len(pieces)]
    att_ref, w_ref, term_ref, grad_ref, buffer, total_ref, sems = refs[len(pieces) :]
    step = pl.program_id(0)

    @pl.when(step == 0)
    def _():
        for i in range(len(pieces)):
            piece_copy(lefts, pieces, buffer, sems, i).start()
        for i in range(len(pieces)):
            piece_copy(lefts, pieces, buffer, sems, i).wait()

    left = buffer[:, pl.ds(pl.multiple_of(step * tile, tile), tile)]
    term_ref[...] = dot_tn(left, att_ref[...]).astype(BF)
    grad = dot_nn(left, w_ref[...])

    @pl.when(step == 0)
    def _():
        total_ref[...] = grad

    @pl.when(step > 0)
    def _():
        total_ref[...] += grad

    @pl.when(step == pl.num_programs(0) - 1)
    def _():
        grad_ref[...] = total_ref[...].astype(BF)


def middle_terms(lefts, starts, attended, weights, column, name):
    total, n = attended.shape
    d = lefts[0].shape[1]
    tile = 512
    pieces = [(start, p.shape[0]) for start, p in zip(starts, lefts)]
    return pl.pallas_call(
        partial(middle_kernel, pieces, tile),
        grid=(d // tile,),
        in_specs=[pl.BlockSpec(memory_space=pl.ANY) for _ in lefts]
        + [
            pl.BlockSpec((total, n), lambda i: (0, 0), pipeline_mode=pl.Buffered(1)),
            pl.BlockSpec((tile, n), lambda i: (i, column)),
        ],
        out_specs=[
            pl.BlockSpec((tile, n), lambda i: (i, 0)),
            pl.BlockSpec((total, n), lambda i: (0, 0)),
        ],
        out_shape=[
            jax.ShapeDtypeStruct((d, n), BF),
            jax.ShapeDtypeStruct((total, n), BF),
        ],
        scratch_shapes=[
            pltpu.VMEM((total, d), BF),
            pltpu.VMEM((total, n), F32),
            pltpu.SemaphoreType.DMA((len(lefts),)),
        ],
        compiler_params=pltpu.CompilerParams(vmem_limit_bytes=VMEM_BYTES),
        cost_estimate=pl.CostEstimate(
            flops=4 * total * d * n,
            transcendentals=0,
            bytes_accessed=2 * total * (d + 2 * n) + 4 * d * n,
        ),
        name=name,
    )(*lefts, attended, weights)


def shard_kernel(n_cols, ctx_ref, *refs):
    ins, out = refs[:-1], refs[-1]
    start = 0
    for i, ref in enumerate(ins):
        value = ref[...] if i < n_cols else ref[...].T
        out[:, start : start + value.shape[1]] = value
        start += value.shape[1]


def weight_shard(ctx, by_column, by_row, size, name):
    d = by_column[0].shape[0]
    count = len(by_column) + len(by_row)
    return pl.pallas_call(
        partial(shard_kernel, len(by_column)),
        grid_spec=pltpu.PrefetchScalarGridSpec(
            num_scalar_prefetch=1,
            grid=(1,),
            in_specs=[pl.BlockSpec((d, size), lambda i, c: (0, c[0])) for _ in by_column]
            + [pl.BlockSpec((size, d), lambda i, c: (c[0], 0)) for _ in by_row],
            out_specs=pl.BlockSpec((d, count * size), lambda i, c: (0, 0)),
        ),
        out_shape=jax.ShapeDtypeStruct((d, count * size), BF),
        compiler_params=pltpu.CompilerParams(vmem_limit_bytes=VMEM_BYTES),
        cost_estimate=pl.CostEstimate(
            flops=0, transcendentals=0, bytes_accessed=4 * d * count * size
        ),
        name=name,
    )(ctx[None].astype(jnp.int32), *by_column, *by_row)


def assemble_kernel(turn, count, width, ctx_ref, *refs):
    pieces, outs = refs[:count], refs[count:]
    step = pl.program_id(0)
    for k in range(count):

        @pl.when(step == k)
        def _():
            for i, out in enumerate(outs):
                part = pieces[k][:, i * width : (i + 1) * width].astype(F32)
                out[...] = part.T if turn else part


def assemble(ctx, pieces, turn, outputs, name):
    count = len(pieces)
    rows, cols = pieces[0].shape
    width = cols // outputs
    if turn:
        block, shape = (width, rows), (width * count, rows)
        index = lambda k, ctx_ref: (k ^ ctx_ref[0], 0)
    else:
        block, shape = (rows, width), (rows, width * count)
        index = lambda k, ctx_ref: (0, k ^ ctx_ref[0])
    return pl.pallas_call(
        partial(assemble_kernel, turn, count, width),
        grid_spec=pltpu.PrefetchScalarGridSpec(
            num_scalar_prefetch=1,
            grid=(count,),
            in_specs=[
                pl.BlockSpec((rows, cols), lambda k, ctx_ref: (0, 0), pipeline_mode=pl.Buffered(1))
                for _ in pieces
            ],
            out_specs=[pl.BlockSpec(block, index) for _ in range(outputs)],
        ),
        out_shape=[jax.ShapeDtypeStruct(shape, F32) for _ in range(outputs)],
        compiler_params=pltpu.CompilerParams(vmem_limit_bytes=VMEM_BYTES),
        cost_estimate=pl.CostEstimate(
            flops=0, transcendentals=0, bytes_accessed=6 * count * rows * cols
        ),
        name=name,
    )(ctx[None].astype(jnp.int32), *pieces)


def gelu_and_slope(u):
    half = 0.5 * (1.0 + lax.erf(u * math.sqrt(0.5)))
    density = jnp.exp(-0.5 * u * u) * (1.0 / math.sqrt(2.0 * math.pi))
    return u * half, half + u * density


def feed_kernel(act_pieces, up_pieces, rows, *refs):
    count = len(act_pieces)
    acts, ups = refs[:count], refs[count : count + len(up_pieces)]
    (
        w_up_ref,
        w_down_ref,
        bias_ref,
        hidden_ref,
        grad_ref,
        sum_ref,
        act_buffer,
        up_buffer,
        act_sems,
        up_sems,
    ) = refs[count + len(up_pieces) :]
    total = hidden_ref.shape[0]
    act_plan = block_copies(act_pieces, rows, total)
    up_plan = block_copies(up_pieces, rows, total)

    def compute(p):
        block = pl.ds(p * rows, rows)
        pre_act = dot_nn(act_buffer[block, :], w_up_ref[...]) + bias_ref[...]
        grad_hidden = dot_nn(up_buffer[block, :], w_down_ref[...])
        hidden, slope = gelu_and_slope(pre_act)
        hidden_ref[block, :] = hidden.astype(BF)
        grad = (grad_hidden * slope).astype(BF)
        grad_ref[block, :] = grad
        part = jnp.sum(grad.astype(F32), axis=0, keepdims=True)
        if p == 0:
            sum_ref[...] = part
        else:
            sum_ref[...] += part

    def act_copy(i):
        return piece_copy(acts, act_pieces, act_buffer, act_sems, i)

    def up_copy(i):
        return piece_copy(ups, up_pieces, up_buffer, up_sems, i)

    @pl.when(pl.program_id(0) == 0)
    def _():
        for act_need, up_need in zip(act_plan, up_plan):
            for i in act_need:
                act_copy(i).start()
            for i in up_need:
                up_copy(i).start()
        for p, (act_need, up_need) in enumerate(zip(act_plan, up_plan)):
            for i in act_need:
                act_copy(i).wait()
            for i in up_need:
                up_copy(i).wait()
            compute(p)

    @pl.when(pl.program_id(0) > 0)
    def _():
        for p in range(len(act_plan)):
            compute(p)


def feed_both(acts, act_starts, ups, up_starts, rows, weights, bias, units, name):
    total = sum(p.shape[0] for p in acts)
    width = acts[0].shape[1]
    tile = 256
    skip = units // tile
    act_pieces = [(start, p.shape[0]) for start, p in zip(act_starts, acts)]
    up_pieces = [(start, p.shape[0]) for start, p in zip(up_starts, ups)]
    return pl.pallas_call(
        partial(feed_kernel, act_pieces, up_pieces, rows),
        grid=(units // tile,),
        in_specs=[pl.BlockSpec(memory_space=pl.ANY) for _ in acts + ups]
        + [
            pl.BlockSpec((width, tile), lambda i: (0, i)),
            pl.BlockSpec((width, tile), lambda i: (0, skip + i)),
            pl.BlockSpec((1, tile), lambda i: (0, i)),
        ],
        out_specs=[
            pl.BlockSpec((total, tile), lambda i: (0, i)),
            pl.BlockSpec((total, tile), lambda i: (0, i)),
            pl.BlockSpec((1, tile), lambda i: (0, i)),
        ],
        out_shape=[
            jax.ShapeDtypeStruct((total, units), BF),
            jax.ShapeDtypeStruct((total, units), BF),
            jax.ShapeDtypeStruct((1, units), F32),
        ],
        scratch_shapes=[
            pltpu.VMEM((total, width), BF),
            pltpu.VMEM((total, width), BF),
            pltpu.SemaphoreType.DMA((len(acts),)),
            pltpu.SemaphoreType.DMA((len(ups),)),
        ],
        compiler_params=pltpu.CompilerParams(vmem_limit_bytes=VMEM_BYTES),
        cost_estimate=pl.CostEstimate(
            flops=4 * total * width * units,
            transcendentals=0,
            bytes_accessed=4 * (total * width + width * units + total * units),
        ),
        name=name,
    )(*acts, *ups, weights, weights, bias)


def gather_small(packed, size):
    index = lax.axis_index("fsdp")
    out = lax.dynamic_update_slice(
        jnp.zeros((size,) + packed.shape, packed.dtype), packed[None], (index, 0)
    )
    for step in range(1, size):
        moved = lax.ppermute(packed, "fsdp", [(i, (i + step) % size) for i in range(size)])
        out = lax.dynamic_update_slice(out, moved[None], ((index + size - step) % size, 0))
    return out


def body(
    prompt_input,
    continuation_input,
    prompt_lengths,
    continuation_lengths,
    query_weight,
    key_weight,
    value_weight,
    query_bias,
    value_bias,
    output_weight,
    output_bias,
    first_gain,
    first_shift,
    second_gain,
    second_shift,
    up_weight,
    up_bias,
    down_weight,
    down_bias,
    prompt_cotangent,
    continuation_cotangent,
):
    prompt_dev = prompt_input.shape[1]
    cont_dev = continuation_input.shape[1]
    cont_len = continuation_input.shape[2]
    width = prompt_input.shape[2]
    rows = prompt_dev
    fsdp_size = lax.axis_size("fsdp")
    ctx_size = lax.axis_size("ctx")
    tp_size = lax.axis_size("tp")
    assert ctx_size == 4 and tp_size == 2 and cont_dev * cont_len == rows
    blocks = ctx_size * tp_size
    total_rows = blocks * rows
    z = lax.axis_index("fsdp")
    ctx = lax.axis_index("ctx")
    tp = lax.axis_index("tp")
    me = 2 * ctx + tp

    heads_tp = query_bias.shape[0]
    heads = heads_tp // ctx_size
    head_width = heads * HD
    units = up_weight.shape[1] // ctx_size
    unit_rows = units // HD
    d_local = query_weight.shape[0]

    def rws(weight, count):
        return lax.dynamic_slice_in_dim(weight, ctx * count, count, axis=0)

    attn_shard = weight_shard(
        ctx, [query_weight, key_weight, value_weight], [output_weight], head_width, "attention_shard"
    )
    (
        attn_shard,
        prompt_input,
        continuation_input,
        prompt_cotangent,
        continuation_cotangent,
        continuation_lengths,
    ) = stage(
        attn_shard,
        prompt_input,
        continuation_input,
        prompt_cotangent,
        continuation_cotangent,
        continuation_lengths,
    )
    attn_full = lax.all_gather(attn_shard, "fsdp", axis=0, tiled=True)
    w_qkv = attn_full[:, : 3 * head_width]
    def own_pair(first, second):
        a = first[0]
        b = second[0].reshape(rows, width)
        return jnp.where(tp == 0, a, b), jnp.where(tp == 0, b, a)

    in_own, in_other = own_pair(prompt_input, continuation_input)
    up_own, up_other = own_pair(prompt_cotangent, continuation_cotangent)
    stacked = jnp.concatenate([in_own, in_other], axis=0).astype(F32)
    normed_pair, inverse_pair = normalize(stacked)
    (
        output_bias,
        first_gain,
        first_shift,
        second_gain,
        second_shift,
        down_bias,
        query_bias,
        value_bias,
        up_bias,
        up_weight,
        continuation_lengths,
        inverse_pair,
    ) = stage(
        output_bias,
        first_gain,
        first_shift,
        second_gain,
        second_shift,
        down_bias,
        query_bias,
        value_bias,
        up_bias,
        up_weight,
        continuation_lengths,
        inverse_pair,
    )
    packed = jnp.concatenate(
        [
            output_bias,
            first_gain,
            first_shift,
            second_gain,
            second_shift,
            down_bias,
            rws(query_bias, heads).reshape(-1),
            rws(value_bias, heads).reshape(-1),
            rws(up_bias, unit_rows).reshape(-1),
        ]
    )
    feed_shard = weight_shard(ctx, [up_weight], [down_weight], units, "feed_shard")
    small, feed_shard = stage(gather_small(packed, fsdp_size), feed_shard)
    w_feed = lax.all_gather(feed_shard, "fsdp", axis=0, tiled=True)
    small = small.astype(F32)
    vectors = [small[:, i * d_local : (i + 1) * d_local].reshape(-1) for i in range(6)]
    obias, gain_one, shift_one, gain_two, shift_two, dbias = vectors
    hd_local = HD // fsdp_size

    def head_vector(start, count):
        piece = small[:, start : start + count * hd_local].reshape(fsdp_size, count, hd_local)
        return piece.transpose(1, 0, 2).reshape(-1)

    start = 6 * d_local
    qbias = head_vector(start, heads)
    vbias = head_vector(start + heads * hd_local, heads)
    ubias = head_vector(start + 2 * heads * hd_local, unit_rows)
    qkv_bias = jnp.concatenate([qbias, jnp.zeros_like(qbias), vbias])

    lens = continuation_lengths[0]
    lens_high = swap_high(lens)
    info = jnp.concatenate(
        [me[None].astype(jnp.int32), prompt_lengths, lens, swap_low(lens), lens_high, swap_low(lens_high)]
    )

    up_along = swap_high(up_own)
    act_pair = (normed_pair * gain_one + shift_one).astype(BF)
    act_pair, up_along = stage(act_pair, up_along)
    up_pair = jnp.concatenate([up_own, up_other], axis=0)
    act_high, act_low, up_corner, up_low, up_far = stage(
        swap_high(act_pair), swap_low(act_pair), swap_tp(up_along), swap_low(up_pair), swap_low(up_along)
    )
    act_pieces = [act_pair, act_low, act_high, swap_low(act_high)]
    act_starts = [0, 2 * rows, 4 * rows, 6 * rows]
    up_pieces = [up_pair, up_low, up_along, up_corner, up_far, swap_low(up_corner)]
    up_starts = [0, 2 * rows, 4 * rows, 5 * rows, 6 * rows, 7 * rows]
    act_pieces, up_pieces = stage(act_pieces, up_pieces)
    normed_one = normed_pair[:rows]
    inverse_one = inverse_pair[:rows]
    x_own = stacked[:rows]

    qkv = project(
        act_pieces, act_starts, rows, attn_full, qkv_bias[None], 0, 3 * head_width, "heads"
    ).reshape(blocks, rows, 3 * head_width)
    attended = attention_forward(info, qkv, cont_len).reshape(total_rows, head_width)
    parts = partial_blocks(attended, rows, attn_full, 3, None, "attention_sent")
    parts = swap_low(parts)
    sums = partial_blocks(attended, rows, attn_full, 3, parts, "attention_kept")
    first = stage(*scatter_first(sums))
    second = scatter_second(sums, first)
    middle = x_own + (scatter_sum(sums, first, second) + obias)
    normed_two, inverse_two = normalize(middle)
    act_two_own = (normed_two * gain_two + shift_two).astype(BF)

    def gather_blocks(own, beside=()):
        half = rows // 2
        across, along, low, *beside = stage(swap_tp(own), swap_high(own), swap_low(own), *beside)
        corner_a, corner_b, across_low, along_low = stage(
            swap_high(across[:half]), swap_tp(along[half:]), swap_low(across), swap_low(along)
        )
        pieces = stage(
            own,
            low,
            across,
            along,
            across_low,
            along_low,
            corner_a,
            corner_b,
            swap_low(corner_a),
            swap_low(corner_b),
        )
        return list(pieces), beside

    act_two, _ = gather_blocks(act_two_own)
    starts = []
    for p in GATHERED[:6]:
        starts.append(p * rows)
    for p in GATHERED[6:]:
        starts += [p * rows, p * rows + rows // 2]

    def to_outputs(own, other):
        first = jnp.where(tp == 0, own, other)
        second = jnp.where(tp == 0, other, own)
        return first[None], second.reshape(1, cont_dev, cont_len, width)

    hidden, grad_pre, ubias_sum = feed_both(
        act_two, starts, up_pieces, up_starts, 2 * rows, w_feed, ubias[None], units, "feed_both"
    )
    parts = partial_blocks(grad_pre, rows, w_feed, 0, None, "act_two_sent")
    parts, hidden = stage(parts, hidden)
    down_term = grad_matmul(up_pieces, up_starts, hidden, 2 * rows, "down_weight_term")
    parts, grad_pre, down_term = stage(swap_low(parts), grad_pre, down_term)
    down_piece = lax.psum_scatter(down_term, "fsdp", scatter_dimension=0, tiled=True)
    sums = partial_blocks(grad_pre, rows, w_feed, 0, parts, "act_two_kept")
    sums, grad_pre, hidden = stage(sums, grad_pre, hidden)
    mlp_parts = partial_blocks(hidden, rows, w_feed, 1, None, "feed_sent")
    first, mlp_parts, hidden, grad_pre = stage(scatter_first(sums), mlp_parts, hidden, grad_pre)
    second, mlp_parts, hidden, grad_pre = stage(
        scatter_second(sums, first), swap_low(mlp_parts), hidden, grad_pre
    )
    grad_act_two = scatter_sum(sums, first, second)
    grad_middle = up_own.astype(F32) + norm_backward(
        grad_act_two, normed_two, inverse_two, gain_two
    )
    middle_low_own = grad_middle.astype(BF)

    middle_low_own, mlp_parts, hidden, grad_pre = stage(
        middle_low_own, mlp_parts, hidden, grad_pre
    )
    up_term = grad_matmul(act_two, starts, grad_pre, 2 * rows, "up_weight_term")
    mlp_sums = partial_blocks(hidden, rows, w_feed, 1, mlp_parts, "feed_kept")
    middle_low, (mlp_sums, up_term, down_piece) = gather_blocks(
        middle_low_own, (mlp_sums, up_term, down_piece)
    )
    up_piece = lax.psum_scatter(up_term, "fsdp", scatter_dimension=0, tiled=True)

    def colsum(value):
        return jnp.sum(value, axis=0, dtype=F32)

    middle_low, mlp_sums = stage(middle_low, mlp_sums)
    out_term, grad_attended = middle_terms(
        middle_low, starts, attended, attn_full, 3, "middle_terms"
    )
    mlp_first, grad_attended, out_term = stage(
        scatter_first(mlp_sums), grad_attended, out_term
    )
    out_piece = lax.psum_scatter(out_term, "fsdp", scatter_dimension=0, tiled=True)
    dqkv = attention_backward(
        info, qkv, grad_attended.reshape(blocks, rows, head_width), cont_len
    ).reshape(total_rows, 3 * head_width)
    mlp_second, dqkv, up_piece = stage(scatter_second(mlp_sums, mlp_first), dqkv, up_piece)
    parts = partial_blocks(dqkv, rows, attn_full, 0, None, "act_one_sent")
    result = (middle + (scatter_sum(mlp_sums, mlp_first, mlp_second) + dbias)).astype(BF)
    parts, result, dqkv, down_high = stage(parts, result, dqkv, swap_high(down_piece))
    qkv_term = grad_matmul(act_pieces, act_starts, dqkv, 2 * rows, "attention_weight_term")
    qkv_piece = lax.psum_scatter(qkv_term, "fsdp", scatter_dimension=0, tiled=True)
    dqkv, parts, result_other, up_high, out_piece = stage(
        dqkv, swap_low(parts), swap_tp(result), swap_high(up_piece), out_piece
    )
    sums = partial_blocks(dqkv, rows, attn_full, 0, parts, "act_one_kept")
    sums, up_far, down_low, down_far, up_low, out_high = stage(
        sums,
        swap_low(up_high),
        swap_low(down_piece),
        swap_low(down_high),
        swap_low(up_piece),
        swap_high(out_piece),
    )
    out_low = swap_low(out_piece)
    (down_grad,) = assemble(
        ctx, [down_piece, down_low, down_high, down_far], True, 1, "down_weight_grad"
    )
    (output_grad,) = assemble(
        ctx, [out_piece, out_low, out_high, swap_low(out_high)], True, 1, "output_weight_grad"
    )
    first, down_grad, output_grad, outputs = stage(
        scatter_first(sums), down_grad, output_grad, to_outputs(result, result_other)
    )
    (up_grad,) = assemble(ctx, [up_piece, up_low, up_high, up_far], False, 1, "up_weight_grad")
    second, up_grad = stage(scatter_second(sums, first), up_grad)
    grad_act_one = scatter_sum(sums, first, second)
    grad_stacked = (
        grad_middle + norm_backward(grad_act_one, normed_one, inverse_one, gain_one)
    ).astype(BF)
    vectors = jnp.stack(
        [
            colsum(middle_low_own),
            colsum(grad_act_one * normed_one),
            colsum(grad_act_one),
            colsum(grad_act_two * normed_two),
            colsum(grad_act_two),
            colsum(up_own),
        ]
    )
    colsum_qkv = colsum(dqkv)
    head_terms = jnp.concatenate(
        [
            colsum_qkv[:head_width].reshape(heads, HD),
            colsum_qkv[2 * head_width :].reshape(heads, HD),
            ubias_sum.reshape(unit_rows, HD),
        ]
    )
    place = lax.broadcasted_iota(jnp.int32, (blocks, 1, 1), 0)
    places = jnp.where(place == me, head_terms[None], 0.0)

    def by_owner(values):
        flat = values.reshape(-1, fsdp_size, values.shape[-1] // fsdp_size)
        return flat.transpose(1, 0, 2).reshape(fsdp_size, -1)

    small = jnp.concatenate([by_owner(vectors), by_owner(places)], axis=1)
    grad_stacked, small, qkv_piece = stage(grad_stacked, small, qkv_piece)
    for swap in (swap_low, swap_high, swap_tp):
        small = small + swap(small)
    stacked_other, small, qkv_high, qkv_low = stage(
        swap_tp(grad_stacked), small, swap_high(qkv_piece), swap_low(qkv_piece)
    )
    qkv_far = swap_low(qkv_high)
    summed = lax.dynamic_slice_in_dim(small, z, 1, axis=0)
    for step in range(1, fsdp_size):
        share = lax.dynamic_slice_in_dim(small, (z + step) % fsdp_size, 1, axis=0)
        pairs = [(i, (i + step) % fsdp_size) for i in range(fsdp_size)]
        summed = summed + lax.ppermute(share, "fsdp", pairs)
    summed = summed[0]
    obias_grad, gain_one_grad, shift_one_grad, gain_two_grad, shift_two_grad, dbias_grad = [
        summed[i * d_local : (i + 1) * d_local] for i in range(6)
    ]
    head_sums = summed[6 * d_local :].reshape(ctx_size, tp_size, 2 * heads + unit_rows, hd_local)
    head_sums = lax.dynamic_index_in_dim(head_sums, tp, axis=1, keepdims=False)
    qbias_grad = head_sums[:, :heads].reshape(heads_tp, hd_local)
    vbias_grad = head_sums[:, heads : 2 * heads].reshape(heads_tp, hd_local)
    ubias_grad = head_sums[:, 2 * heads :].reshape(ctx_size * unit_rows, hd_local)

    prompt_output, continuation_output = outputs
    prompt_input_grad, continuation_input_grad = to_outputs(grad_stacked, stacked_other)
    query_grad, key_grad, value_grad = assemble(
        ctx, [qkv_piece, qkv_low, qkv_high, qkv_far], False, 3, "attention_weight_grads"
    )
    return (
        prompt_output,
        continuation_output,
        prompt_input_grad,
        continuation_input_grad,
        query_grad,
        key_grad,
        value_grad,
        qbias_grad,
        vbias_grad,
        output_grad,
        obias_grad,
        gain_one_grad,
        shift_one_grad,
        gain_two_grad,
        shift_two_grad,
        up_grad,
        ubias_grad,
        down_grad,
        dbias_grad,
    )


def solution(mesh):
    return jax.shard_map(
        body,
        mesh=mesh,
        in_specs=(
            P("fsdp", "ctx", None),
            P("fsdp", "ctx", None, None),
            P("fsdp"),
            P("fsdp", "ctx"),
            P("fsdp", "tp"),
            P("fsdp", "tp"),
            P("fsdp", "tp"),
            P("tp", "fsdp"),
            P("tp", "fsdp"),
            P("tp", "fsdp"),
            P("fsdp"),
            P("fsdp"),
            P("fsdp"),
            P("fsdp"),
            P("fsdp"),
            P("fsdp", "tp"),
            P("tp", "fsdp"),
            P("tp", "fsdp"),
            P("fsdp"),
            P("fsdp", "ctx", None),
            P("fsdp", "ctx", None, None),
        ),
        out_specs=(
            P("fsdp", "ctx", None),
            P("fsdp", "ctx", None, None),
            P("fsdp", "ctx", None),
            P("fsdp", "ctx", None, None),
            P("fsdp", "tp"),
            P("fsdp", "tp"),
            P("fsdp", "tp"),
            P("tp", "fsdp"),
            P("tp", "fsdp"),
            P("tp", "fsdp"),
            P("fsdp"),
            P("fsdp"),
            P("fsdp"),
            P("fsdp"),
            P("fsdp"),
            P("fsdp", "tp"),
            P("tp", "fsdp"),
            P("tp", "fsdp"),
            P("fsdp"),
        ),
        check_vma=False,
    )
```

```python
from functools import partial
import math

import jax
import jax.numpy as jnp
from jax import lax
from jax.experimental import pallas as pl
from jax.experimental.pallas import tpu as pltpu
from jax.sharding import PartitionSpec as P

HD = 128
BF = jnp.bfloat16
F32 = jnp.float32
VMEM_BYTES = 62 << 20


norm_epsilon = 1e-05


def normalize(values):
    centre = jnp.mean(values, axis=-1, keepdims=True)
    centered = values - centre
    inverse = lax.rsqrt(jnp.mean(centered * centered, axis=-1, keepdims=True) + norm_epsilon)
    return (centered * inverse, inverse)


def norm_backward(incoming, normed, inverse, gain_vec):
    scaled = incoming * gain_vec
    return inverse * (
        scaled
        - jnp.mean(scaled, axis=-1, keepdims=True)
        - normed * jnp.mean(scaled * normed, axis=-1, keepdims=True)
    )


def swap_tp(value):
    return lax.ppermute(value, "tp", [(0, 1), (1, 0)])


def swap_low(value):
    return lax.ppermute(value, "ctx", [(0, 1), (1, 0), (2, 3), (3, 2)])


def swap_high(value):
    return lax.ppermute(value, "ctx", [(0, 2), (2, 0), (1, 3), (3, 1)])


def stage(*values):
    return lax.optimization_barrier(values)


def swap_any(value, distance):
    return lax.ppermute(value, ("ctx", "tp"), [(i, i ^ distance) for i in range(8)])


GATHERED = (0, 2, 1, 4, 3, 6, 5, 7)


def scatter_first(sums):
    return [swap_tp(sums[2]), swap_high(sums[3])]


def scatter_second(sums, first):
    half = sums[1].shape[0]
    by_tp, by_high = first
    across = sums[1].astype(F32) + by_high[:half].astype(F32)
    along = sums[4].astype(F32) + by_tp[half:].astype(F32)
    return [swap_tp(across.astype(BF)), swap_high(along.astype(BF))]


def scatter_sum(sums, first, second):
    half = sums[1].shape[0]
    by_tp = jnp.concatenate([second[0], first[0][:half]], axis=0)
    by_high = jnp.concatenate([first[1][half:], second[1]], axis=0)
    return sums[0] + by_tp.astype(F32) + by_high.astype(F32)


def pair_mask(rows, limits, split):
    row = lax.broadcasted_iota(jnp.int32, (rows, rows), 0)
    col = lax.broadcasted_iota(jnp.int32, (rows, rows), 1)
    mask = col <= row
    for seq in range(rows // split):
        inside = (row >= seq * split) & (row < (seq + 1) * split)
        limit = jnp.where(inside, limits[seq] + seq * split, 0)
        lower = jnp.where(inside, seq * split, 0)
        ok = (col >= lower) & (col < limit)
        mask = mask & (jnp.logical_not(inside) | ok)
    return mask


def attention_tiles(info_ref, tiles, rows, cont_len):
    me = info_ref[0]
    prompt_len = info_ref[1]
    per_block = rows // cont_len
    col = lax.broadcasted_iota(jnp.int32, (rows, rows), 1)
    row = lax.broadcasted_iota(jnp.int32, (rows, rows), 0)
    plan = []
    for t in range(tiles):
        keys = []
        for j in range(t + 1):
            mask = None
            if j == tiles - 1:
                mask = (col + j * rows) < prompt_len
            if j == t:
                mask = (col <= row) if mask is None else mask & (col <= row)
            keys.append((2 * j, mask))
        plan.append((2 * t, keys))
    for t in range(tiles):
        keys = []
        for j in range(tiles):
            keys.append((2 * j, (col + j * rows) < prompt_len if j == tiles - 1 else None))
        base = 2 + ((2 * t) ^ (me & (2 * tiles - 2))) // 2 * per_block
        limits = [info_ref[base + s] for s in range(per_block)]
        keys.append((2 * t + 1, pair_mask(rows, limits, cont_len)))
        plan.append((2 * t + 1, keys))
    return me, plan


def dot_nt(a, b):
    return lax.dot_general(a, b, (((1,), (1,)), ((), ())), preferred_element_type=F32)


def dot_nn(a, b):
    return lax.dot_general(a, b, (((1,), (0,)), ((), ())), preferred_element_type=F32)


def dot_tn(a, b):
    return lax.dot_general(a, b, (((0,), (0,)), ((), ())), preferred_element_type=F32)


def softmax_tiles(query, keys, scale):
    scores = []
    for key, mask in keys:
        score = dot_nt(query, key) * scale
        scores.append(score if mask is None else jnp.where(mask, score, -1e30))
    top = jnp.max(scores[0], axis=-1, keepdims=True)
    for s in scores[1:]:
        top = jnp.maximum(top, jnp.max(s, axis=-1, keepdims=True))
    weights = [jnp.exp(s - top) for s in scores]
    total = jnp.sum(weights[0], axis=-1, keepdims=True)
    for w in weights[1:]:
        total = total + jnp.sum(w, axis=-1, keepdims=True)
    inverse = 1.0 / total
    return [w * inverse for w in weights]


def attention_forward_kernel(tiles, rows, cont_len, heads, info_ref, qkv_ref, out_ref):
    h = pl.program_id(0)
    scale = 1.0 / math.sqrt(HD)
    me, plan = attention_tiles(info_ref, tiles, rows, cont_len)

    def load(kind, block):
        cols = pl.ds(pl.multiple_of((kind * heads + h) * HD, HD), HD)
        return qkv_ref[block ^ me, :, cols]

    for block, keys in plan:
        query = load(0, block)
        probs = softmax_tiles(query, [(load(1, kb), mask) for kb, mask in keys], scale)
        total = None
        for p, (kb, _) in zip(probs, keys):
            term = dot_nn(p.astype(BF), load(2, kb))
            total = term if total is None else total + term
        cols = pl.ds(pl.multiple_of(h * HD, HD), HD)
        out_ref[block ^ me, :, cols] = total.astype(BF)


def attention_backward_kernel(
    tiles, rows, cont_len, heads, info_ref, qkv_ref, grad_ref, out_ref, dkey_ref, dvalue_ref
):
    h = pl.program_id(0)
    scale = 1.0 / math.sqrt(HD)
    me, plan = attention_tiles(info_ref, tiles, rows, cont_len)

    def columns(kind):
        return pl.ds(pl.multiple_of((kind * heads + h) * HD, HD), HD)

    def load(kind, block):
        return qkv_ref[block ^ me, :, columns(kind)]

    seen = set()
    for block, keys in plan:
        query = load(0, block)
        grad = grad_ref[block ^ me, :, columns(0)]
        probs = softmax_tiles(query, [(load(1, kb), mask) for kb, mask in keys], scale)
        gprobs = [dot_nt(grad, load(2, kb)) for kb, _ in keys]
        delta = jnp.sum(probs[0] * gprobs[0], axis=-1, keepdims=True)
        for p, g in zip(probs[1:], gprobs[1:]):
            delta = delta + jnp.sum(p * g, axis=-1, keepdims=True)
        dquery = None
        for p, g, (kb, _) in zip(probs, gprobs, keys):
            dscore = (p * (g - delta)).astype(BF)
            term = dot_nn(dscore, load(1, kb))
            dquery = term if dquery is None else dquery + term
            dkey = dot_tn(dscore, query)
            dvalue = dot_tn(p.astype(BF), grad)
            if kb in seen:
                dkey_ref[kb] += dkey
                dvalue_ref[kb] += dvalue
            else:
                dkey_ref[kb] = dkey
                dvalue_ref[kb] = dvalue
                seen.add(kb)
        out_ref[block ^ me, :, columns(0)] = (dquery * scale).astype(BF)
    for kb in sorted(seen):
        out_ref[kb ^ me, :, columns(1)] = (dkey_ref[kb] * scale).astype(BF)
        out_ref[kb ^ me, :, columns(2)] = dvalue_ref[kb].astype(BF)


def attention_cost(blocks, rows, heads, matmuls):
    tiles = blocks // 2
    pairs = (tiles * (tiles + 1)) // 2 + tiles * (tiles + 1)
    return pl.CostEstimate(
        flops=2 * matmuls * pairs * heads * rows * rows * HD,
        transcendentals=pairs * heads * rows * rows,
        bytes_accessed=2 * blocks * rows * heads * HD * (4 if matmuls == 2 else 7),
    )


def attention_forward(info, qkv, cont_len):
    blocks, rows, width = qkv.shape
    heads = width // (3 * HD)
    return pl.pallas_call(
        partial(attention_forward_kernel, blocks // 2, rows, cont_len, heads),
        grid=(heads,),
        in_specs=[
            pl.BlockSpec(memory_space=pltpu.SMEM),
            pl.BlockSpec((blocks, rows, width), lambda h: (0, 0, 0)),
        ],
        out_specs=pl.BlockSpec((blocks, rows, heads * HD), lambda h: (0, 0, 0)),
        out_shape=jax.ShapeDtypeStruct((blocks, rows, heads * HD), BF),
        compiler_params=pltpu.CompilerParams(vmem_limit_bytes=32 << 20),
        cost_estimate=attention_cost(blocks, rows, heads, 2),
        name="attention_forward",
    )(info, qkv)


def attention_backward(info, qkv, grad, cont_len):
    blocks, rows, width = qkv.shape
    heads = width // (3 * HD)
    return pl.pallas_call(
        partial(attention_backward_kernel, blocks // 2, rows, cont_len, heads),
        grid=(heads,),
        in_specs=[
            pl.BlockSpec(memory_space=pltpu.SMEM),
            pl.BlockSpec((blocks, rows, width), lambda h: (0, 0, 0)),
            pl.BlockSpec((blocks, rows, heads * HD), lambda h: (0, 0, 0)),
        ],
        out_specs=pl.BlockSpec((blocks, rows, width), lambda h: (0, 0, 0)),
        out_shape=jax.ShapeDtypeStruct((blocks, rows, width), BF),
        scratch_shapes=[
            pltpu.VMEM((blocks, rows, HD), F32),
            pltpu.VMEM((blocks, rows, HD), F32),
        ],
        compiler_params=pltpu.CompilerParams(vmem_limit_bytes=32 << 20),
        cost_estimate=attention_cost(blocks, rows, heads, 7),
        name="attention_backward",
    )(info, qkv, grad)


def block_copies(pieces, rows, total):
    seen, plan = set(), []
    for start in range(0, total, rows):
        need = [
            i
            for i, (begin, size) in enumerate(pieces)
            if begin < start + rows and start < begin + size and i not in seen
        ]
        seen.update(need)
        plan.append(need)
    return plan


def piece_copy(refs, pieces, buffer, sems, i):
    begin, size = pieces[i]
    return pltpu.make_async_copy(refs[i], buffer.at[pl.ds(begin, size), :], sems.at[i])


def grad_matmul_kernel(pieces, rows, tile, *refs):
    lefts = refs[: len(pieces)]
    right_hbm, out_ref, buffer, right_ref, sems, right_sems = refs[len(pieces) :]
    step = pl.program_id(0)
    plan = block_copies(pieces, rows, right_ref.shape[0])
    columns = pl.ds(pl.multiple_of(step * tile, tile), tile)

    def right_copy(p):
        block = pl.ds(p * rows, rows)
        return pltpu.make_async_copy(right_hbm.at[block], right_ref.at[block], right_sems.at[p])

    @pl.when(step == 0)
    def _():
        for p, need in enumerate(plan):
            right_copy(p).start()
            for i in need:
                piece_copy(lefts, pieces, buffer, sems, i).start()
        total = None
        for p, need in enumerate(plan):
            right_copy(p).wait()
            for i in need:
                piece_copy(lefts, pieces, buffer, sems, i).wait()
            block = pl.ds(p * rows, rows)
            term = dot_tn(buffer[block, columns], right_ref[block, :])
            total = term if total is None else total + term
        out_ref[...] = total.astype(BF)

    @pl.when(step > 0)
    def _():
        out_ref[...] = dot_tn(buffer[:, columns], right_ref[...]).astype(BF)


def grad_matmul(lefts, starts, right, rows, name):
    d = lefts[0].shape[1]
    total_rows, n = right.shape
    tile = 512
    pieces = [(start, p.shape[0]) for start, p in zip(starts, lefts)]
    return pl.pallas_call(
        partial(grad_matmul_kernel, pieces, rows, tile),
        grid=(d // tile,),
        in_specs=[pl.BlockSpec(memory_space=pl.ANY) for _ in range(len(lefts) + 1)],
        out_specs=pl.BlockSpec((tile, n), lambda i: (i, 0)),
        out_shape=jax.ShapeDtypeStruct((d, n), BF),
        scratch_shapes=[
            pltpu.VMEM((total_rows, d), BF),
            pltpu.VMEM((total_rows, n), BF),
            pltpu.SemaphoreType.DMA((len(lefts),)),
            pltpu.SemaphoreType.DMA((total_rows // rows,)),
        ],
        compiler_params=pltpu.CompilerParams(vmem_limit_bytes=VMEM_BYTES),
        cost_estimate=pl.CostEstimate(
            flops=2 * total_rows * d * n,
            transcendentals=0,
            bytes_accessed=2 * (total_rows * (d + n) + d * n),
        ),
        name=name,
    )(*lefts, right)


def sent_kernel(rows, low_ref, high_ref, w_ref, out_ref):
    for i, left in enumerate((low_ref, high_ref)):
        out_ref[pl.ds(2 * i * rows, 2 * rows), :] = dot_nt(left[...], w_ref[...]).astype(BF)


def kept_kernel(rows, low_ref, high_ref, w_ref, arrived_ref, own_ref, *outs):
    across_ref, to_tp_ref, to_high_ref, along_ref = outs
    half = rows // 2
    low = dot_nt(low_ref[...], w_ref[...])
    low = low + arrived_ref[pl.ds(0, 2 * rows), :].astype(F32)
    own_ref[...] = low[:rows]
    across_ref[...] = low[rows : rows + half].astype(BF)
    to_tp_ref[pl.ds(0, half), :] = low[rows + half :].astype(BF)
    high = dot_nt(high_ref[...], w_ref[...])
    high = (high + arrived_ref[pl.ds(2 * rows, 2 * rows), :].astype(F32)).astype(BF)
    to_tp_ref[pl.ds(half, half), :] = high[rows + half :]
    to_high_ref[pl.ds(0, half), :] = high[rows : rows + half]
    to_high_ref[pl.ds(half, half), :] = high[:half]
    along_ref[...] = high[half:rows]


def partial_blocks(left, rows, weights, column, arrived, name):
    k = left.shape[1]
    d = weights.shape[0]
    tile = 512
    pair = 2 * rows
    if arrived is None:
        first, kernel, more = 1, sent_kernel, []
        outs = [(4 * rows, BF)]
    else:
        first, kernel, more = 0, kept_kernel, [arrived]
        outs = [(rows, F32), (rows // 2, BF), (rows, BF), (rows, BF), (rows // 2, BF)]
    result = pl.pallas_call(
        partial(kernel, rows),
        grid=(d // tile,),
        in_specs=[
            pl.BlockSpec((pair, k), lambda i: (first, 0), pipeline_mode=pl.Buffered(1)),
            pl.BlockSpec((pair, k), lambda i: (first + 2, 0), pipeline_mode=pl.Buffered(1)),
            pl.BlockSpec((tile, k), lambda i: (i, column)),
        ]
        + [pl.BlockSpec((2 * pair, tile), lambda i: (0, i)) for _ in more],
        out_specs=[pl.BlockSpec((n, tile), lambda i: (0, i)) for n, _ in outs],
        out_shape=[jax.ShapeDtypeStruct((n, d), t) for n, t in outs],
        compiler_params=pltpu.CompilerParams(vmem_limit_bytes=VMEM_BYTES),
        cost_estimate=pl.CostEstimate(
            flops=8 * rows * d * k,
            transcendentals=0,
            bytes_accessed=2 * (4 * rows * (k + d) + d * k),
        ),
        name=name,
    )(left, left, weights, *more)
    return result[0] if arrived is None else result


def project_kernel(pieces, rows, *refs):
    lefts, (w_ref, bias_ref, out_ref, buffer, sems) = refs[: len(pieces)], refs[len(pieces) :]
    total = out_ref.shape[0]
    plan = block_copies(pieces, rows, total)

    def compute(p):
        block = pl.ds(p * rows, rows)
        out_ref[block, :] = (dot_nn(buffer[block, :], w_ref[...]) + bias_ref[...]).astype(BF)

    @pl.when(pl.program_id(0) == 0)
    def _():
        for need in plan:
            for i in need:
                piece_copy(lefts, pieces, buffer, sems, i).start()
        for p, need in enumerate(plan):
            for i in need:
                piece_copy(lefts, pieces, buffer, sems, i).wait()
            compute(p)

    @pl.when(pl.program_id(0) > 0)
    def _():
        for p in range(len(plan)):
            compute(p)


def project(lefts, starts, rows, weights, bias, column, n, name):
    total = sum(p.shape[0] for p in lefts)
    width = lefts[0].shape[1]
    pieces = [(start, p.shape[0]) for start, p in zip(starts, lefts)]
    tile = 256
    skip = column // tile
    return pl.pallas_call(
        partial(project_kernel, pieces, rows),
        grid=(n // tile,),
        in_specs=[pl.BlockSpec(memory_space=pl.ANY) for _ in lefts]
        + [
            pl.BlockSpec((width, tile), lambda i: (0, skip + i)),
            pl.BlockSpec((1, tile), lambda i: (0, i)),
        ],
        out_specs=pl.BlockSpec((total, tile), lambda i: (0, i)),
        out_shape=jax.ShapeDtypeStruct((total, n), BF),
        scratch_shapes=[
            pltpu.VMEM((total, width), BF),
            pltpu.SemaphoreType.DMA((len(lefts),)),
        ],
        compiler_params=pltpu.CompilerParams(vmem_limit_bytes=VMEM_BYTES),
        cost_estimate=pl.CostEstimate(
            flops=2 * total * width * n,
            transcendentals=0,
            bytes_accessed=2 * (total * (width + n) + width * n),
        ),
        name=name,
    )(*lefts, weights, bias)


def middle_kernel(pieces, tile, *refs):
    lefts = refs[: len(pieces)]
    att_ref, w_ref, term_ref, grad_ref, buffer, total_ref, sems = refs[len(pieces) :]
    step = pl.program_id(0)

    @pl.when(step == 0)
    def _():
        for i in range(len(pieces)):
            piece_copy(lefts, pieces, buffer, sems, i).start()
        for i in range(len(pieces)):
            piece_copy(lefts, pieces, buffer, sems, i).wait()

    left = buffer[:, pl.ds(pl.multiple_of(step * tile, tile), tile)]
    term_ref[...] = dot_tn(left, att_ref[...]).astype(BF)
    grad = dot_nn(left, w_ref[...])

    @pl.when(step == 0)
    def _():
        total_ref[...] = grad

    @pl.when(step > 0)
    def _():
        total_ref[...] += grad

    @pl.when(step == pl.num_programs(0) - 1)
    def _():
        grad_ref[...] = total_ref[...].astype(BF)


def middle_terms(lefts, starts, attended, weights, column, name):
    total, n = attended.shape
    d = lefts[0].shape[1]
    tile = 512
    pieces = [(start, p.shape[0]) for start, p in zip(starts, lefts)]
    return pl.pallas_call(
        partial(middle_kernel, pieces, tile),
        grid=(d // tile,),
        in_specs=[pl.BlockSpec(memory_space=pl.ANY) for _ in lefts]
        + [
            pl.BlockSpec((total, n), lambda i: (0, 0), pipeline_mode=pl.Buffered(1)),
            pl.BlockSpec((tile, n), lambda i: (i, column)),
        ],
        out_specs=[
            pl.BlockSpec((tile, n), lambda i: (i, 0)),
            pl.BlockSpec((total, n), lambda i: (0, 0)),
        ],
        out_shape=[
            jax.ShapeDtypeStruct((d, n), BF),
            jax.ShapeDtypeStruct((total, n), BF),
        ],
        scratch_shapes=[
            pltpu.VMEM((total, d), BF),
            pltpu.VMEM((total, n), F32),
            pltpu.SemaphoreType.DMA((len(lefts),)),
        ],
        compiler_params=pltpu.CompilerParams(vmem_limit_bytes=VMEM_BYTES),
        cost_estimate=pl.CostEstimate(
            flops=4 * total * d * n,
            transcendentals=0,
            bytes_accessed=2 * total * (d + 2 * n) + 4 * d * n,
        ),
        name=name,
    )(*lefts, attended, weights)


def shard_kernel(n_cols, ctx_ref, *refs):
    ins, out = refs[:-1], refs[-1]
    start = 0
    for i, ref in enumerate(ins):
        value = ref[...] if i < n_cols else ref[...].T
        out[:, start : start + value.shape[1]] = value
        start += value.shape[1]


def weight_shard(ctx, by_column, by_row, size, name):
    d = by_column[0].shape[0]
    count = len(by_column) + len(by_row)
    return pl.pallas_call(
        partial(shard_kernel, len(by_column)),
        grid_spec=pltpu.PrefetchScalarGridSpec(
            num_scalar_prefetch=1,
            grid=(1,),
            in_specs=[pl.BlockSpec((d, size), lambda i, c: (0, c[0])) for _ in by_column]
            + [pl.BlockSpec((size, d), lambda i, c: (c[0], 0)) for _ in by_row],
            out_specs=pl.BlockSpec((d, count * size), lambda i, c: (0, 0)),
        ),
        out_shape=jax.ShapeDtypeStruct((d, count * size), BF),
        compiler_params=pltpu.CompilerParams(vmem_limit_bytes=VMEM_BYTES),
        cost_estimate=pl.CostEstimate(
            flops=0, transcendentals=0, bytes_accessed=4 * d * count * size
        ),
        name=name,
    )(ctx[None].astype(jnp.int32), *by_column, *by_row)


def assemble_kernel(turn, count, width, ctx_ref, *refs):
    pieces, outs = refs[:count], refs[count:]
    step = pl.program_id(0)
    for k in range(count):

        @pl.when(step == k)
        def _():
            for i, out in enumerate(outs):
                part = pieces[k][:, i * width : (i + 1) * width].astype(F32)
                out[...] = part.T if turn else part


def assemble(ctx, pieces, turn, outputs, name):
    count = len(pieces)
    rows, cols = pieces[0].shape
    width = cols // outputs
    if turn:
        block, shape = (width, rows), (width * count, rows)
        index = lambda k, ctx_ref: (k ^ ctx_ref[0], 0)
    else:
        block, shape = (rows, width), (rows, width * count)
        index = lambda k, ctx_ref: (0, k ^ ctx_ref[0])
    return pl.pallas_call(
        partial(assemble_kernel, turn, count, width),
        grid_spec=pltpu.PrefetchScalarGridSpec(
            num_scalar_prefetch=1,
            grid=(count,),
            in_specs=[
                pl.BlockSpec((rows, cols), lambda k, ctx_ref: (0, 0), pipeline_mode=pl.Buffered(1))
                for _ in pieces
            ],
            out_specs=[pl.BlockSpec(block, index) for _ in range(outputs)],
        ),
        out_shape=[jax.ShapeDtypeStruct(shape, F32) for _ in range(outputs)],
        compiler_params=pltpu.CompilerParams(vmem_limit_bytes=VMEM_BYTES),
        cost_estimate=pl.CostEstimate(
            flops=0, transcendentals=0, bytes_accessed=6 * count * rows * cols
        ),
        name=name,
    )(ctx[None].astype(jnp.int32), *pieces)


def gelu_and_slope(u):
    half = 0.5 * (1.0 + lax.erf(u * math.sqrt(0.5)))
    density = jnp.exp(-0.5 * u * u) * (1.0 / math.sqrt(2.0 * math.pi))
    return u * half, half + u * density


def feed_kernel(act_pieces, up_pieces, rows, *refs):
    count = len(act_pieces)
    acts, ups = refs[:count], refs[count : count + len(up_pieces)]
    (
        w_up_ref,
        w_down_ref,
        bias_ref,
        hidden_ref,
        grad_ref,
        sum_ref,
        act_buffer,
        up_buffer,
        act_sems,
        up_sems,
    ) = refs[count + len(up_pieces) :]
    total = hidden_ref.shape[0]
    act_plan = block_copies(act_pieces, rows, total)
    up_plan = block_copies(up_pieces, rows, total)

    def compute(p):
        block = pl.ds(p * rows, rows)
        pre_act = dot_nn(act_buffer[block, :], w_up_ref[...]) + bias_ref[...]
        grad_hidden = dot_nn(up_buffer[block, :], w_down_ref[...])
        hidden, slope = gelu_and_slope(pre_act)
        hidden_ref[block, :] = hidden.astype(BF)
        grad = (grad_hidden * slope).astype(BF)
        grad_ref[block, :] = grad
        part = jnp.sum(grad.astype(F32), axis=0, keepdims=True)
        if p == 0:
            sum_ref[...] = part
        else:
            sum_ref[...] += part

    def act_copy(i):
        return piece_copy(acts, act_pieces, act_buffer, act_sems, i)

    def up_copy(i):
        return piece_copy(ups, up_pieces, up_buffer, up_sems, i)

    @pl.when(pl.program_id(0) == 0)
    def _():
        for act_need, up_need in zip(act_plan, up_plan):
            for i in act_need:
                act_copy(i).start()
            for i in up_need:
                up_copy(i).start()
        for p, (act_need, up_need) in enumerate(zip(act_plan, up_plan)):
            for i in act_need:
                act_copy(i).wait()
            for i in up_need:
                up_copy(i).wait()
            compute(p)

    @pl.when(pl.program_id(0) > 0)
    def _():
        for p in range(len(act_plan)):
            compute(p)


def feed_both(acts, act_starts, ups, up_starts, rows, weights, bias, units, name):
    total = sum(p.shape[0] for p in acts)
    width = acts[0].shape[1]
    tile = 512
    skip = units // tile
    act_pieces = [(start, p.shape[0]) for start, p in zip(act_starts, acts)]
    up_pieces = [(start, p.shape[0]) for start, p in zip(up_starts, ups)]
    return pl.pallas_call(
        partial(feed_kernel, act_pieces, up_pieces, rows),
        grid=(units // tile,),
        in_specs=[pl.BlockSpec(memory_space=pl.ANY) for _ in acts + ups]
        + [
            pl.BlockSpec((width, tile), lambda i: (0, i)),
            pl.BlockSpec((width, tile), lambda i: (0, skip + i)),
            pl.BlockSpec((1, tile), lambda i: (0, i)),
        ],
        out_specs=[
            pl.BlockSpec((total, tile), lambda i: (0, i)),
            pl.BlockSpec((total, tile), lambda i: (0, i)),
            pl.BlockSpec((1, tile), lambda i: (0, i)),
        ],
        out_shape=[
            jax.ShapeDtypeStruct((total, units), BF),
            jax.ShapeDtypeStruct((total, units), BF),
            jax.ShapeDtypeStruct((1, units), F32),
        ],
        scratch_shapes=[
            pltpu.VMEM((total, width), BF),
            pltpu.VMEM((total, width), BF),
            pltpu.SemaphoreType.DMA((len(acts),)),
            pltpu.SemaphoreType.DMA((len(ups),)),
        ],
        compiler_params=pltpu.CompilerParams(vmem_limit_bytes=VMEM_BYTES),
        cost_estimate=pl.CostEstimate(
            flops=4 * total * width * units,
            transcendentals=0,
            bytes_accessed=4 * (total * width + width * units + total * units),
        ),
        name=name,
    )(*acts, *ups, weights, weights, bias)


def gather_small(packed, size):
    index = lax.axis_index("fsdp")
    out = lax.dynamic_update_slice(
        jnp.zeros((size,) + packed.shape, packed.dtype), packed[None], (index, 0)
    )
    for step in range(1, size):
        moved = lax.ppermute(packed, "fsdp", [(i, (i + step) % size) for i in range(size)])
        out = lax.dynamic_update_slice(out, moved[None], ((index + size - step) % size, 0))
    return out


def body(
    prompt_input,
    continuation_input,
    prompt_lengths,
    continuation_lengths,
    query_weight,
    key_weight,
    value_weight,
    query_bias,
    value_bias,
    output_weight,
    output_bias,
    first_gain,
    first_shift,
    second_gain,
    second_shift,
    up_weight,
    up_bias,
    down_weight,
    down_bias,
    prompt_cotangent,
    continuation_cotangent,
):
    prompt_dev = prompt_input.shape[1]
    cont_dev = continuation_input.shape[1]
    cont_len = continuation_input.shape[2]
    width = prompt_input.shape[2]
    rows = prompt_dev
    fsdp_size = lax.axis_size("fsdp")
    ctx_size = lax.axis_size("ctx")
    tp_size = lax.axis_size("tp")
    assert ctx_size == 4 and tp_size == 2 and cont_dev * cont_len == rows
    blocks = ctx_size * tp_size
    total_rows = blocks * rows
    z = lax.axis_index("fsdp")
    ctx = lax.axis_index("ctx")
    tp = lax.axis_index("tp")
    me = 2 * ctx + tp

    heads_tp = query_bias.shape[0]
    heads = heads_tp // ctx_size
    head_width = heads * HD
    units = up_weight.shape[1] // ctx_size
    unit_rows = units // HD
    d_local = query_weight.shape[0]

    def rws(weight, count):
        return lax.dynamic_slice_in_dim(weight, ctx * count, count, axis=0)

    attn_shard = weight_shard(
        ctx, [query_weight, key_weight, value_weight], [output_weight], head_width, "attention_shard"
    )
    (
        attn_shard,
        prompt_input,
        continuation_input,
        prompt_cotangent,
        continuation_cotangent,
        continuation_lengths,
    ) = stage(
        attn_shard,
        prompt_input,
        continuation_input,
        prompt_cotangent,
        continuation_cotangent,
        continuation_lengths,
    )
    attn_full = lax.all_gather(attn_shard, "fsdp", axis=0, tiled=True)
    w_qkv = attn_full[:, : 3 * head_width]
    def own_pair(first, second):
        a = first[0]
        b = second[0].reshape(rows, width)
        return jnp.where(tp == 0, a, b), jnp.where(tp == 0, b, a)

    in_own, in_other = own_pair(prompt_input, continuation_input)
    up_own, up_other = own_pair(prompt_cotangent, continuation_cotangent)
    stacked = jnp.concatenate([in_own, in_other], axis=0).astype(F32)
    normed_pair, inverse_pair = normalize(stacked)
    (
        output_bias,
        first_gain,
        first_shift,
        second_gain,
        second_shift,
        down_bias,
        query_bias,
        value_bias,
        up_bias,
        up_weight,
        continuation_lengths,
        inverse_pair,
    ) = stage(
        output_bias,
        first_gain,
        first_shift,
        second_gain,
        second_shift,
        down_bias,
        query_bias,
        value_bias,
        up_bias,
        up_weight,
        continuation_lengths,
        inverse_pair,
    )
    packed = jnp.concatenate(
        [
            output_bias,
            first_gain,
            first_shift,
            second_gain,
            second_shift,
            down_bias,
            rws(query_bias, heads).reshape(-1),
            rws(value_bias, heads).reshape(-1),
            rws(up_bias, unit_rows).reshape(-1),
        ]
    )
    feed_shard = weight_shard(ctx, [up_weight], [down_weight], units, "feed_shard")
    small, feed_shard = stage(gather_small(packed, fsdp_size), feed_shard)
    w_feed = lax.all_gather(feed_shard, "fsdp", axis=0, tiled=True)
    small = small.astype(F32)
    vectors = [small[:, i * d_local : (i + 1) * d_local].reshape(-1) for i in range(6)]
    obias, gain_one, shift_one, gain_two, shift_two, dbias = vectors
    hd_local = HD // fsdp_size

    def head_vector(start, count):
        piece = small[:, start : start + count * hd_local].reshape(fsdp_size, count, hd_local)
        return piece.transpose(1, 0, 2).reshape(-1)

    start = 6 * d_local
    qbias = head_vector(start, heads)
    vbias = head_vector(start + heads * hd_local, heads)
    ubias = head_vector(start + 2 * heads * hd_local, unit_rows)
    qkv_bias = jnp.concatenate([qbias, jnp.zeros_like(qbias), vbias])

    lens = continuation_lengths[0]
    lens_high = swap_high(lens)
    info = jnp.concatenate(
        [me[None].astype(jnp.int32), prompt_lengths, lens, swap_low(lens), lens_high, swap_low(lens_high)]
    )

    up_along = swap_high(up_own)
    act_pair = (normed_pair * gain_one + shift_one).astype(BF)
    act_pair, up_along = stage(act_pair, up_along)
    up_pair = jnp.concatenate([up_own, up_other], axis=0)
    act_high, act_low, up_corner, up_low, up_far = stage(
        swap_high(act_pair), swap_low(act_pair), swap_tp(up_along), swap_low(up_pair), swap_low(up_along)
    )
    act_pieces = [act_pair, act_low, act_high, swap_low(act_high)]
    act_starts = [0, 2 * rows, 4 * rows, 6 * rows]
    up_pieces = [up_pair, up_low, up_along, up_corner, up_far, swap_low(up_corner)]
    up_starts = [0, 2 * rows, 4 * rows, 5 * rows, 6 * rows, 7 * rows]
    act_pieces, up_pieces = stage(act_pieces, up_pieces)
    normed_one = normed_pair[:rows]
    inverse_one = inverse_pair[:rows]
    x_own = stacked[:rows]

    qkv = project(
        act_pieces, act_starts, rows, attn_full, qkv_bias[None], 0, 3 * head_width, "heads"
    ).reshape(blocks, rows, 3 * head_width)
    attended = attention_forward(info, qkv, cont_len).reshape(total_rows, head_width)
    parts = partial_blocks(attended, rows, attn_full, 3, None, "attention_sent")
    parts = swap_low(parts)
    sums = partial_blocks(attended, rows, attn_full, 3, parts, "attention_kept")
    first = stage(*scatter_first(sums))
    second = scatter_second(sums, first)
    middle = x_own + (scatter_sum(sums, first, second) + obias)
    normed_two, inverse_two = normalize(middle)
    act_two_own = (normed_two * gain_two + shift_two).astype(BF)

    def gather_blocks(own, beside=()):
        half = rows // 2
        across, along, low, *beside = stage(swap_tp(own), swap_high(own), swap_low(own), *beside)
        corner_a, corner_b, across_low, along_low = stage(
            swap_high(across[:half]), swap_tp(along[half:]), swap_low(across), swap_low(along)
        )
        pieces = stage(
            own,
            low,
            across,
            along,
            across_low,
            along_low,
            corner_a,
            corner_b,
            swap_low(corner_a),
            swap_low(corner_b),
        )
        return list(pieces), beside

    act_two, _ = gather_blocks(act_two_own)
    starts = []
    for p in GATHERED[:6]:
        starts.append(p * rows)
    for p in GATHERED[6:]:
        starts += [p * rows, p * rows + rows // 2]

    def to_outputs(own, other):
        first = jnp.where(tp == 0, own, other)
        second = jnp.where(tp == 0, other, own)
        return first[None], second.reshape(1, cont_dev, cont_len, width)

    hidden, grad_pre, ubias_sum = feed_both(
        act_two, starts, up_pieces, up_starts, 2 * rows, w_feed, ubias[None], units, "feed_both"
    )
    parts = partial_blocks(grad_pre, rows, w_feed, 0, None, "act_two_sent")
    parts, hidden = stage(parts, hidden)
    down_term = grad_matmul(up_pieces, up_starts, hidden, 2 * rows, "down_weight_term")
    parts, grad_pre, down_term = stage(swap_low(parts), grad_pre, down_term)
    down_piece = lax.psum_scatter(down_term, "fsdp", scatter_dimension=0, tiled=True)
    sums = partial_blocks(grad_pre, rows, w_feed, 0, parts, "act_two_kept")
    sums, grad_pre, hidden = stage(sums, grad_pre, hidden)
    mlp_parts = partial_blocks(hidden, rows, w_feed, 1, None, "feed_sent")
    first, mlp_parts, hidden, grad_pre = stage(scatter_first(sums), mlp_parts, hidden, grad_pre)
    second, mlp_parts, hidden, grad_pre = stage(
        scatter_second(sums, first), swap_low(mlp_parts), hidden, grad_pre
    )
    grad_act_two = scatter_sum(sums, first, second)
    grad_middle = up_own.astype(F32) + norm_backward(
        grad_act_two, normed_two, inverse_two, gain_two
    )
    middle_low_own = grad_middle.astype(BF)

    middle_low_own, mlp_parts, hidden, grad_pre = stage(
        middle_low_own, mlp_parts, hidden, grad_pre
    )
    up_term = grad_matmul(act_two, starts, grad_pre, 2 * rows, "up_weight_term")
    mlp_sums = partial_blocks(hidden, rows, w_feed, 1, mlp_parts, "feed_kept")
    middle_low, (mlp_sums, up_term, down_piece) = gather_blocks(
        middle_low_own, (mlp_sums, up_term, down_piece)
    )
    up_piece = lax.psum_scatter(up_term, "fsdp", scatter_dimension=0, tiled=True)

    def colsum(value):
        return jnp.sum(value, axis=0, dtype=F32)

    middle_low, mlp_sums = stage(middle_low, mlp_sums)
    out_term, grad_attended = middle_terms(
        middle_low, starts, attended, attn_full, 3, "middle_terms"
    )
    mlp_first, grad_attended, out_term = stage(
        scatter_first(mlp_sums), grad_attended, out_term
    )
    out_piece = lax.psum_scatter(out_term, "fsdp", scatter_dimension=0, tiled=True)
    dqkv = attention_backward(
        info, qkv, grad_attended.reshape(blocks, rows, head_width), cont_len
    ).reshape(total_rows, 3 * head_width)
    mlp_second, dqkv, up_piece = stage(scatter_second(mlp_sums, mlp_first), dqkv, up_piece)
    parts = partial_blocks(dqkv, rows, attn_full, 0, None, "act_one_sent")
    result = (middle + (scatter_sum(mlp_sums, mlp_first, mlp_second) + dbias)).astype(BF)
    parts, result, dqkv, down_high = stage(parts, result, dqkv, swap_high(down_piece))
    qkv_term = grad_matmul(act_pieces, act_starts, dqkv, 2 * rows, "attention_weight_term")
    qkv_piece = lax.psum_scatter(qkv_term, "fsdp", scatter_dimension=0, tiled=True)
    dqkv, parts, result_other, up_high, out_piece = stage(
        dqkv, swap_low(parts), swap_tp(result), swap_high(up_piece), out_piece
    )
    sums = partial_blocks(dqkv, rows, attn_full, 0, parts, "act_one_kept")
    sums, up_far, down_low, down_far, up_low, out_high = stage(
        sums,
        swap_low(up_high),
        swap_low(down_piece),
        swap_low(down_high),
        swap_low(up_piece),
        swap_high(out_piece),
    )
    out_low = swap_low(out_piece)
    (down_grad,) = assemble(
        ctx, [down_piece, down_low, down_high, down_far], True, 1, "down_weight_grad"
    )
    (output_grad,) = assemble(
        ctx, [out_piece, out_low, out_high, swap_low(out_high)], True, 1, "output_weight_grad"
    )
    first, down_grad, output_grad, outputs = stage(
        scatter_first(sums), down_grad, output_grad, to_outputs(result, result_other)
    )
    (up_grad,) = assemble(ctx, [up_piece, up_low, up_high, up_far], False, 1, "up_weight_grad")
    second, up_grad = stage(scatter_second(sums, first), up_grad)
    grad_act_one = scatter_sum(sums, first, second)
    grad_stacked = (
        grad_middle + norm_backward(grad_act_one, normed_one, inverse_one, gain_one)
    ).astype(BF)
    vectors = jnp.stack(
        [
            colsum(middle_low_own),
            colsum(grad_act_one * normed_one),
            colsum(grad_act_one),
            colsum(grad_act_two * normed_two),
            colsum(grad_act_two),
            colsum(up_own),
        ]
    )
    colsum_qkv = colsum(dqkv)
    head_terms = jnp.concatenate(
        [
            colsum_qkv[:head_width].reshape(heads, HD),
            colsum_qkv[2 * head_width :].reshape(heads, HD),
            ubias_sum.reshape(unit_rows, HD),
        ]
    )
    place = lax.broadcasted_iota(jnp.int32, (blocks, 1, 1), 0)
    places = jnp.where(place == me, head_terms[None], 0.0)

    def by_owner(values):
        flat = values.reshape(-1, fsdp_size, values.shape[-1] // fsdp_size)
        return flat.transpose(1, 0, 2).reshape(fsdp_size, -1)

    small = jnp.concatenate([by_owner(vectors), by_owner(places)], axis=1)
    grad_stacked, small, qkv_piece = stage(grad_stacked, small, qkv_piece)
    for swap in (swap_low, swap_high, swap_tp):
        small = small + swap(small)
    stacked_other, small, qkv_high, qkv_low = stage(
        swap_tp(grad_stacked), small, swap_high(qkv_piece), swap_low(qkv_piece)
    )
    qkv_far = swap_low(qkv_high)
    summed = lax.dynamic_slice_in_dim(small, z, 1, axis=0)
    shares = []
    for step in range(1, fsdp_size):
        share = lax.dynamic_slice_in_dim(small, (z + step) % fsdp_size, 1, axis=0)
        pairs = [(i, (i + step) % fsdp_size) for i in range(fsdp_size)]
        shares.append(lax.ppermute(share, "fsdp", pairs))
    query_grad, key_grad, value_grad = assemble(
        ctx, [qkv_piece, qkv_low, qkv_high, qkv_far], False, 3, "attention_weight_grads"
    )
    prompt_input_grad, continuation_input_grad = to_outputs(grad_stacked, stacked_other)
    (
        shares,
        query_grad,
        key_grad,
        value_grad,
        prompt_input_grad,
        continuation_input_grad,
    ) = stage(
        shares, query_grad, key_grad, value_grad, prompt_input_grad, continuation_input_grad
    )
    summed = (summed + sum(shares))[0]
    obias_grad, gain_one_grad, shift_one_grad, gain_two_grad, shift_two_grad, dbias_grad = [
        summed[i * d_local : (i + 1) * d_local] for i in range(6)
    ]
    head_sums = summed[6 * d_local :].reshape(ctx_size, tp_size, 2 * heads + unit_rows, hd_local)
    head_sums = lax.dynamic_index_in_dim(head_sums, tp, axis=1, keepdims=False)
    qbias_grad = head_sums[:, :heads].reshape(heads_tp, hd_local)
    vbias_grad = head_sums[:, heads : 2 * heads].reshape(heads_tp, hd_local)
    ubias_grad = head_sums[:, 2 * heads :].reshape(ctx_size * unit_rows, hd_local)

    prompt_output, continuation_output = outputs
    return (
        prompt_output,
        continuation_output,
        prompt_input_grad,
        continuation_input_grad,
        query_grad,
        key_grad,
        value_grad,
        qbias_grad,
        vbias_grad,
        output_grad,
        obias_grad,
        gain_one_grad,
        shift_one_grad,
        gain_two_grad,
        shift_two_grad,
        up_grad,
        ubias_grad,
        down_grad,
        dbias_grad,
    )


def solution(mesh):
    return jax.shard_map(
        body,
        mesh=mesh,
        in_specs=(
            P("fsdp", "ctx", None),
            P("fsdp", "ctx", None, None),
            P("fsdp"),
            P("fsdp", "ctx"),
            P("fsdp", "tp"),
            P("fsdp", "tp"),
            P("fsdp", "tp"),
            P("tp", "fsdp"),
            P("tp", "fsdp"),
            P("tp", "fsdp"),
            P("fsdp"),
            P("fsdp"),
            P("fsdp"),
            P("fsdp"),
            P("fsdp"),
            P("fsdp", "tp"),
            P("tp", "fsdp"),
            P("tp", "fsdp"),
            P("fsdp"),
            P("fsdp", "ctx", None),
            P("fsdp", "ctx", None, None),
        ),
        out_specs=(
            P("fsdp", "ctx", None),
            P("fsdp", "ctx", None, None),
            P("fsdp", "ctx", None),
            P("fsdp", "ctx", None, None),
            P("fsdp", "tp"),
            P("fsdp", "tp"),
            P("fsdp", "tp"),
            P("tp", "fsdp"),
            P("tp", "fsdp"),
            P("tp", "fsdp"),
            P("fsdp"),
            P("fsdp"),
            P("fsdp"),
            P("fsdp"),
            P("fsdp"),
            P("fsdp", "tp"),
            P("tp", "fsdp"),
            P("tp", "fsdp"),
            P("fsdp"),
        ),
        check_vma=False,
    )
```

```python
from functools import partial
import math

import jax
import jax.numpy as jnp
from jax import lax
from jax.experimental import pallas as pl
from jax.experimental.pallas import tpu as pltpu
from jax.sharding import PartitionSpec as P

HD = 128
BF = jnp.bfloat16
F32 = jnp.float32
VMEM_BYTES = 62 << 20


norm_epsilon = 1e-05


def normalize(values):
    centre = jnp.mean(values, axis=-1, keepdims=True)
    centered = values - centre
    inverse = lax.rsqrt(jnp.mean(centered * centered, axis=-1, keepdims=True) + norm_epsilon)
    return (centered * inverse, inverse)


def norm_backward(incoming, normed, inverse, gain_vec):
    scaled = incoming * gain_vec
    return inverse * (
        scaled
        - jnp.mean(scaled, axis=-1, keepdims=True)
        - normed * jnp.mean(scaled * normed, axis=-1, keepdims=True)
    )


def swap_tp(value):
    return lax.ppermute(value, "tp", [(0, 1), (1, 0)])


def swap_low(value):
    return lax.ppermute(value, "ctx", [(0, 1), (1, 0), (2, 3), (3, 2)])


def swap_high(value):
    return lax.ppermute(value, "ctx", [(0, 2), (2, 0), (1, 3), (3, 1)])


def stage(*values):
    return lax.optimization_barrier(values)


def swap_any(value, distance):
    return lax.ppermute(value, ("ctx", "tp"), [(i, i ^ distance) for i in range(8)])


GATHERED = (0, 2, 1, 4, 3, 6, 5, 7)


def scatter_first(sums):
    return [swap_tp(sums[2]), swap_high(sums[3])]


def scatter_second(sums, first):
    half = sums[1].shape[0]
    by_tp, by_high = first
    across = sums[1].astype(F32) + by_high[:half].astype(F32)
    along = sums[4].astype(F32) + by_tp[half:].astype(F32)
    return [swap_tp(across.astype(BF)), swap_high(along.astype(BF))]


def scatter_sum(sums, first, second):
    half = sums[1].shape[0]
    by_tp = jnp.concatenate([second[0], first[0][:half]], axis=0)
    by_high = jnp.concatenate([first[1][half:], second[1]], axis=0)
    return sums[0] + by_tp.astype(F32) + by_high.astype(F32)


def pair_mask(rows, limits, split):
    row = lax.broadcasted_iota(jnp.int32, (rows, rows), 0)
    col = lax.broadcasted_iota(jnp.int32, (rows, rows), 1)
    mask = col <= row
    for seq in range(rows // split):
        inside = (row >= seq * split) & (row < (seq + 1) * split)
        limit = jnp.where(inside, limits[seq] + seq * split, 0)
        lower = jnp.where(inside, seq * split, 0)
        ok = (col >= lower) & (col < limit)
        mask = mask & (jnp.logical_not(inside) | ok)
    return mask


def attention_tiles(info_ref, tiles, rows, cont_len):
    me = info_ref[0]
    prompt_len = info_ref[1]
    per_block = rows // cont_len
    col = lax.broadcasted_iota(jnp.int32, (rows, rows), 1)
    row = lax.broadcasted_iota(jnp.int32, (rows, rows), 0)
    plan = []
    for t in range(tiles):
        keys = []
        for j in range(t + 1):
            mask = None
            if j == tiles - 1:
                mask = (col + j * rows) < prompt_len
            if j == t:
                mask = (col <= row) if mask is None else mask & (col <= row)
            keys.append((2 * j, mask))
        plan.append((2 * t, keys))
    for t in range(tiles):
        keys = []
        for j in range(tiles):
            keys.append((2 * j, (col + j * rows) < prompt_len if j == tiles - 1 else None))
        base = 2 + ((2 * t) ^ (me & (2 * tiles - 2))) // 2 * per_block
        limits = [info_ref[base + s] for s in range(per_block)]
        keys.append((2 * t + 1, pair_mask(rows, limits, cont_len)))
        plan.append((2 * t + 1, keys))
    return me, plan


def dot_nt(a, b):
    return lax.dot_general(a, b, (((1,), (1,)), ((), ())), preferred_element_type=F32)


def dot_nn(a, b):
    return lax.dot_general(a, b, (((1,), (0,)), ((), ())), preferred_element_type=F32)


def dot_tn(a, b):
    return lax.dot_general(a, b, (((0,), (0,)), ((), ())), preferred_element_type=F32)


def softmax_tiles(query, keys, scale):
    scores = []
    for key, mask in keys:
        score = dot_nt(query, key) * scale
        scores.append(score if mask is None else jnp.where(mask, score, -1e30))
    top = jnp.max(scores[0], axis=-1, keepdims=True)
    for s in scores[1:]:
        top = jnp.maximum(top, jnp.max(s, axis=-1, keepdims=True))
    weights = [jnp.exp(s - top) for s in scores]
    total = jnp.sum(weights[0], axis=-1, keepdims=True)
    for w in weights[1:]:
        total = total + jnp.sum(w, axis=-1, keepdims=True)
    inverse = 1.0 / total
    return [w * inverse for w in weights]


def attention_forward_kernel(tiles, rows, cont_len, heads, info_ref, qkv_ref, out_ref):
    h = pl.program_id(0)
    scale = 1.0 / math.sqrt(HD)
    me, plan = attention_tiles(info_ref, tiles, rows, cont_len)

    def load(kind, block):
        cols = pl.ds(pl.multiple_of((kind * heads + h) * HD, HD), HD)
        return qkv_ref[block ^ me, :, cols]

    for block, keys in plan:
        query = load(0, block)
        probs = softmax_tiles(query, [(load(1, kb), mask) for kb, mask in keys], scale)
        total = None
        for p, (kb, _) in zip(probs, keys):
            term = dot_nn(p.astype(BF), load(2, kb))
            total = term if total is None else total + term
        cols = pl.ds(pl.multiple_of(h * HD, HD), HD)
        out_ref[block ^ me, :, cols] = total.astype(BF)


def attention_backward_kernel(
    tiles, rows, cont_len, heads, info_ref, qkv_ref, grad_ref, out_ref, dkey_ref, dvalue_ref
):
    h = pl.program_id(0)
    scale = 1.0 / math.sqrt(HD)
    me, plan = attention_tiles(info_ref, tiles, rows, cont_len)

    def columns(kind):
        return pl.ds(pl.multiple_of((kind * heads + h) * HD, HD), HD)

    def load(kind, block):
        return qkv_ref[block ^ me, :, columns(kind)]

    seen = set()
    for block, keys in plan:
        query = load(0, block)
        grad = grad_ref[block ^ me, :, columns(0)]
        probs = softmax_tiles(query, [(load(1, kb), mask) for kb, mask in keys], scale)
        gprobs = [dot_nt(grad, load(2, kb)) for kb, _ in keys]
        delta = jnp.sum(probs[0] * gprobs[0], axis=-1, keepdims=True)
        for p, g in zip(probs[1:], gprobs[1:]):
            delta = delta + jnp.sum(p * g, axis=-1, keepdims=True)
        dquery = None
        for p, g, (kb, _) in zip(probs, gprobs, keys):
            dscore = (p * (g - delta)).astype(BF)
            term = dot_nn(dscore, load(1, kb))
            dquery = term if dquery is None else dquery + term
            dkey = dot_tn(dscore, query)
            dvalue = dot_tn(p.astype(BF), grad)
            if kb in seen:
                dkey_ref[kb] += dkey
                dvalue_ref[kb] += dvalue
            else:
                dkey_ref[kb] = dkey
                dvalue_ref[kb] = dvalue
                seen.add(kb)
        out_ref[block ^ me, :, columns(0)] = (dquery * scale).astype(BF)
    for kb in sorted(seen):
        out_ref[kb ^ me, :, columns(1)] = (dkey_ref[kb] * scale).astype(BF)
        out_ref[kb ^ me, :, columns(2)] = dvalue_ref[kb].astype(BF)


def attention_cost(blocks, rows, heads, matmuls):
    tiles = blocks // 2
    pairs = (tiles * (tiles + 1)) // 2 + tiles * (tiles + 1)
    return pl.CostEstimate(
        flops=2 * matmuls * pairs * heads * rows * rows * HD,
        transcendentals=pairs * heads * rows * rows,
        bytes_accessed=2 * blocks * rows * heads * HD * (4 if matmuls == 2 else 7),
    )


def attention_forward(info, qkv, cont_len):
    blocks, rows, width = qkv.shape
    heads = width // (3 * HD)
    return pl.pallas_call(
        partial(attention_forward_kernel, blocks // 2, rows, cont_len, heads),
        grid=(heads,),
        in_specs=[
            pl.BlockSpec(memory_space=pltpu.SMEM),
            pl.BlockSpec((blocks, rows, width), lambda h: (0, 0, 0)),
        ],
        out_specs=pl.BlockSpec((blocks, rows, heads * HD), lambda h: (0, 0, 0)),
        out_shape=jax.ShapeDtypeStruct((blocks, rows, heads * HD), BF),
        compiler_params=pltpu.CompilerParams(vmem_limit_bytes=32 << 20),
        cost_estimate=attention_cost(blocks, rows, heads, 2),
        name="attention_forward",
    )(info, qkv)


def attention_backward(info, qkv, grad, cont_len):
    blocks, rows, width = qkv.shape
    heads = width // (3 * HD)
    return pl.pallas_call(
        partial(attention_backward_kernel, blocks // 2, rows, cont_len, heads),
        grid=(heads,),
        in_specs=[
            pl.BlockSpec(memory_space=pltpu.SMEM),
            pl.BlockSpec((blocks, rows, width), lambda h: (0, 0, 0)),
            pl.BlockSpec((blocks, rows, heads * HD), lambda h: (0, 0, 0)),
        ],
        out_specs=pl.BlockSpec((blocks, rows, width), lambda h: (0, 0, 0)),
        out_shape=jax.ShapeDtypeStruct((blocks, rows, width), BF),
        scratch_shapes=[
            pltpu.VMEM((blocks, rows, HD), F32),
            pltpu.VMEM((blocks, rows, HD), F32),
        ],
        compiler_params=pltpu.CompilerParams(vmem_limit_bytes=32 << 20),
        cost_estimate=attention_cost(blocks, rows, heads, 7),
        name="attention_backward",
    )(info, qkv, grad)


def block_copies(pieces, rows, total):
    seen, plan = set(), []
    for start in range(0, total, rows):
        need = [
            i
            for i, (begin, size) in enumerate(pieces)
            if begin < start + rows and start < begin + size and i not in seen
        ]
        seen.update(need)
        plan.append(need)
    return plan


def piece_copy(refs, pieces, buffer, sems, i):
    begin, size = pieces[i]
    return pltpu.make_async_copy(refs[i], buffer.at[pl.ds(begin, size), :], sems.at[i])


def grad_matmul_kernel(pieces, rows, tile, *refs):
    lefts = refs[: len(pieces)]
    right_hbm, out_ref, buffer, right_ref, sems, right_sems = refs[len(pieces) :]
    step = pl.program_id(0)
    plan = block_copies(pieces, rows, right_ref.shape[0])
    columns = pl.ds(pl.multiple_of(step * tile, tile), tile)

    def right_copy(p):
        block = pl.ds(p * rows, rows)
        return pltpu.make_async_copy(right_hbm.at[block], right_ref.at[block], right_sems.at[p])

    @pl.when(step == 0)
    def _():
        for p, need in enumerate(plan):
            right_copy(p).start()
            for i in need:
                piece_copy(lefts, pieces, buffer, sems, i).start()
        total = None
        for p, need in enumerate(plan):
            right_copy(p).wait()
            for i in need:
                piece_copy(lefts, pieces, buffer, sems, i).wait()
            block = pl.ds(p * rows, rows)
            term = dot_tn(buffer[block, columns], right_ref[block, :])
            total = term if total is None else total + term
        out_ref[...] = total.astype(BF)

    @pl.when(step > 0)
    def _():
        out_ref[...] = dot_tn(buffer[:, columns], right_ref[...]).astype(BF)


def grad_matmul(lefts, starts, right, rows, name):
    d = lefts[0].shape[1]
    total_rows, n = right.shape
    tile = 1024
    pieces = [(start, p.shape[0]) for start, p in zip(starts, lefts)]
    return pl.pallas_call(
        partial(grad_matmul_kernel, pieces, rows, tile),
        grid=(d // tile,),
        in_specs=[pl.BlockSpec(memory_space=pl.ANY) for _ in range(len(lefts) + 1)],
        out_specs=pl.BlockSpec((tile, n), lambda i: (i, 0)),
        out_shape=jax.ShapeDtypeStruct((d, n), BF),
        scratch_shapes=[
            pltpu.VMEM((total_rows, d), BF),
            pltpu.VMEM((total_rows, n), BF),
            pltpu.SemaphoreType.DMA((len(lefts),)),
            pltpu.SemaphoreType.DMA((total_rows // rows,)),
        ],
        compiler_params=pltpu.CompilerParams(vmem_limit_bytes=VMEM_BYTES),
        cost_estimate=pl.CostEstimate(
            flops=2 * total_rows * d * n,
            transcendentals=0,
            bytes_accessed=2 * (total_rows * (d + n) + d * n),
        ),
        name=name,
    )(*lefts, right)


def sent_kernel(rows, low_ref, high_ref, w_ref, out_ref):
    for i, left in enumerate((low_ref, high_ref)):
        out_ref[pl.ds(2 * i * rows, 2 * rows), :] = dot_nt(left[...], w_ref[...]).astype(BF)


def kept_kernel(rows, low_ref, high_ref, w_ref, arrived_ref, own_ref, *outs):
    across_ref, to_tp_ref, to_high_ref, along_ref = outs
    half = rows // 2
    low = dot_nt(low_ref[...], w_ref[...])
    low = low + arrived_ref[pl.ds(0, 2 * rows), :].astype(F32)
    own_ref[...] = low[:rows]
    across_ref[...] = low[rows : rows + half].astype(BF)
    to_tp_ref[pl.ds(0, half), :] = low[rows + half :].astype(BF)
    high = dot_nt(high_ref[...], w_ref[...])
    high = (high + arrived_ref[pl.ds(2 * rows, 2 * rows), :].astype(F32)).astype(BF)
    to_tp_ref[pl.ds(half, half), :] = high[rows + half :]
    to_high_ref[pl.ds(0, half), :] = high[rows : rows + half]
    to_high_ref[pl.ds(half, half), :] = high[:half]
    along_ref[...] = high[half:rows]


def partial_blocks(left, rows, weights, column, arrived, name):
    k = left.shape[1]
    d = weights.shape[0]
    tile = 1024
    pair = 2 * rows
    if arrived is None:
        first, kernel, more = 1, sent_kernel, []
        outs = [(4 * rows, BF)]
    else:
        first, kernel, more = 0, kept_kernel, [arrived]
        outs = [(rows, F32), (rows // 2, BF), (rows, BF), (rows, BF), (rows // 2, BF)]
    result = pl.pallas_call(
        partial(kernel, rows),
        grid=(d // tile,),
        in_specs=[
            pl.BlockSpec((pair, k), lambda i: (first, 0), pipeline_mode=pl.Buffered(1)),
            pl.BlockSpec((pair, k), lambda i: (first + 2, 0), pipeline_mode=pl.Buffered(1)),
            pl.BlockSpec((tile, k), lambda i: (i, column)),
        ]
        + [pl.BlockSpec((2 * pair, tile), lambda i: (0, i)) for _ in more],
        out_specs=[pl.BlockSpec((n, tile), lambda i: (0, i)) for n, _ in outs],
        out_shape=[jax.ShapeDtypeStruct((n, d), t) for n, t in outs],
        compiler_params=pltpu.CompilerParams(vmem_limit_bytes=VMEM_BYTES),
        cost_estimate=pl.CostEstimate(
            flops=8 * rows * d * k,
            transcendentals=0,
            bytes_accessed=2 * (4 * rows * (k + d) + d * k),
        ),
        name=name,
    )(left, left, weights, *more)
    return result[0] if arrived is None else result


def project_kernel(pieces, rows, *refs):
    lefts, (w_ref, bias_ref, out_ref, buffer, sems) = refs[: len(pieces)], refs[len(pieces) :]
    total = out_ref.shape[0]
    plan = block_copies(pieces, rows, total)

    def compute(p):
        block = pl.ds(p * rows, rows)
        out_ref[block, :] = (dot_nn(buffer[block, :], w_ref[...]) + bias_ref[...]).astype(BF)

    @pl.when(pl.program_id(0) == 0)
    def _():
        for need in plan:
            for i in need:
                piece_copy(lefts, pieces, buffer, sems, i).start()
        for p, need in enumerate(plan):
            for i in need:
                piece_copy(lefts, pieces, buffer, sems, i).wait()
            compute(p)

    @pl.when(pl.program_id(0) > 0)
    def _():
        for p in range(len(plan)):
            compute(p)


def project(lefts, starts, rows, weights, bias, column, n, name):
    total = sum(p.shape[0] for p in lefts)
    width = lefts[0].shape[1]
    pieces = [(start, p.shape[0]) for start, p in zip(starts, lefts)]
    tile = 256
    skip = column // tile
    return pl.pallas_call(
        partial(project_kernel, pieces, rows),
        grid=(n // tile,),
        in_specs=[pl.BlockSpec(memory_space=pl.ANY) for _ in lefts]
        + [
            pl.BlockSpec((width, tile), lambda i: (0, skip + i)),
            pl.BlockSpec((1, tile), lambda i: (0, i)),
        ],
        out_specs=pl.BlockSpec((total, tile), lambda i: (0, i)),
        out_shape=jax.ShapeDtypeStruct((total, n), BF),
        scratch_shapes=[
            pltpu.VMEM((total, width), BF),
            pltpu.SemaphoreType.DMA((len(lefts),)),
        ],
        compiler_params=pltpu.CompilerParams(vmem_limit_bytes=VMEM_BYTES),
        cost_estimate=pl.CostEstimate(
            flops=2 * total * width * n,
            transcendentals=0,
            bytes_accessed=2 * (total * (width + n) + width * n),
        ),
        name=name,
    )(*lefts, weights, bias)


def middle_kernel(pieces, tile, *refs):
    lefts = refs[: len(pieces)]
    att_ref, w_ref, term_ref, grad_ref, buffer, total_ref, sems = refs[len(pieces) :]
    step = pl.program_id(0)

    @pl.when(step == 0)
    def _():
        for i in range(len(pieces)):
            piece_copy(lefts, pieces, buffer, sems, i).start()
        for i in range(len(pieces)):
            piece_copy(lefts, pieces, buffer, sems, i).wait()

    left = buffer[:, pl.ds(pl.multiple_of(step * tile, tile), tile)]
    term_ref[...] = dot_tn(left, att_ref[...]).astype(BF)
    grad = dot_nn(left, w_ref[...])

    @pl.when(step == 0)
    def _():
        total_ref[...] = grad

    @pl.when(step > 0)
    def _():
        total_ref[...] += grad

    @pl.when(step == pl.num_programs(0) - 1)
    def _():
        grad_ref[...] = total_ref[...].astype(BF)


def middle_terms(lefts, starts, attended, weights, column, name):
    total, n = attended.shape
    d = lefts[0].shape[1]
    tile = 512
    pieces = [(start, p.shape[0]) for start, p in zip(starts, lefts)]
    return pl.pallas_call(
        partial(middle_kernel, pieces, tile),
        grid=(d // tile,),
        in_specs=[pl.BlockSpec(memory_space=pl.ANY) for _ in lefts]
        + [
            pl.BlockSpec((total, n), lambda i: (0, 0), pipeline_mode=pl.Buffered(1)),
            pl.BlockSpec((tile, n), lambda i: (i, column)),
        ],
        out_specs=[
            pl.BlockSpec((tile, n), lambda i: (i, 0)),
            pl.BlockSpec((total, n), lambda i: (0, 0)),
        ],
        out_shape=[
            jax.ShapeDtypeStruct((d, n), BF),
            jax.ShapeDtypeStruct((total, n), BF),
        ],
        scratch_shapes=[
            pltpu.VMEM((total, d), BF),
            pltpu.VMEM((total, n), F32),
            pltpu.SemaphoreType.DMA((len(lefts),)),
        ],
        compiler_params=pltpu.CompilerParams(vmem_limit_bytes=VMEM_BYTES),
        cost_estimate=pl.CostEstimate(
            flops=4 * total * d * n,
            transcendentals=0,
            bytes_accessed=2 * total * (d + 2 * n) + 4 * d * n,
        ),
        name=name,
    )(*lefts, attended, weights)


def shard_kernel(n_cols, ctx_ref, *refs):
    ins, out = refs[:-1], refs[-1]
    start = 0
    for i, ref in enumerate(ins):
        value = ref[...] if i < n_cols else ref[...].T
        out[:, start : start + value.shape[1]] = value
        start += value.shape[1]


def weight_shard(ctx, by_column, by_row, size, name):
    d = by_column[0].shape[0]
    count = len(by_column) + len(by_row)
    return pl.pallas_call(
        partial(shard_kernel, len(by_column)),
        grid_spec=pltpu.PrefetchScalarGridSpec(
            num_scalar_prefetch=1,
            grid=(1,),
            in_specs=[pl.BlockSpec((d, size), lambda i, c: (0, c[0])) for _ in by_column]
            + [pl.BlockSpec((size, d), lambda i, c: (c[0], 0)) for _ in by_row],
            out_specs=pl.BlockSpec((d, count * size), lambda i, c: (0, 0)),
        ),
        out_shape=jax.ShapeDtypeStruct((d, count * size), BF),
        compiler_params=pltpu.CompilerParams(vmem_limit_bytes=VMEM_BYTES),
        cost_estimate=pl.CostEstimate(
            flops=0, transcendentals=0, bytes_accessed=4 * d * count * size
        ),
        name=name,
    )(ctx[None].astype(jnp.int32), *by_column, *by_row)


def assemble_kernel(turn, count, width, ctx_ref, *refs):
    pieces, outs = refs[:count], refs[count:]
    step = pl.program_id(0)
    for k in range(count):

        @pl.when(step == k)
        def _():
            for i, out in enumerate(outs):
                part = pieces[k][:, i * width : (i + 1) * width].astype(F32)
                out[...] = part.T if turn else part


def assemble(ctx, pieces, turn, outputs, name):
    count = len(pieces)
    rows, cols = pieces[0].shape
    width = cols // outputs
    if turn:
        block, shape = (width, rows), (width * count, rows)
        index = lambda k, ctx_ref: (k ^ ctx_ref[0], 0)
    else:
        block, shape = (rows, width), (rows, width * count)
        index = lambda k, ctx_ref: (0, k ^ ctx_ref[0])
    return pl.pallas_call(
        partial(assemble_kernel, turn, count, width),
        grid_spec=pltpu.PrefetchScalarGridSpec(
            num_scalar_prefetch=1,
            grid=(count,),
            in_specs=[
                pl.BlockSpec((rows, cols), lambda k, ctx_ref: (0, 0), pipeline_mode=pl.Buffered(1))
                for _ in pieces
            ],
            out_specs=[pl.BlockSpec(block, index) for _ in range(outputs)],
        ),
        out_shape=[jax.ShapeDtypeStruct(shape, F32) for _ in range(outputs)],
        compiler_params=pltpu.CompilerParams(vmem_limit_bytes=VMEM_BYTES),
        cost_estimate=pl.CostEstimate(
            flops=0, transcendentals=0, bytes_accessed=6 * count * rows * cols
        ),
        name=name,
    )(ctx[None].astype(jnp.int32), *pieces)


def gelu_and_slope(u):
    half = 0.5 * (1.0 + lax.erf(u * math.sqrt(0.5)))
    density = jnp.exp(-0.5 * u * u) * (1.0 / math.sqrt(2.0 * math.pi))
    return u * half, half + u * density


def feed_kernel(act_pieces, up_pieces, rows, *refs):
    count = len(act_pieces)
    acts, ups = refs[:count], refs[count : count + len(up_pieces)]
    (
        w_up_ref,
        w_down_ref,
        bias_ref,
        hidden_ref,
        grad_ref,
        sum_ref,
        act_buffer,
        up_buffer,
        act_sems,
        up_sems,
    ) = refs[count + len(up_pieces) :]
    total = hidden_ref.shape[0]
    act_plan = block_copies(act_pieces, rows, total)
    up_plan = block_copies(up_pieces, rows, total)

    def compute(p):
        block = pl.ds(p * rows, rows)
        pre_act = dot_nn(act_buffer[block, :], w_up_ref[...]) + bias_ref[...]
        grad_hidden = dot_nn(up_buffer[block, :], w_down_ref[...])
        hidden, slope = gelu_and_slope(pre_act)
        hidden_ref[block, :] = hidden.astype(BF)
        grad = (grad_hidden * slope).astype(BF)
        grad_ref[block, :] = grad
        part = jnp.sum(grad.astype(F32), axis=0, keepdims=True)
        if p == 0:
            sum_ref[...] = part
        else:
            sum_ref[...] += part

    def act_copy(i):
        return piece_copy(acts, act_pieces, act_buffer, act_sems, i)

    def up_copy(i):
        return piece_copy(ups, up_pieces, up_buffer, up_sems, i)

    @pl.when(pl.program_id(0) == 0)
    def _():
        for act_need, up_need in zip(act_plan, up_plan):
            for i in act_need:
                act_copy(i).start()
            for i in up_need:
                up_copy(i).start()
        for p, (act_need, up_need) in enumerate(zip(act_plan, up_plan)):
            for i in act_need:
                act_copy(i).wait()
            for i in up_need:
                up_copy(i).wait()
            compute(p)

    @pl.when(pl.program_id(0) > 0)
    def _():
        for p in range(len(act_plan)):
            compute(p)


def feed_both(acts, act_starts, ups, up_starts, rows, weights, bias, units, name):
    total = sum(p.shape[0] for p in acts)
    width = acts[0].shape[1]
    tile = 512
    skip = units // tile
    act_pieces = [(start, p.shape[0]) for start, p in zip(act_starts, acts)]
    up_pieces = [(start, p.shape[0]) for start, p in zip(up_starts, ups)]
    return pl.pallas_call(
        partial(feed_kernel, act_pieces, up_pieces, rows),
        grid=(units // tile,),
        in_specs=[pl.BlockSpec(memory_space=pl.ANY) for _ in acts + ups]
        + [
            pl.BlockSpec((width, tile), lambda i: (0, i)),
            pl.BlockSpec((width, tile), lambda i: (0, skip + i)),
            pl.BlockSpec((1, tile), lambda i: (0, i)),
        ],
        out_specs=[
            pl.BlockSpec((total, tile), lambda i: (0, i)),
            pl.BlockSpec((total, tile), lambda i: (0, i)),
            pl.BlockSpec((1, tile), lambda i: (0, i)),
        ],
        out_shape=[
            jax.ShapeDtypeStruct((total, units), BF),
            jax.ShapeDtypeStruct((total, units), BF),
            jax.ShapeDtypeStruct((1, units), F32),
        ],
        scratch_shapes=[
            pltpu.VMEM((total, width), BF),
            pltpu.VMEM((total, width), BF),
            pltpu.SemaphoreType.DMA((len(acts),)),
            pltpu.SemaphoreType.DMA((len(ups),)),
        ],
        compiler_params=pltpu.CompilerParams(vmem_limit_bytes=VMEM_BYTES),
        cost_estimate=pl.CostEstimate(
            flops=4 * total * width * units,
            transcendentals=0,
            bytes_accessed=4 * (total * width + width * units + total * units),
        ),
        name=name,
    )(*acts, *ups, weights, weights, bias)


def gather_small(packed, size):
    index = lax.axis_index("fsdp")
    out = lax.dynamic_update_slice(
        jnp.zeros((size,) + packed.shape, packed.dtype), packed[None], (index, 0)
    )
    for step in range(1, size):
        moved = lax.ppermute(packed, "fsdp", [(i, (i + step) % size) for i in range(size)])
        out = lax.dynamic_update_slice(out, moved[None], ((index + size - step) % size, 0))
    return out


def body(
    prompt_input,
    continuation_input,
    prompt_lengths,
    continuation_lengths,
    query_weight,
    key_weight,
    value_weight,
    query_bias,
    value_bias,
    output_weight,
    output_bias,
    first_gain,
    first_shift,
    second_gain,
    second_shift,
    up_weight,
    up_bias,
    down_weight,
    down_bias,
    prompt_cotangent,
    continuation_cotangent,
):
    prompt_dev = prompt_input.shape[1]
    cont_dev = continuation_input.shape[1]
    cont_len = continuation_input.shape[2]
    width = prompt_input.shape[2]
    rows = prompt_dev
    fsdp_size = lax.axis_size("fsdp")
    ctx_size = lax.axis_size("ctx")
    tp_size = lax.axis_size("tp")
    assert ctx_size == 4 and tp_size == 2 and cont_dev * cont_len == rows
    blocks = ctx_size * tp_size
    total_rows = blocks * rows
    z = lax.axis_index("fsdp")
    ctx = lax.axis_index("ctx")
    tp = lax.axis_index("tp")
    me = 2 * ctx + tp

    heads_tp = query_bias.shape[0]
    heads = heads_tp // ctx_size
    head_width = heads * HD
    units = up_weight.shape[1] // ctx_size
    unit_rows = units // HD
    d_local = query_weight.shape[0]

    def rws(weight, count):
        return lax.dynamic_slice_in_dim(weight, ctx * count, count, axis=0)

    attn_shard = weight_shard(
        ctx, [query_weight, key_weight, value_weight], [output_weight], head_width, "attention_shard"
    )
    (
        attn_shard,
        prompt_input,
        continuation_input,
        prompt_cotangent,
        continuation_cotangent,
        continuation_lengths,
    ) = stage(
        attn_shard,
        prompt_input,
        continuation_input,
        prompt_cotangent,
        continuation_cotangent,
        continuation_lengths,
    )
    attn_full = lax.all_gather(attn_shard, "fsdp", axis=0, tiled=True)
    w_qkv = attn_full[:, : 3 * head_width]
    def own_pair(first, second):
        a = first[0]
        b = second[0].reshape(rows, width)
        return jnp.where(tp == 0, a, b), jnp.where(tp == 0, b, a)

    in_own, in_other = own_pair(prompt_input, continuation_input)
    up_own, up_other = own_pair(prompt_cotangent, continuation_cotangent)
    stacked = jnp.concatenate([in_own, in_other], axis=0).astype(F32)
    normed_pair, inverse_pair = normalize(stacked)
    (
        output_bias,
        first_gain,
        first_shift,
        second_gain,
        second_shift,
        down_bias,
        query_bias,
        value_bias,
        up_bias,
        up_weight,
        continuation_lengths,
        inverse_pair,
    ) = stage(
        output_bias,
        first_gain,
        first_shift,
        second_gain,
        second_shift,
        down_bias,
        query_bias,
        value_bias,
        up_bias,
        up_weight,
        continuation_lengths,
        inverse_pair,
    )
    packed = jnp.concatenate(
        [
            output_bias,
            first_gain,
            first_shift,
            second_gain,
            second_shift,
            down_bias,
            rws(query_bias, heads).reshape(-1),
            rws(value_bias, heads).reshape(-1),
            rws(up_bias, unit_rows).reshape(-1),
        ]
    )
    feed_shard = weight_shard(ctx, [up_weight], [down_weight], units, "feed_shard")
    small, feed_shard = stage(gather_small(packed, fsdp_size), feed_shard)
    w_feed = lax.all_gather(feed_shard, "fsdp", axis=0, tiled=True)
    small = small.astype(F32)
    vectors = [small[:, i * d_local : (i + 1) * d_local].reshape(-1) for i in range(6)]
    obias, gain_one, shift_one, gain_two, shift_two, dbias = vectors
    hd_local = HD // fsdp_size

    def head_vector(start, count):
        piece = small[:, start : start + count * hd_local].reshape(fsdp_size, count, hd_local)
        return piece.transpose(1, 0, 2).reshape(-1)

    start = 6 * d_local
    qbias = head_vector(start, heads)
    vbias = head_vector(start + heads * hd_local, heads)
    ubias = head_vector(start + 2 * heads * hd_local, unit_rows)
    qkv_bias = jnp.concatenate([qbias, jnp.zeros_like(qbias), vbias])

    lens = continuation_lengths[0]
    lens_high = swap_high(lens)
    info = jnp.concatenate(
        [me[None].astype(jnp.int32), prompt_lengths, lens, swap_low(lens), lens_high, swap_low(lens_high)]
    )

    up_along = swap_high(up_own)
    act_pair = (normed_pair * gain_one + shift_one).astype(BF)
    act_pair, up_along = stage(act_pair, up_along)
    up_pair = jnp.concatenate([up_own, up_other], axis=0)
    act_high, act_low, up_corner, up_low, up_far = stage(
        swap_high(act_pair), swap_low(act_pair), swap_tp(up_along), swap_low(up_pair), swap_low(up_along)
    )
    act_pieces = [act_pair, act_low, act_high, swap_low(act_high)]
    act_starts = [0, 2 * rows, 4 * rows, 6 * rows]
    up_pieces = [up_pair, up_low, up_along, up_corner, up_far, swap_low(up_corner)]
    up_starts = [0, 2 * rows, 4 * rows, 5 * rows, 6 * rows, 7 * rows]
    act_pieces, up_pieces = stage(act_pieces, up_pieces)
    normed_one = normed_pair[:rows]
    inverse_one = inverse_pair[:rows]
    x_own = stacked[:rows]

    qkv = project(
        act_pieces, act_starts, rows, attn_full, qkv_bias[None], 0, 3 * head_width, "heads"
    ).reshape(blocks, rows, 3 * head_width)
    attended = attention_forward(info, qkv, cont_len).reshape(total_rows, head_width)
    parts = partial_blocks(attended, rows, attn_full, 3, None, "attention_sent")
    parts = swap_low(parts)
    sums = partial_blocks(attended, rows, attn_full, 3, parts, "attention_kept")
    first = stage(*scatter_first(sums))
    second = scatter_second(sums, first)
    middle = x_own + (scatter_sum(sums, first, second) + obias)
    normed_two, inverse_two = normalize(middle)
    act_two_own = (normed_two * gain_two + shift_two).astype(BF)

    def gather_blocks(own, beside=()):
        half = rows // 2
        across, along, low, *beside = stage(swap_tp(own), swap_high(own), swap_low(own), *beside)
        corner_a, corner_b, across_low, along_low = stage(
            swap_high(across[:half]), swap_tp(along[half:]), swap_low(across), swap_low(along)
        )
        pieces = stage(
            own,
            low,
            across,
            along,
            across_low,
            along_low,
            corner_a,
            corner_b,
            swap_low(corner_a),
            swap_low(corner_b),
        )
        return list(pieces), beside

    act_two, _ = gather_blocks(act_two_own)
    starts = []
    for p in GATHERED[:6]:
        starts.append(p * rows)
    for p in GATHERED[6:]:
        starts += [p * rows, p * rows + rows // 2]

    def to_outputs(own, other):
        first = jnp.where(tp == 0, own, other)
        second = jnp.where(tp == 0, other, own)
        return first[None], second.reshape(1, cont_dev, cont_len, width)

    hidden, grad_pre, ubias_sum = feed_both(
        act_two, starts, up_pieces, up_starts, 2 * rows, w_feed, ubias[None], units, "feed_both"
    )
    parts = partial_blocks(grad_pre, rows, w_feed, 0, None, "act_two_sent")
    parts, hidden = stage(parts, hidden)
    down_term = grad_matmul(up_pieces, up_starts, hidden, 2 * rows, "down_weight_term")
    parts, grad_pre, down_term = stage(swap_low(parts), grad_pre, down_term)
    down_piece = lax.psum_scatter(down_term, "fsdp", scatter_dimension=0, tiled=True)
    sums = partial_blocks(grad_pre, rows, w_feed, 0, parts, "act_two_kept")
    sums, grad_pre, hidden = stage(sums, grad_pre, hidden)
    mlp_parts = partial_blocks(hidden, rows, w_feed, 1, None, "feed_sent")
    first, mlp_parts, hidden, grad_pre = stage(scatter_first(sums), mlp_parts, hidden, grad_pre)
    second, mlp_parts, hidden, grad_pre = stage(
        scatter_second(sums, first), swap_low(mlp_parts), hidden, grad_pre
    )
    grad_act_two = scatter_sum(sums, first, second)
    grad_middle = up_own.astype(F32) + norm_backward(
        grad_act_two, normed_two, inverse_two, gain_two
    )
    middle_low_own = grad_middle.astype(BF)

    middle_low_own, mlp_parts, hidden, grad_pre = stage(
        middle_low_own, mlp_parts, hidden, grad_pre
    )
    up_term = grad_matmul(act_two, starts, grad_pre, 2 * rows, "up_weight_term")
    mlp_sums = partial_blocks(hidden, rows, w_feed, 1, mlp_parts, "feed_kept")
    middle_low, (mlp_sums, up_term, down_piece) = gather_blocks(
        middle_low_own, (mlp_sums, up_term, down_piece)
    )
    up_piece = lax.psum_scatter(up_term, "fsdp", scatter_dimension=0, tiled=True)

    def colsum(value):
        return jnp.sum(value, axis=0, dtype=F32)

    middle_low, mlp_sums = stage(middle_low, mlp_sums)
    out_term, grad_attended = middle_terms(
        middle_low, starts, attended, attn_full, 3, "middle_terms"
    )
    mlp_first, grad_attended, out_term = stage(
        scatter_first(mlp_sums), grad_attended, out_term
    )
    out_piece = lax.psum_scatter(out_term, "fsdp", scatter_dimension=0, tiled=True)
    dqkv = attention_backward(
        info, qkv, grad_attended.reshape(blocks, rows, head_width), cont_len
    ).reshape(total_rows, 3 * head_width)
    mlp_second, dqkv, up_piece = stage(scatter_second(mlp_sums, mlp_first), dqkv, up_piece)
    parts = partial_blocks(dqkv, rows, attn_full, 0, None, "act_one_sent")
    result = (middle + (scatter_sum(mlp_sums, mlp_first, mlp_second) + dbias)).astype(BF)
    parts, result, dqkv, down_high = stage(parts, result, dqkv, swap_high(down_piece))
    qkv_term = grad_matmul(act_pieces, act_starts, dqkv, 2 * rows, "attention_weight_term")
    dqkv, parts, result_other, up_high, out_piece, qkv_term = stage(
        dqkv, swap_low(parts), swap_tp(result), swap_high(up_piece), out_piece, qkv_term
    )
    qkv_piece = lax.psum_scatter(qkv_term, "fsdp", scatter_dimension=0, tiled=True)
    sums = partial_blocks(dqkv, rows, attn_full, 0, parts, "act_one_kept")
    sums, up_far, down_low, down_far, up_low, out_high = stage(
        sums,
        swap_low(up_high),
        swap_low(down_piece),
        swap_low(down_high),
        swap_low(up_piece),
        swap_high(out_piece),
    )
    out_low = swap_low(out_piece)
    (down_grad,) = assemble(
        ctx, [down_piece, down_low, down_high, down_far], True, 1, "down_weight_grad"
    )
    (output_grad,) = assemble(
        ctx, [out_piece, out_low, out_high, swap_low(out_high)], True, 1, "output_weight_grad"
    )
    first, down_grad, output_grad, outputs = stage(
        scatter_first(sums), down_grad, output_grad, to_outputs(result, result_other)
    )
    (up_grad,) = assemble(ctx, [up_piece, up_low, up_high, up_far], False, 1, "up_weight_grad")
    second, up_grad = stage(scatter_second(sums, first), up_grad)
    grad_act_one = scatter_sum(sums, first, second)
    grad_stacked = (
        grad_middle + norm_backward(grad_act_one, normed_one, inverse_one, gain_one)
    ).astype(BF)
    vectors = jnp.stack(
        [
            colsum(middle_low_own),
            colsum(grad_act_one * normed_one),
            colsum(grad_act_one),
            colsum(grad_act_two * normed_two),
            colsum(grad_act_two),
            colsum(up_own),
        ]
    )
    colsum_qkv = colsum(dqkv)
    head_terms = jnp.concatenate(
        [
            colsum_qkv[:head_width].reshape(heads, HD),
            colsum_qkv[2 * head_width :].reshape(heads, HD),
            ubias_sum.reshape(unit_rows, HD),
        ]
    )
    place = lax.broadcasted_iota(jnp.int32, (blocks, 1, 1), 0)
    places = jnp.where(place == me, head_terms[None], 0.0)

    def by_owner(values):
        flat = values.reshape(-1, fsdp_size, values.shape[-1] // fsdp_size)
        return flat.transpose(1, 0, 2).reshape(fsdp_size, -1)

    small = jnp.concatenate([by_owner(vectors), by_owner(places)], axis=1)
    grad_stacked, small, qkv_piece = stage(grad_stacked, small, qkv_piece)
    for swap in (swap_low, swap_high, swap_tp):
        small = small + swap(small)
    stacked_other, small, qkv_high, qkv_low = stage(
        swap_tp(grad_stacked), small, swap_high(qkv_piece), swap_low(qkv_piece)
    )
    qkv_far = swap_low(qkv_high)
    summed = lax.dynamic_slice_in_dim(small, z, 1, axis=0)
    shares = []
    for step in range(1, fsdp_size):
        share = lax.dynamic_slice_in_dim(small, (z + step) % fsdp_size, 1, axis=0)
        pairs = [(i, (i + step) % fsdp_size) for i in range(fsdp_size)]
        shares.append(lax.ppermute(share, "fsdp", pairs))
    query_grad, key_grad, value_grad = assemble(
        ctx, [qkv_piece, qkv_low, qkv_high, qkv_far], False, 3, "attention_weight_grads"
    )
    prompt_input_grad, continuation_input_grad = to_outputs(grad_stacked, stacked_other)
    (
        shares,
        query_grad,
        key_grad,
        value_grad,
        prompt_input_grad,
        continuation_input_grad,
    ) = stage(
        shares, query_grad, key_grad, value_grad, prompt_input_grad, continuation_input_grad
    )
    summed = (summed + sum(shares))[0]
    obias_grad, gain_one_grad, shift_one_grad, gain_two_grad, shift_two_grad, dbias_grad = [
        summed[i * d_local : (i + 1) * d_local] for i in range(6)
    ]
    head_sums = summed[6 * d_local :].reshape(ctx_size, tp_size, 2 * heads + unit_rows, hd_local)
    head_sums = lax.dynamic_index_in_dim(head_sums, tp, axis=1, keepdims=False)
    qbias_grad = head_sums[:, :heads].reshape(heads_tp, hd_local)
    vbias_grad = head_sums[:, heads : 2 * heads].reshape(heads_tp, hd_local)
    ubias_grad = head_sums[:, 2 * heads :].reshape(ctx_size * unit_rows, hd_local)

    prompt_output, continuation_output = outputs
    return (
        prompt_output,
        continuation_output,
        prompt_input_grad,
        continuation_input_grad,
        query_grad,
        key_grad,
        value_grad,
        qbias_grad,
        vbias_grad,
        output_grad,
        obias_grad,
        gain_one_grad,
        shift_one_grad,
        gain_two_grad,
        shift_two_grad,
        up_grad,
        ubias_grad,
        down_grad,
        dbias_grad,
    )


def solution(mesh):
    return jax.shard_map(
        body,
        mesh=mesh,
        in_specs=(
            P("fsdp", "ctx", None),
            P("fsdp", "ctx", None, None),
            P("fsdp"),
            P("fsdp", "ctx"),
            P("fsdp", "tp"),
            P("fsdp", "tp"),
            P("fsdp", "tp"),
            P("tp", "fsdp"),
            P("tp", "fsdp"),
            P("tp", "fsdp"),
            P("fsdp"),
            P("fsdp"),
            P("fsdp"),
            P("fsdp"),
            P("fsdp"),
            P("fsdp", "tp"),
            P("tp", "fsdp"),
            P("tp", "fsdp"),
            P("fsdp"),
            P("fsdp", "ctx", None),
            P("fsdp", "ctx", None, None),
        ),
        out_specs=(
            P("fsdp", "ctx", None),
            P("fsdp", "ctx", None, None),
            P("fsdp", "ctx", None),
            P("fsdp", "ctx", None, None),
            P("fsdp", "tp"),
            P("fsdp", "tp"),
            P("fsdp", "tp"),
            P("tp", "fsdp"),
            P("tp", "fsdp"),
            P("tp", "fsdp"),
            P("fsdp"),
            P("fsdp"),
            P("fsdp"),
            P("fsdp"),
            P("fsdp"),
            P("fsdp", "tp"),
            P("tp", "fsdp"),
            P("tp", "fsdp"),
            P("fsdp"),
        ),
        check_vma=False,
    )
```
